32 devices in a mesh: cfg: 2 (over y), req: 4 (over x, core), seq: 4 (over z).
Axes of the slice: x: 2, y: 2, z: 4, core: 2. Of those that a mesh axis runs over, the one named last changes fastest.
Arguments:
- image_hidden: bfloat16 [2, 4, 512, 1536], P('cfg', 'req', 'seq'), may hold values from -6 to 6
- text_hidden: bfloat16 [2, 4, 160, 1536], P('cfg', 'req', 'seq'), may hold values from -6 to 6
- modulation: float32 [2, 4, 10, 1536], P('cfg', 'req'), may hold values from -3 to 3
- attn_weight: bfloat16 [1536, 5120], P(None, 'seq'), may hold values from -8 to 8
- proj_weight: bfloat16 [1024, 1536], replicated, may hold values from -0.1875 to 0.1875
- mlp_in_weight: bfloat16 [1536, 6144], P(None, 'seq'), may hold values from -0.15625 to 0.15625
- mlp_out_weight: bfloat16 [6144, 1536], P('seq'), may hold values from -0.078125 to 0.078125
- final_weight: bfloat16 [64, 1536], replicated, may hold values from -0.15625 to 0.15625
- latents: float32 [4, 64, 512], P('req', 'cfg', 'seq'), may hold values from -6 to 6
- guidance: float32 [4], P('req'), may hold values from 3 to 7
- text_lengths: int32 [2, 4], P('cfg', 'req'), may hold values from 1 to 154, 385 in all within a row
- step_index: int32 [4], P('req'), may hold values from 0 to 27
- step_count: int32 [4], P('req'), may hold values from 1 to 3
Outputs:
- velocity: float32 [4, 64, 512], P('req', 'cfg', 'seq')
- new_latents: float32 [4, 64, 512], P('req', 'cfg', 'seq')
The draws below stay inside these ranges and needn't reach their ends.
All inputs are finite; a program needn't handle non-finite values. No bound on the sum of `text_lengths` on one device may be relied on, other than what follows from the above.
Results may differ from the reference program's by a relative error of at most 0.017.
Values may be sent and summed in bfloat16 or wider, within the bound.
A program may use at most 128 MiB of HBM per device.

```python
import math
import jax
import jax.numpy as jnp
import numpy as np
from jax import lax

D = 1536
HEADS = 16
HEAD = 64
FF = 6144
PATCH = 64
TXT = 160
TXT_MAX = 154
STEPS = 28
IMG = 512
REQ = 4
N_SEQ = 4


def draw_attn_weight(key, part):
    base = jnp.clip(jax.random.normal(key, (D, HEADS, 5, HEAD), jnp.float32), -6.0, 6.0) / jnp.sqrt(float(D))
    base = jnp.clip(base, -8.0, 8.0)
    return base.reshape(D, HEADS * 5 * HEAD).astype(jnp.bfloat16)


def draw_image_hidden(key, part):
    first_key = jax.random.fold_in(key, 21)
    second_key = jax.random.fold_in(key, 22)
    ramp = (jnp.arange(IMG, dtype=jnp.float32) + 0.5) / IMG
    shared = jnp.clip(jax.random.normal(first_key, (REQ, IMG, D), jnp.float32), -6.0, 6.0)
    other = jnp.clip(jax.random.normal(second_key, (REQ, IMG, D), jnp.float32), -6.0, 6.0)
    mixing = ramp[None, :, None]
    second = (1.0 - mixing) * shared + mixing * other
    result = jnp.clip(jnp.stack([shared, second], axis=0), -6.0, 6.0)
    return result.astype(jnp.bfloat16)


def draw_modulation(key, part):
    base = 0.5 * jax.random.normal(jax.random.fold_in(key, 31), (REQ, 10, D), jnp.float32)
    offset = 0.1 * jax.random.normal(jax.random.fold_in(key, 32), (REQ, 10, D), jnp.float32)
    result = jnp.stack([base, base + offset], axis=0)
    return jnp.clip(result, -3.0, 3.0).astype(jnp.float32)


def plant(array, own_key, smallest, top_value):
    longest = array.shape.index(max(array.shape))
    spots = []
    for shift in (0, 1):
        where = [jax.random.randint(jax.random.fold_in(own_key, axis), (), 0, length) for axis, length in enumerate(array.shape)]
        where[longest] = (where[longest] + shift) % array.shape[longest]
        spots.append(tuple(where))
    return array.at[spots[0]].set(smallest).at[spots[1]].set(top_value)


def levels(own_key, dims, shards, least, largest):
    gain, own = 1.0, jax.random.fold_in(own_key, 6)
    for axis_at, shards_of in shards:
        heights = jnp.exp(jax.random.uniform(jax.random.fold_in(own, axis_at), (shards_of,), jnp.float32, least / len(shards), largest / len(shards)))
        gain = gain * jnp.repeat(heights, dims[axis_at] // shards_of).reshape([-1 if axis == axis_at else 1 for axis in range(len(dims))])
    return gain


def split_up(number_of, total, most, lean):
    weights = [(1 << 20) // math.isqrt(rank ** lean) + 1 for rank in range(2, number_of + 1)]
    surplus, holding = total - most - (number_of - 1), [1] * (number_of - 1)
    while surplus > 0:
        movable = [i for i in range(number_of - 1) if holding[i] < most]
        whole, budget = sum([weights[i] for i in movable]), surplus
        for i in movable:
            extra = min(most - holding[i], max(1, budget * weights[i] // whole), surplus)
            holding[i] = holding[i] + extra
            surplus = surplus - extra
    return np.array([most] + holding)


def ragged_sizes(stream_key, count, total, most, slope):
    if count == 2:
        one = jax.random.randint(stream_key, (), max(1, total - most), min(most, total - 1) + 1)
        return jnp.stack([one, total - one])
    sizes = jnp.asarray(split_up(count, total, most, slope), jnp.int32)
    twos = (count - 1) // 2
    giver, sink = sizes[1:1 + 2 * twos:2], sizes[2:2 + 2 * twos:2]
    room = jnp.minimum(giver - 1, most - sink)
    passed = jax.random.randint(jax.random.fold_in(stream_key, 1), (twos,), 0, 1 << 20) % (room + 1)
    sizes = sizes.at[1:1 + 2 * twos:2].set(giver - passed).at[2:2 + 2 * twos:2].set(sink + passed)
    return sizes[jax.random.permutation(jax.random.fold_in(stream_key, 2), count)]


def normal_values(rng, shape, scale, reach, shards=(), held_as=jnp.bfloat16):
    level = levels(rng, shape, shards, -0.22, 0.18) if shards else 1.0
    values = jax.random.normal(rng, shape, jnp.float32) * scale * level
    return jnp.minimum(jnp.maximum(values, -reach), reach).astype(held_as)


def setup_inputs(seed: int = 0) -> dict:
    key_list = jax.random.split(jax.random.key(seed), 14)
    image_hidden = draw_image_hidden(jax.random.fold_in(key_list[13], 71), 0)
    text_hidden = normal_values(key_list[1], (2, REQ, TXT, D), 1.0, 6.0, ((0, 2), (1, 4), (2, 4)))
    modulation = draw_modulation(jax.random.fold_in(key_list[13], 71), 0)
    attn_weight = draw_attn_weight(jax.random.fold_in(key_list[13], 71), 0)
    proj_weight = normal_values(key_list[4], (HEADS * HEAD, D), (HEADS * HEAD) ** -0.5, 0.1875)
    mlp_in_weight = normal_values(key_list[5], (D, FF), D ** -0.5, 0.15625, ((1, 4),))
    mlp_out_weight = normal_values(key_list[6], (FF, D), FF ** -0.5, 0.078125, ((0, 4),))
    final_weight = normal_values(key_list[7], (PATCH, D), D ** -0.5, 0.15625)
    latents = normal_values(key_list[8], (REQ, PATCH, IMG), 1.0, 6.0, ((0, 4), (1, 2), (2, 4)), jnp.float32)
    guidance = jnp.clip(3.0 + 4.0 * jax.random.uniform(key_list[9], (REQ,), jnp.float32) ** levels(key_list[9], (REQ,), ((0, 4),), -0.2, 0.2), 3.0, 7.0)
    text_lengths = jax.vmap(lambda own: ragged_sizes(own, REQ, (TXT_MAX // 2) * (REQ + 1), TXT_MAX, 0))(jax.random.split(key_list[10], 2)).reshape((2, REQ)).astype(jnp.int32)
    step_index = plant(jax.random.randint(key_list[11], (REQ,), 0, STEPS), jax.random.fold_in(key_list[11], 1), 0, STEPS - 1).astype(jnp.int32)
    step_count = plant(jax.random.randint(key_list[12], (REQ,), 1, 4), jax.random.fold_in(key_list[12], 1), 1, 3).astype(jnp.int32)
    return dict(image_hidden=image_hidden, text_hidden=text_hidden, modulation=modulation, attn_weight=attn_weight, proj_weight=proj_weight, mlp_in_weight=mlp_in_weight, mlp_out_weight=mlp_out_weight, final_weight=final_weight, latents=latents, guidance=guidance, text_lengths=text_lengths, step_index=step_index, step_count=step_count)


EPS_NORM = 1e-06

def modulate(rows_in, scale_row, shift_row):
    values = rows_in.astype(jnp.float32)
    center = lax.optimization_barrier(jnp.mean(values, axis=-1, keepdims=True))
    spread = lax.optimization_barrier(jnp.mean(jnp.square(values - center), axis=-1, keepdims=True))
    return ((values - center) * lax.rsqrt(spread + EPS_NORM) * (1.0 + scale_row) + shift_row).astype(jnp.bfloat16)

def sigma_of(index):
    remain = 1.0 - index.astype(jnp.float32) / STEPS
    return 3.0 * remain / (1.0 + 2.0 * remain)

def mlp_part(hidden, mod_rows, mlp_in_weight, mlp_out_weight):
    mlp_norm = modulate(hidden, mod_rows[8], mod_rows[7])
    inner = jax.nn.gelu(jnp.dot(mlp_norm, mlp_in_weight, preferred_element_type=jnp.float32), approximate=True).astype(jnp.bfloat16)
    units = FF // N_SEQ
    inner_groups = jnp.transpose(inner.reshape(IMG, N_SEQ, units), (1, 0, 2))
    weight_groups = mlp_out_weight.reshape(N_SEQ, units, D)

    def add_group(carry, items):
        inner_group, weight_group = items
        partial_sum = jnp.dot(inner_group, weight_group, preferred_element_type=jnp.float32).astype(jnp.bfloat16)
        return (carry + partial_sum.astype(jnp.float32), None)
    mlp_out, unused = lax.scan(add_group, jnp.zeros((IMG, D), jnp.float32), (inner_groups, weight_groups))
    return hidden + mod_rows[9] * mlp_out

def branch_velocity(image_rows, text_rows, mod_rows, length, attn_weight, proj_weight, mlp_in_weight, mlp_out_weight, final_weight):
    image_norm = modulate(image_rows, mod_rows[1], mod_rows[0])
    text_norm = modulate(text_rows, mod_rows[4], mod_rows[3])
    split_cols = attn_weight.reshape(D, HEADS, 5, HEAD)
    image_cols = split_cols[:, :, 0:3, :].reshape(D, HEADS * 3 * HEAD)
    text_cols = split_cols[:, :, 3:5, :].reshape(D, HEADS * 2 * HEAD)
    image_qkv = jnp.dot(image_norm, image_cols, preferred_element_type=jnp.float32).astype(jnp.bfloat16)
    image_qkv = image_qkv.reshape(IMG, HEADS, 3, HEAD)
    text_kv = jnp.dot(text_norm, text_cols, preferred_element_type=jnp.float32).astype(jnp.bfloat16)
    text_kv = text_kv.reshape(TXT, HEADS, 2, HEAD)
    keys_all = jnp.concatenate([image_qkv[:, :, 1], text_kv[:, :, 0]], axis=0)
    values_all = jnp.concatenate([image_qkv[:, :, 2], text_kv[:, :, 1]], axis=0)
    slots = jnp.arange(TXT, dtype=jnp.int32)
    valid = jnp.concatenate([jnp.ones((IMG,), dtype=bool), slots < length])
    queries = jnp.transpose(image_qkv[:, :, 0], (1, 0, 2))
    keys_all = jnp.transpose(keys_all, (1, 0, 2))
    values_all = jnp.transpose(values_all, (1, 0, 2))

    def one_head(items):
        query_head, key_head, value_head = items
        scores = jnp.dot(query_head, key_head.T, preferred_element_type=jnp.float32) * HEAD ** (-0.5)
        scores = jnp.where(valid[None, :], scores, -1e+30)
        row_max = lax.optimization_barrier(jnp.max(scores, axis=1, keepdims=True))
        weights = jnp.exp(scores - row_max)
        total = lax.optimization_barrier(jnp.sum(weights, axis=1, keepdims=True))
        probs = weights.astype(jnp.bfloat16)
        return (jnp.dot(probs, value_head, preferred_element_type=jnp.float32) / total).astype(jnp.bfloat16)
    attended = lax.map(one_head, (queries, keys_all, values_all))
    attended = jnp.transpose(attended, (1, 0, 2)).reshape(IMG, HEADS * HEAD)
    hidden = image_rows.astype(jnp.float32) + mod_rows[2] * jnp.dot(attended, proj_weight, preferred_element_type=jnp.float32)
    block_out = mlp_part(hidden, mod_rows, mlp_in_weight, mlp_out_weight)
    final_norm = modulate(block_out, mod_rows[6], mod_rows[5])
    return jnp.dot(final_weight, final_norm.T, preferred_element_type=jnp.float32)

def reference(image_hidden, text_hidden, modulation, attn_weight, proj_weight, mlp_in_weight, mlp_out_weight, final_weight, latents, guidance, text_lengths, step_index, step_count):

    def per_request(items):
        image_pair, text_pair, mod_pair, length_pair, guide_one, latent_one, index_one, count_one = items
        cond_vel = branch_velocity(image_pair[0], text_pair[0], mod_pair[0], length_pair[0], attn_weight, proj_weight, mlp_in_weight, mlp_out_weight, final_weight)
        uncond_vel = branch_velocity(image_pair[1], text_pair[1], mod_pair[1], length_pair[1], attn_weight, proj_weight, mlp_in_weight, mlp_out_weight, final_weight)
        guided = uncond_vel + guide_one * (cond_vel - uncond_vel)
        entries = PATCH * IMG
        rms_cond = jnp.sqrt(jnp.sum(cond_vel * cond_vel) / entries + EPS_NORM)
        rms_guided = jnp.sqrt(jnp.sum(guided * guided) / entries + EPS_NORM)
        result_vel = 0.7 * (guided * (rms_cond / rms_guided)) + 0.3 * guided
        next_index = jnp.minimum(index_one + count_one, STEPS)
        step_size = sigma_of(next_index) - sigma_of(index_one)
        return (result_vel, latent_one + step_size * result_vel)
    velocity, new_latents = lax.map(per_request, (jnp.swapaxes(image_hidden, 0, 1), jnp.swapaxes(text_hidden, 0, 1), jnp.swapaxes(modulation, 0, 1), jnp.swapaxes(text_lengths, 0, 1), guidance, latents, step_index, step_count))
    return (velocity, new_latents)
```

```python
import functools
import math

import jax
import jax.numpy as jnp
from jax import lax
from jax.experimental import pallas as pl
from jax.experimental.pallas import tpu as pltpu
from jax.sharding import PartitionSpec as P

HEADS = 16
HEAD = 64
STEPS = 28


EPS_NORM = 1e-06


def partner(value, axis, distance):
    mask = 2**distance
    pairs = [(source, source ^ mask) for source in range(lax.axis_size(axis))]
    return lax.ppermute(value, axis, pairs)


def shifted(value, axis, shift):
    size = lax.axis_size(axis)
    return lax.ppermute(value, axis, [(source, (source - shift) % size) for source in range(size)])


def modulate(rows_in, scale_row, shift_row):
    values = rows_in.astype(jnp.float32)
    center = jnp.mean(values, axis=-1, keepdims=True)
    spread = jnp.mean(jnp.square(values - center), axis=-1, keepdims=True)
    return (
        (values - center) * lax.rsqrt(spread + EPS_NORM) * (1.0 + scale_row) + shift_row
    ).astype(jnp.bfloat16)


def sigma_of(index):
    remain = 1.0 - index.astype(jnp.float32) / STEPS
    return 3.0 * remain / (1.0 + 2.0 * remain)


def split_columns(weight_piece):
    width_in = weight_piece.shape[0]
    head_count = weight_piece.shape[1] // (5 * HEAD)
    shaped = weight_piece.reshape(width_in, head_count, 5, HEAD)
    image_cols = shaped[:, :, 0:3, :].reshape(width_in, head_count * 3 * HEAD)
    text_cols = shaped[:, :, 3:5, :].reshape(width_in, head_count * 2 * HEAD)
    return (image_cols, text_cols)


def local(
    image_hidden,
    text_hidden,
    modulation,
    attn_weight,
    proj_weight,
    mlp_in_weight,
    mlp_out_weight,
    final_weight,
    latents,
    guidance,
    text_lengths,
    step_index,
    step_count,
):
    seq_size = lax.axis_size("seq")
    local_heads = HEADS // seq_size
    image_rows = image_hidden[0, 0]
    text_rows = text_hidden[0, 0]
    mod_rows = modulation[0, 0]
    local_rows = image_rows.shape[0]
    image_total = local_rows * seq_size
    text_total = text_rows.shape[0] * seq_size
    image_norm = modulate(image_rows, mod_rows[1], mod_rows[0])
    text_norm = modulate(text_rows, mod_rows[4], mod_rows[3])
    seq_index = lax.axis_index("seq")
    own_norm = jnp.concatenate([image_norm, text_norm], axis=0)
    gathered = jnp.stack([own_norm] + [shifted(own_norm, "seq", k) for k in range(1, seq_size)])
    image_all = gathered[:, :local_rows].reshape(image_total, -1)
    text_all = gathered[:, local_rows:].reshape(text_total, -1)
    image_cols, text_cols = split_columns(attn_weight)
    image_qkv = jnp.dot(image_all, image_cols, preferred_element_type=jnp.float32).astype(
        jnp.bfloat16
    )
    text_kv = jnp.dot(text_all, text_cols, preferred_element_type=jnp.float32).astype(
        jnp.bfloat16
    )
    image_qkv = image_qkv.reshape(image_total, local_heads, 3, HEAD)
    text_kv = text_kv.reshape(text_total, local_heads, 2, HEAD)
    keys_all = jnp.concatenate([image_qkv[:, :, 1], text_kv[:, :, 0]], axis=0)
    values_all = jnp.concatenate([image_qkv[:, :, 2], text_kv[:, :, 1]], axis=0)
    text_local = text_rows.shape[0]
    sources = (seq_index + jnp.arange(seq_size, dtype=jnp.int32)) % seq_size
    slots = (sources[:, None] * text_local + jnp.arange(text_local, dtype=jnp.int32)).reshape(-1)
    valid = jnp.concatenate([jnp.ones((image_total,), dtype=bool), slots < text_lengths[0, 0]])
    block_rows = local_rows
    while block_rows < 512 and image_total % (block_rows * 2) == 0:
        block_rows = block_rows * 2
    block_total = image_total // block_rows
    query_blocks = image_qkv[:, :, 0].reshape(block_total, block_rows, local_heads, HEAD)

    def attend(query_block):
        scores = jnp.einsum(
            "qhe,khe->hqk", query_block, keys_all, preferred_element_type=jnp.float32
        ) * HEAD ** (-0.5)
        scores = jnp.where(valid[None, None, :], scores, -1e30)
        row_max = jnp.max(scores, axis=2, keepdims=True)
        weights = jnp.exp(scores - row_max)
        total = jnp.sum(weights, axis=2, keepdims=True)
        probs = weights.astype(jnp.bfloat16)
        mixed = (
            jnp.einsum("hqk,khe->hqe", probs, values_all, preferred_element_type=jnp.float32)
            / total
        )
        return jnp.transpose(mixed.astype(jnp.bfloat16), (1, 0, 2))

    attended = lax.map(attend, query_blocks).reshape(image_total, local_heads * HEAD)
    attended = attended.reshape(seq_size, local_rows, local_heads * HEAD)
    head_width = local_heads * HEAD
    projected = jnp.zeros((local_rows, proj_weight.shape[1]), jnp.float32)
    for k in range(seq_size):
        piece = attended[k] if k == 0 else shifted(attended[k], "seq", -k)
        rows = lax.dynamic_slice_in_dim(
            proj_weight, ((seq_index - k) % seq_size) * head_width, head_width, 0
        )
        projected = projected + jnp.dot(piece, rows, preferred_element_type=jnp.float32)
    hidden = image_rows.astype(jnp.float32) + mod_rows[2] * projected
    mlp_norm = modulate(hidden, mod_rows[8], mod_rows[7])
    mlp_out = jnp.zeros((local_rows, mlp_out_weight.shape[1]), jnp.float32)
    for k in range(seq_size):
        piece = mlp_norm if k == 0 else shifted(mlp_norm, "seq", k)
        inner = jax.nn.gelu(
            jnp.dot(piece, mlp_in_weight, preferred_element_type=jnp.float32), approximate=True
        ).astype(jnp.bfloat16)
        part = jnp.dot(inner, mlp_out_weight, preferred_element_type=jnp.float32).astype(
            jnp.bfloat16
        )
        part = part if k == 0 else shifted(part, "seq", -k)
        mlp_out = mlp_out + part.astype(jnp.float32)
    block_out = hidden + mod_rows[9] * mlp_out
    final_norm = modulate(block_out, mod_rows[6], mod_rows[5])
    own_vel = lax.dot_general(
        final_weight, final_norm, (((1,), (1,)), ((), ())), preferred_element_type=jnp.float32
    )
    partner_vel = partner(own_vel.astype(jnp.bfloat16), "cfg", 0).astype(own_vel.dtype)
    leading = lax.axis_index("cfg") == 0
    cond_vel = jnp.where(leading, own_vel, partner_vel)
    uncond_vel = jnp.where(leading, partner_vel, own_vel)
    guided = uncond_vel + guidance[0] * (cond_vel - uncond_vel)
    squares = jnp.stack([jnp.sum(cond_vel * cond_vel), jnp.sum(guided * guided)])
    squares = sum(
        [squares] + [shifted(squares, "seq", k) for k in range(1, seq_size)], jnp.zeros(2)
    )
    cond_sq, guided_sq = squares[0], squares[1]
    entries = own_vel.shape[0] * image_total
    rms_cond = jnp.sqrt(cond_sq / entries + EPS_NORM)
    rms_guided = jnp.sqrt(guided_sq / entries + EPS_NORM)
    result_vel = 0.7 * (guided * (rms_cond / rms_guided)) + 0.3 * guided
    channel_half = latents.shape[1]
    channel_start = lax.axis_index("cfg") * channel_half
    own_channels = lax.dynamic_slice_in_dim(result_vel, channel_start, channel_half, 0)
    next_index = jnp.minimum(step_index[0] + step_count[0], STEPS)
    step_size = sigma_of(next_index) - sigma_of(step_index[0])
    moved = latents[0] + step_size * own_channels
    return (own_channels[None], moved[None])


BF16 = jnp.bfloat16
F32 = jnp.float32
MESH_ID = pl.DeviceIdType.MESH
EXP_SCALE = math.log2(math.e) * HEAD ** (-0.5)
TILE = 256


def normalised(values, scale_row, shift_row):
    center = jnp.mean(values, axis=-1, keepdims=True)
    moved = values - center
    spread = jnp.mean(moved * moved, axis=-1, keepdims=True)
    return moved * lax.rsqrt(spread + EPS_NORM) * (1.0 + scale_row) + shift_row


def gelu_tanh(v):
    return 0.5 * v * (1.0 + jnp.tanh(0.7978845608028654 * (v + 0.044715 * (v * v * v))))


def fused_kernel(
    unit_plan,
    image,
    text,
    mod,
    wa_hbm,
    wp_hbm,
    wi_hbm,
    wo_hbm,
    final_w,
    latents,
    guidance,
    text_len,
    step_index,
    step_count,
    vel_ref,
    new_ref,
    wa_own,
    wi_own,
    wo_own,
    wp,
    wa_far,
    wi_far,
    wo_far,
    hid,
    nrm,
    txt,
    txt_out,
    txt_in,
    q_s,
    k_s,
    v_s,
    kt_s,
    vt_s,
    att,
    hs,
    inner,
    rs,
    rr,
    mo,
    vel_own,
    vel_oth,
    pay_out,
    pay_in,
    sum_in,
    w_r,
    w_s,
    i_r,
    i_s,
    t_r,
    t_s,
    o_r,
    o_s,
    r_r,
    r_s,
    f_r,
    f_s,
    l_s,
):
    c = lax.axis_index("cfg")
    r = lax.axis_index("req")
    s = lax.axis_index("seq")
    half = s // 2
    is_mid = (s == 1) | (s == 2)
    om = 3 - s
    pe = half * 3
    oe = 3 - pe
    near_mid = 1 + half
    far_mid = 2 - half
    rows_local = image.shape[0]
    rows_all = hid.shape[0]
    near_rows = 2 * rows_local
    width = image.shape[1]
    piece = width // 8
    text_local = text.shape[0]
    text_all = txt.shape[0]

    rx = lax.rem(r + 2, 4)
    rc = r + 1 - 2 * lax.rem(r, 2)
    rcx = lax.rem(rc + 2, 4)
    cy = 1 - c
    dev_x = (c, rx, s)
    dev_y = (cy, r, s)
    dev_c = (c, rc, s)
    dev_om = (c, r, om)
    dev_pe = (c, r, pe)
    dev_oe = (c, r, oe)
    dev_near = (c, r, near_mid)
    dev_far = (c, r, far_mid)

    def rcopy(src, dst, ssem, rsem, dev):
        return pltpu.make_async_remote_copy(
            src_ref=src, dst_ref=dst, send_sem=ssem, recv_sem=rsem, device_id=dev, device_id_type=MESH_ID
        )

    def rows_of(first, count, align):
        return pl.ds(pl.multiple_of(first, align), count)

    own_rows = rows_of(s * rows_local, rows_local, 128)
    weights = {"a": (wa_hbm, wa_far), "i": (wi_hbm, wi_far), "o": (wo_hbm, wo_far)}
    units = len(unit_plan)

    def piece_rows(cc, rr_, first=0, count=None):
        start = (cc * 4 + rr_) * piece + first
        return rows_of(start, piece if count is None else count, 32)

    def wcopy(u, k, rows, dev, src=None):
        kind, col, ncol = unit_plan[u]
        far = weights[kind][1]
        at = far.at[rows, pl.ds(col, ncol)]
        return rcopy(at if src is None else src, at, w_s.at[u, k], w_r.at[u, k], dev)

    hp = piece // 2

    def w_step(u, step):
        if u < 0 or u >= units:
            return
        if step == 1:
            mine = piece_rows(c, r)
            wcopy(u, 0, mine, dev_pe).wait_recv()
            wcopy(u, 1, mine, dev_x).start()
            wcopy(u, 2, mine, dev_y).start()
            wcopy(u, 5, mine, dev_c).start()
        elif step == 2:
            wcopy(u, 1, piece_rows(c, rx), dev_x).wait_recv()
            wcopy(u, 3, piece_rows(c, rx, 0, hp), dev_y).start()
            wcopy(u, 2, piece_rows(cy, r), dev_y).wait_recv()
            wcopy(u, 4, piece_rows(cy, r, hp, hp), dev_x).start()
            wcopy(u, 6, piece_rows(c, rx), dev_c).start()
            wcopy(u, 7, piece_rows(cy, r), dev_c).start()
        elif step == 3:
            wcopy(u, 3, piece_rows(cy, rx, 0, hp), dev_y).wait_recv()
            wcopy(u, 4, piece_rows(cy, rx, hp, hp), dev_x).wait_recv()
            wcopy(u, 8, piece_rows(cy, rx), dev_c).start()
        elif step == 4:
            wcopy(u, 5, piece_rows(c, rc), dev_c).wait_recv()
            wcopy(u, 6, piece_rows(c, rcx), dev_c).wait_recv()
            wcopy(u, 7, piece_rows(cy, rc), dev_c).wait_recv()
            wcopy(u, 8, piece_rows(cy, rcx), dev_c).wait_recv()

    def w_sent(u):
        mine = piece_rows(c, r)
        wcopy(u, 1, mine, dev_x).wait_send()
        wcopy(u, 2, mine, dev_y).wait_send()
        wcopy(u, 5, mine, dev_c).wait_send()
        wcopy(u, 3, piece_rows(c, rx, 0, hp), dev_y).wait_send()
        wcopy(u, 4, piece_rows(cy, r, hp, hp), dev_x).wait_send()
        wcopy(u, 6, piece_rows(c, rx), dev_c).wait_send()
        wcopy(u, 7, piece_rows(cy, r), dev_c).wait_send()
        wcopy(u, 8, piece_rows(cy, rx), dev_c).wait_send()

    chunks = 4
    chunk = rows_local // chunks

    def end_image(k):
        src = image.at[pl.ds(k * chunk, chunk)]
        dst = hid.at[rows_of(s * rows_local + k * chunk, chunk, 32)]
        return rcopy(src, dst, i_s.at[k], i_r.at[k], dev_near)

    def pe_rows(k):
        return hid.at[rows_of(pe * rows_local + k * chunk, chunk, 32)]

    def oe_rows(k):
        return hid.at[rows_of(oe * rows_local + k * chunk, chunk, 32)]

    def forward_image(k):
        rcopy(pe_rows(k), pe_rows(k), i_s.at[k], i_r.at[k], dev_om).wait_recv()
        rcopy(pe_rows(k), pe_rows(k), i_s.at[chunks + k], i_r.at[chunks + k], dev_om).start()

    own_image = rcopy(image, hid.at[own_rows], i_s.at[2 * chunks], i_r.at[2 * chunks], dev_om)
    text_to_mid = rcopy(txt_out, txt_in, t_s.at[0], t_r.at[0], dev_near)

    def text_half(which):
        return txt.at[rows_of(which * 2 * text_local, 2 * text_local, 16)]

    def att_copy(j, pair):
        return rcopy(att.at[pair], att.at[pair], o_s.at[j], o_r.at[j], dev_om)

    out_units = [u for u in range(units) if unit_plan[u][0] == "o"]

    def r_copy(j):
        cols = pl.ds(unit_plan[out_units[j]][1], unit_plan[out_units[j]][2])
        return rcopy(rs.at[:, cols], rr.at[:, cols], r_s.at[j], r_r.at[j], dev_om)

    vel_copy = rcopy(vel_own, vel_oth, f_s.at[0], f_r.at[0], dev_y)
    pay_copy = rcopy(pay_out, pay_in, f_s.at[1], f_r.at[1], dev_pe)
    sums_at = pay_out.at[pl.ds(32, 8)]
    sum_copy_om = rcopy(sums_at, sum_in, f_s.at[2], f_r.at[2], dev_om)
    sum_copy_oe = rcopy(sums_at, sum_in, f_s.at[3], f_r.at[2], dev_oe)

    def load(i, src, dst):
        return pltpu.make_async_copy(src, dst, l_s.at[i])

    loads = [
        load(0, image, hid.at[own_rows]),
        load(1, wa_hbm, wa_own),
        load(2, wp_hbm, wp),
        load(3, wi_hbm, wi_own),
        load(4, wo_hbm, wo_own),
    ]

    barrier = pltpu.get_barrier_semaphore()

    def greet(devs):
        for dev in devs:
            pl.semaphore_signal(barrier, inc=1, device_id=dev, device_id_type=MESH_ID)

    @pl.when(is_mid)
    def _():
        for item in loads:
            item.start()
        greet((dev_pe, dev_om, dev_oe, dev_x, dev_y, dev_c))

    @pl.when(jnp.logical_not(is_mid))
    def _():
        greet((dev_near, dev_far))

    text_norm = normalised(text[...].astype(F32), mod[4:5, :], mod[3:4, :])
    pad = txt_out.shape[0] - text_local
    txt_out[...] = jnp.concatenate([text_norm, jnp.zeros((pad, width), F32)], axis=0).astype(BF16)

    def finish(guided_half, sums):
        entries = 2.0 * guided_half.shape[0] * rows_all
        rms_cond = jnp.sqrt(sums[0:1, :] / entries + EPS_NORM)
        rms_guided = jnp.sqrt(sums[4:5, :] / entries + EPS_NORM)
        velocity = 0.7 * (guided_half * (rms_cond / rms_guided)) + 0.3 * guided_half
        zero = jnp.zeros(guided_half.shape, F32)
        now = step_index[0]
        after = jnp.minimum(now + step_count[0], STEPS)

        def sigma(i):
            remain = 1.0 - (zero + i.astype(F32)) / STEPS
            return 3.0 * remain / (1.0 + 2.0 * remain)

        vel_ref[...] = velocity
        new_ref[...] = latents[...] + (sigma(after) - sigma(now)) * velocity

    @pl.when(jnp.logical_not(is_mid))
    def _():
        pl.semaphore_wait(barrier, 2)

        def unit_send(u):
            kind, col, ncol = unit_plan[u]
            mine = piece_rows(c, r)
            src = weights[kind][0].at[mine, pl.ds(col, ncol)]
            return wcopy(u, 0, mine, dev_near, src)

        order = []
        head = [unit_send(u) for u in range(5)]
        order += [head[0], end_image(0), head[1], end_image(1), head[2], end_image(2)]
        order += [text_to_mid, end_image(3), head[3], head[4]]
        order += [unit_send(u) for u in range(5, units)]
        for at, item in enumerate(order):
            item.start()
            if at >= 1:
                order[at - 1].wait_send()
        order[-1].wait_send()
        pay_copy.wait_recv()
        sum_copy_oe.wait_recv()
        finish(pay_in[0:32, :], pay_in[32:40, :] + sum_in[...])

    @pl.when(is_mid)
    def _():
        pl.semaphore_wait(barrier, 6)
        own_image.start()

        def norm_rows(first, count, read, scale, shift):
            @pl.loop(0, count // 32)
            def _(b):
                at = first + b * 32
                out = normalised(read(at), mod[scale : scale + 1, :], mod[shift : shift + 1, :])
                nrm[rows_of(at, 32, 32), :] = out.astype(BF16)

        def read_hid(at):
            return hid[rows_of(at, 32, 32), :].astype(F32)

        def read_hs(at):
            return hs[rows_of(at, 32, 32), :]

        def qkv(rows, w, base):
            @pl.loop(0, 2)
            def _(p):
                cols = rows_of(p * 10 * HEAD, 10 * HEAD, 128)
                y = jnp.dot(nrm[rows, :], w[:, cols], preferred_element_type=F32)
                for j in range(2):
                    o = j * 5 * HEAD
                    head = base + 2 * p + j
                    q_s[head, rows, :] = y[:, o : o + HEAD].astype(BF16)
                    k_s[head, rows, :] = y[:, o + HEAD : o + 2 * HEAD].astype(BF16)
                    v_s[head, rows, :] = y[:, o + 2 * HEAD : o + 3 * HEAD].astype(BF16)

        def text_kv(w, base):
            @pl.loop(0, 2)
            def _(p):
                cols = rows_of(p * 10 * HEAD, 10 * HEAD, 128)
                y = jnp.dot(txt[...], w[:, cols], preferred_element_type=F32)
                for j in range(2):
                    o = j * 5 * HEAD + 3 * HEAD
                    head = base + 2 * p + j
                    kt_s[head] = y[:, o : o + HEAD].astype(BF16)
                    vt_s[head] = y[:, o + HEAD : o + 2 * HEAD].astype(BF16)

        slots = lax.broadcasted_iota(jnp.int32, (1, text_all), 1)
        valid = slots < text_len[0, 0]
        nt = (((1,), (1,)), ((), ()))

        def attend(slot, pair):
            @pl.loop(0, rows_all // TILE)
            def _(b):
                rows = rows_of(b * TILE, TILE, TILE)
                parts = []
                for j in range(2):
                    head = slot + j
                    query = q_s[head, rows, :]
                    s_i = lax.dot_general(query, k_s[head], nt, preferred_element_type=F32)
                    s_t = lax.dot_general(query, kt_s[head], nt, preferred_element_type=F32)
                    s_t = jnp.where(valid, s_t, -1e30)
                    top = jnp.maximum(
                        jnp.max(s_i, axis=1, keepdims=True), jnp.max(s_t, axis=1, keepdims=True)
                    )
                    p_i = jnp.exp2((s_i - top) * EXP_SCALE)
                    p_t = jnp.exp2((s_t - top) * EXP_SCALE)
                    total = jnp.sum(p_i, axis=1, keepdims=True) + jnp.sum(p_t, axis=1, keepdims=True)
                    mixed = jnp.dot(p_i.astype(BF16), v_s[head], preferred_element_type=F32)
                    mixed += jnp.dot(p_t.astype(BF16), vt_s[head], preferred_element_type=F32)
                    parts.append(mixed / total)
                att[pair, rows, :] = jnp.concatenate(parts, axis=1).astype(BF16)

        def block(plane):
            return rows_of(plane * rows_local, rows_local, 128)

        def project(first):
            rows = rows_of(first, near_rows, TILE)
            @pl.loop(0, width // TILE)
            def _(t):
                cols = rows_of(t * TILE, TILE, TILE)
                lhs = jnp.concatenate([att[p, rows, :] for p in range(att.shape[0])], axis=1)
                y = jnp.dot(lhs, wp[:, cols], preferred_element_type=F32)
                hs[rows, cols] = hid[rows, cols].astype(F32) + mod[2:3, cols] * y

        def mlp_in(first, w, base):
            rows = rows_of(first, near_rows, TILE)
            @pl.loop(0, width // TILE)
            def _(t):
                cols = rows_of(t * TILE, TILE, TILE)
                y = jnp.dot(nrm[rows, :], w[:, cols], preferred_element_type=F32)
                inner[rows, rows_of(base + t * TILE, TILE, TILE)] = gelu_tanh(y).astype(BF16)

        def mlp_out(first, col, ncol, far):
            rows = rows_of(first, near_rows, TILE)
            @pl.loop(0, ncol // TILE)
            def _(t):
                cols = rows_of(col + t * TILE, TILE, TILE)
                y = jnp.dot(inner[rows, 0:width], wo_own[:, cols], preferred_element_type=F32)
                y += jnp.dot(inner[rows, width : 2 * width], wo_far[:, cols], preferred_element_type=F32)
                if far:
                    rs[:, cols] = y.astype(BF16)
                else:
                    mo[:, cols] = y

        near_first = half * near_rows
        far_first = (1 - half) * near_rows

        loads[0].wait()
        norm_rows(s * rows_local, rows_local, read_hid, 1, 0)
        loads[1].wait()
        qkv(block(s), wa_own, 0)
        w_step(0, 1)
        forward_image(0)
        w_step(0, 2)
        w_step(1, 1)
        w_step(0, 3)
        forward_image(1)
        own_image.wait_recv()
        norm_rows(om * rows_local, rows_local, read_hid, 1, 0)
        w_step(1, 2)
        w_step(2, 1)
        w_step(1, 3)
        forward_image(2)
        qkv(block(om), wa_own, 0)
        text_to_mid.wait_recv()
        theirs = txt_in[...].astype(F32)[0:text_local]
        mine = txt_out[...].astype(F32)[0:text_local]
        first = jnp.where(half == 0, theirs, mine)
        second = jnp.where(half == 0, mine, theirs)
        txt[rows_of(half * 2 * text_local, 2 * text_local, 16), :] = jnp.concatenate(
            [first, second], axis=0
        ).astype(BF16)
        text_send = rcopy(text_half(half), text_half(half), t_s.at[1], t_r.at[1], dev_om)
        text_send.start()
        w_step(2, 2)
        forward_image(3)
        w_step(2, 3)
        w_step(3, 1)
        norm_rows(pe * rows_local, rows_local, read_hid, 1, 0)
        qkv(block(pe), wa_own, 0)
        w_step(3, 2)
        w_step(4, 1)
        w_step(3, 3)
        for k in range(chunks):
            rcopy(oe_rows(k), oe_rows(k), i_s.at[chunks + k], i_r.at[chunks + k], dev_om).wait_recv()
        norm_rows(oe * rows_local, rows_local, read_hid, 1, 0)
        qkv(block(oe), wa_own, 0)
        rcopy(text_half(1 - half), text_half(1 - half), t_s.at[1], t_r.at[1], dev_om).wait_recv()
        text_kv(wa_own, 0)
        w_step(4, 2)
        attend(0, 2 * s)
        att_copy(0, 2 * s).start()
        w_step(4, 3)
        w_step(5, 1)
        attend(2, 2 * s + 1)
        att_copy(1, 2 * s + 1).start()
        for u in range(5):
            w_step(u, 4)

        @pl.loop(0, 4)
        def _(p):
            qkv(block(p), wa_far, 4)

        text_kv(wa_far, 4)
        w_step(5, 2)
        w_step(6, 1)
        attend(4, 2 * pe)
        att_copy(2, 2 * pe).start()
        w_step(5, 3)
        attend(6, 2 * pe + 1)
        att_copy(3, 2 * pe + 1).start()
        w_step(6, 2)
        w_step(7, 1)
        w_step(6, 3)
        loads[2].wait()
        att_copy(0, 2 * om).wait_recv()
        att_copy(1, 2 * om + 1).wait_recv()
        att_copy(2, 2 * oe).wait_recv()
        att_copy(3, 2 * oe + 1).wait_recv()
        project(far_first)
        w_step(7, 2)
        w_step(8, 1)
        norm_rows(far_first, near_rows, read_hs, 8, 7)
        loads[3].wait()
        mlp_in(far_first, wi_own, 0)
        w_step(7, 3)
        project(near_first)
        norm_rows(near_first, near_rows, read_hs, 8, 7)
        w_step(8, 2)
        w_step(9, 1)
        mlp_in(near_first, wi_own, 0)
        w_step(8, 3)
        for u in range(5, 8):
            w_step(u, 4)
        mlp_in(far_first, wi_far, width)
        w_step(9, 2)
        w_step(10, 1)
        mlp_in(near_first, wi_far, width)
        loads[4].wait()
        for j, u in enumerate(out_units):
            w_step(u + 1, 3)
            w_step(u, 4)
            mlp_out(far_first, unit_plan[u][1], unit_plan[u][2], True)
            r_copy(j).start()
            w_step(u + 2, 2)
            w_step(u + 3, 1)
            mlp_out(near_first, unit_plan[u][1], unit_plan[u][2], False)
        for j in range(len(out_units)):
            r_copy(j).wait_recv()

        @pl.loop(0, near_rows // 32)
        def _(b):
            at = near_first + b * 32
            here = rows_of(b * 32, 32, 32)
            rows = rows_of(at, 32, 32)
            value = hs[rows, :] + mod[9:10, :] * (mo[here, :] + rr[here, :].astype(F32))
            nrm[rows, :] = normalised(value, mod[6:7, :], mod[5:6, :]).astype(BF16)

        own_vel = lax.dot_general(
            final_w[...], nrm[rows_of(near_first, near_rows, TILE), :], nt, preferred_element_type=F32
        )
        vel_own[...] = own_vel
        vel_copy.start()
        vel_copy.wait_recv()
        oth_vel = vel_oth[...]
        cond = jnp.where(c == 0, own_vel, oth_vel)
        uncond = jnp.where(c == 0, oth_vel, own_vel)
        guided = uncond + guidance[0] * (cond - uncond)

        def total_of(v):
            return jnp.sum(jnp.sum(v * v, axis=1, keepdims=True), axis=0, keepdims=True)

        line = lax.broadcasted_iota(jnp.int32, (8, 128), 0)
        sums = jnp.where(line < 4, total_of(cond), total_of(guided))
        patch_half = pay_out.shape[0] - 8
        mine_half = jnp.where(c == 0, guided[0:patch_half, :], guided[patch_half:, :])
        low, high = mine_half[:, 0:rows_local], mine_half[:, rows_local:]
        pay_out[0:patch_half, :] = jnp.where(half == 0, low, high)
        pay_out[patch_half:, :] = sums
        sum_copy_om.start()
        sum_copy_oe.start()
        pay_copy.start()
        sum_copy_om.wait_recv()
        finish(jnp.where(half == 0, high, low), sums + sum_in[...])

        own_image.wait_send()
        for k in range(chunks):
            rcopy(pe_rows(k), pe_rows(k), i_s.at[chunks + k], i_r.at[chunks + k], dev_om).wait_send()
        text_send.wait_send()
        for j in range(4):
            att_copy(j, 2 * s).wait_send()
        for j in range(len(out_units)):
            r_copy(j).wait_send()
        for u in range(units):
            w_sent(u)
        vel_copy.wait_send()
        pay_copy.wait_send()
        sum_copy_om.wait_send()
        sum_copy_oe.wait_send()


def fused_local(
    image_hidden,
    text_hidden,
    modulation,
    attn_weight,
    proj_weight,
    mlp_in_weight,
    mlp_out_weight,
    final_weight,
    latents,
    guidance,
    text_lengths,
    step_index,
    step_count,
):
    rows, width = image_hidden.shape[2:]
    text_rows = text_hidden.shape[2]
    padded = -(-text_rows // 16) * 16
    cols_a = attn_weight.shape[1]
    units_here = mlp_in_weight.shape[1]
    plan = [("a", k * 256, 256) for k in range(cols_a // 256)]
    plan += [("i", k * 512, 512) for k in range(units_here // 512)]
    plan += [("o", k * 512, 512) for k in range(width // 512)]
    channels = latents.shape[1]
    heads = 2 * (HEADS // 4)
    near = 2 * rows
    count = len(plan)
    outs = sum(1 for item in plan if item[0] == "o")
    vmem = pl.BlockSpec(memory_space=pltpu.VMEM)
    anywhere = pl.BlockSpec(memory_space=pl.ANY)
    smem = pl.BlockSpec(memory_space=pltpu.SMEM)
    dma = pltpu.SemaphoreType.DMA
    velocity, moved = pl.pallas_call(
        functools.partial(fused_kernel, plan),
        out_shape=[jax.ShapeDtypeStruct((channels, rows), F32)] * 2,
        in_specs=[anywhere, vmem, vmem, anywhere, anywhere, anywhere, anywhere, vmem, vmem, smem, smem, smem, smem],
        out_specs=[vmem, vmem],
        scratch_shapes=[
            pltpu.VMEM((width, cols_a), BF16),
            pltpu.VMEM((width, units_here), BF16),
            pltpu.VMEM((units_here, width), BF16),
            pltpu.VMEM(proj_weight.shape, BF16),
            pltpu.VMEM((width, cols_a), BF16),
            pltpu.VMEM((width, units_here), BF16),
            pltpu.VMEM((units_here, width), BF16),
            pltpu.VMEM((4 * rows, width), BF16),
            pltpu.VMEM((4 * rows, width), BF16),
            pltpu.VMEM((4 * text_rows, width), BF16),
            pltpu.VMEM((padded, width), BF16),
            pltpu.VMEM((padded, width), BF16),
            pltpu.VMEM((heads, 4 * rows, HEAD), BF16),
            pltpu.VMEM((heads, 4 * rows, HEAD), BF16),
            pltpu.VMEM((heads, 4 * rows, HEAD), BF16),
            pltpu.VMEM((heads, 4 * text_rows, HEAD), BF16),
            pltpu.VMEM((heads, 4 * text_rows, HEAD), BF16),
            pltpu.VMEM((HEADS // 2, 4 * rows, 2 * HEAD), BF16),
            pltpu.VMEM((4 * rows, width), F32),
            pltpu.VMEM((4 * rows, 2 * units_here), BF16),
            pltpu.VMEM((near, width), BF16),
            pltpu.VMEM((near, width), BF16),
            pltpu.VMEM((near, width), F32),
            pltpu.VMEM((2 * channels, near), F32),
            pltpu.VMEM((2 * channels, near), F32),
            pltpu.VMEM((channels + 8, rows), F32),
            pltpu.VMEM((channels + 8, rows), F32),
            pltpu.VMEM((8, 128), F32),
            dma((count, 9)),
            dma((count, 9)),
            dma((9,)),
            dma((9,)),
            dma((2,)),
            dma((2,)),
            dma((4,)),
            dma((4,)),
            dma((outs,)),
            dma((outs,)),
            dma((3,)),
            dma((4,)),
            dma((5,)),
        ],
        compiler_params=pltpu.CompilerParams(
            collective_id=0, has_side_effects=True, vmem_limit_bytes=60 * 2**20
        ),
        cost_estimate=pl.CostEstimate(flops=15 * 10**9, bytes_accessed=17 * 10**6, transcendentals=5 * 10**6),
    )(
        image_hidden[0, 0],
        text_hidden[0, 0],
        modulation[0, 0],
        attn_weight,
        proj_weight,
        mlp_in_weight,
        mlp_out_weight,
        final_weight,
        latents[0],
        guidance,
        text_lengths,
        step_index,
        step_count,
    )
    return velocity[None], moved[None]


def solution(mesh):
    in_specs = (
        P("cfg", "req", "seq", None),
        P("cfg", "req", "seq", None),
        P("cfg", "req", None, None),
        P(None, "seq"),
        P(),
        P(None, "seq"),
        P("seq", None),
        P(),
        P("req", "cfg", "seq"),
        P("req"),
        P("cfg", "req"),
        P("req"),
        P("req"),
    )
    out_specs = (P("req", "cfg", "seq"), P("req", "cfg", "seq"))
    shape = dict(mesh.shape)
    line = shape == {"cfg": 2, "req": 4, "seq": 4}
    body = fused_local if line else local
    return jax.shard_map(body, mesh=mesh, in_specs=in_specs, out_specs=out_specs, check_vma=False)
```

```python
import functools
import math

import jax
import jax.numpy as jnp
from jax import lax
from jax.experimental import pallas as pl
from jax.experimental.pallas import tpu as pltpu
from jax.sharding import PartitionSpec as P

HEADS = 16
HEAD = 64
STEPS = 28


EPS_NORM = 1e-06


def partner(value, axis, distance):
    mask = 2**distance
    pairs = [(source, source ^ mask) for source in range(lax.axis_size(axis))]
    return lax.ppermute(value, axis, pairs)


def shifted(value, axis, shift):
    size = lax.axis_size(axis)
    return lax.ppermute(value, axis, [(source, (source - shift) % size) for source in range(size)])


def modulate(rows_in, scale_row, shift_row):
    values = rows_in.astype(jnp.float32)
    center = jnp.mean(values, axis=-1, keepdims=True)
    spread = jnp.mean(jnp.square(values - center), axis=-1, keepdims=True)
    return (
        (values - center) * lax.rsqrt(spread + EPS_NORM) * (1.0 + scale_row) + shift_row
    ).astype(jnp.bfloat16)


def sigma_of(index):
    remain = 1.0 - index.astype(jnp.float32) / STEPS
    return 3.0 * remain / (1.0 + 2.0 * remain)


def split_columns(weight_piece):
    width_in = weight_piece.shape[0]
    head_count = weight_piece.shape[1] // (5 * HEAD)
    shaped = weight_piece.reshape(width_in, head_count, 5, HEAD)
    image_cols = shaped[:, :, 0:3, :].reshape(width_in, head_count * 3 * HEAD)
    text_cols = shaped[:, :, 3:5, :].reshape(width_in, head_count * 2 * HEAD)
    return (image_cols, text_cols)


def local(
    image_hidden,
    text_hidden,
    modulation,
    attn_weight,
    proj_weight,
    mlp_in_weight,
    mlp_out_weight,
    final_weight,
    latents,
    guidance,
    text_lengths,
    step_index,
    step_count,
):
    seq_size = lax.axis_size("seq")
    local_heads = HEADS // seq_size
    image_rows = image_hidden[0, 0]
    text_rows = text_hidden[0, 0]
    mod_rows = modulation[0, 0]
    local_rows = image_rows.shape[0]
    image_total = local_rows * seq_size
    text_total = text_rows.shape[0] * seq_size
    image_norm = modulate(image_rows, mod_rows[1], mod_rows[0])
    text_norm = modulate(text_rows, mod_rows[4], mod_rows[3])
    seq_index = lax.axis_index("seq")
    own_norm = jnp.concatenate([image_norm, text_norm], axis=0)
    gathered = jnp.stack([own_norm] + [shifted(own_norm, "seq", k) for k in range(1, seq_size)])
    image_all = gathered[:, :local_rows].reshape(image_total, -1)
    text_all = gathered[:, local_rows:].reshape(text_total, -1)
    image_cols, text_cols = split_columns(attn_weight)
    image_qkv = jnp.dot(image_all, image_cols, preferred_element_type=jnp.float32).astype(
        jnp.bfloat16
    )
    text_kv = jnp.dot(text_all, text_cols, preferred_element_type=jnp.float32).astype(
        jnp.bfloat16
    )
    image_qkv = image_qkv.reshape(image_total, local_heads, 3, HEAD)
    text_kv = text_kv.reshape(text_total, local_heads, 2, HEAD)
    keys_all = jnp.concatenate([image_qkv[:, :, 1], text_kv[:, :, 0]], axis=0)
    values_all = jnp.concatenate([image_qkv[:, :, 2], text_kv[:, :, 1]], axis=0)
    text_local = text_rows.shape[0]
    sources = (seq_index + jnp.arange(seq_size, dtype=jnp.int32)) % seq_size
    slots = (sources[:, None] * text_local + jnp.arange(text_local, dtype=jnp.int32)).reshape(-1)
    valid = jnp.concatenate([jnp.ones((image_total,), dtype=bool), slots < text_lengths[0, 0]])
    block_rows = local_rows
    while block_rows < 512 and image_total % (block_rows * 2) == 0:
        block_rows = block_rows * 2
    block_total = image_total // block_rows
    query_blocks = image_qkv[:, :, 0].reshape(block_total, block_rows, local_heads, HEAD)

    def attend(query_block):
        scores = jnp.einsum(
            "qhe,khe->hqk", query_block, keys_all, preferred_element_type=jnp.float32
        ) * HEAD ** (-0.5)
        scores = jnp.where(valid[None, None, :], scores, -1e30)
        row_max = jnp.max(scores, axis=2, keepdims=True)
        weights = jnp.exp(scores - row_max)
        total = jnp.sum(weights, axis=2, keepdims=True)
        probs = weights.astype(jnp.bfloat16)
        mixed = (
            jnp.einsum("hqk,khe->hqe", probs, values_all, preferred_element_type=jnp.float32)
            / total
        )
        return jnp.transpose(mixed.astype(jnp.bfloat16), (1, 0, 2))

    attended = lax.map(attend, query_blocks).reshape(image_total, local_heads * HEAD)
    attended = attended.reshape(seq_size, local_rows, local_heads * HEAD)
    head_width = local_heads * HEAD
    projected = jnp.zeros((local_rows, proj_weight.shape[1]), jnp.float32)
    for k in range(seq_size):
        piece = attended[k] if k == 0 else shifted(attended[k], "seq", -k)
        rows = lax.dynamic_slice_in_dim(
            proj_weight, ((seq_index - k) % seq_size) * head_width, head_width, 0
        )
        projected = projected + jnp.dot(piece, rows, preferred_element_type=jnp.float32)
    hidden = image_rows.astype(jnp.float32) + mod_rows[2] * projected
    mlp_norm = modulate(hidden, mod_rows[8], mod_rows[7])
    mlp_out = jnp.zeros((local_rows, mlp_out_weight.shape[1]), jnp.float32)
    for k in range(seq_size):
        piece = mlp_norm if k == 0 else shifted(mlp_norm, "seq", k)
        inner = jax.nn.gelu(
            jnp.dot(piece, mlp_in_weight, preferred_element_type=jnp.float32), approximate=True
        ).astype(jnp.bfloat16)
        part = jnp.dot(inner, mlp_out_weight, preferred_element_type=jnp.float32).astype(
            jnp.bfloat16
        )
        part = part if k == 0 else shifted(part, "seq", -k)
        mlp_out = mlp_out + part.astype(jnp.float32)
    block_out = hidden + mod_rows[9] * mlp_out
    final_norm = modulate(block_out, mod_rows[6], mod_rows[5])
    own_vel = lax.dot_general(
        final_weight, final_norm, (((1,), (1,)), ((), ())), preferred_element_type=jnp.float32
    )
    partner_vel = partner(own_vel.astype(jnp.bfloat16), "cfg", 0).astype(own_vel.dtype)
    leading = lax.axis_index("cfg") == 0
    cond_vel = jnp.where(leading, own_vel, partner_vel)
    uncond_vel = jnp.where(leading, partner_vel, own_vel)
    guided = uncond_vel + guidance[...] * (cond_vel - uncond_vel)
    squares = jnp.stack([jnp.sum(cond_vel * cond_vel), jnp.sum(guided * guided)])
    squares = sum(
        [squares] + [shifted(squares, "seq", k) for k in range(1, seq_size)], jnp.zeros(2)
    )
    cond_sq, guided_sq = squares[0], squares[1]
    entries = own_vel.shape[0] * image_total
    rms_cond = jnp.sqrt(cond_sq / entries + EPS_NORM)
    rms_guided = jnp.sqrt(guided_sq / entries + EPS_NORM)
    result_vel = 0.7 * (guided * (rms_cond / rms_guided)) + 0.3 * guided
    channel_half = latents.shape[1]
    channel_start = lax.axis_index("cfg") * channel_half
    own_channels = lax.dynamic_slice_in_dim(result_vel, channel_start, channel_half, 0)
    next_index = jnp.minimum(step_index[0] + step_count[0], STEPS)
    step_size = sigma_of(next_index) - sigma_of(step_index[0])
    moved = latents[0] + step_size * own_channels
    return (own_channels[None], moved[None])


BF16 = jnp.bfloat16
F32 = jnp.float32
MESH_ID = pl.DeviceIdType.MESH
EXP_SCALE = math.log2(math.e) * HEAD ** (-0.5)
TILE = 256
UNITS = [
    ("a", 0, 256, "q"), ("a", 256, 256, "q"), ("a", 512, 256, "q"), ("a", 768, 256, "q"),
    ("a", 1024, 256, "q"), ("i", 0, 256, "q"), ("i", 256, 256, "q"), ("i", 512, 256, "q"),
    ("i", 768, 256, "q"), ("i", 1024, 256, "q"), ("i", 1280, 256, "q"), ("o", 0, 256, "y"),
    ("o", 256, 256, "x"), ("o", 512, 256, "q"), ("o", 768, 256, "q"), ("o", 1024, 256, "x"),
    ("o", 1280, 256, "y"),
]
FIRST_SENDS = [
    ("w", 0, 0), ("t",), ("i", 0), ("w", 1, 0), ("w", 2, 0), ("i", 1),
    ("w", 3, 0), ("w", 4, 0), ("i", 2), ("i", 3), ("w", 5, 0),
]
STREAM = [
    ("norm_own",), ("qkv_own",), ("w", 0, 1), ("tcomb",), ("w", 0, 2), ("f", 0),
    ("w", 0, 3), ("norm_om",), ("qkv_om",), ("w", 1, 1), ("w", 2, 1), ("w", 1, 2),
    ("f", 1), ("tkv_own",), ("w", 2, 2), ("w", 3, 1), ("w", 1, 3), ("w", 2, 3),
    ("w", 4, 1), ("w", 3, 2), ("f", 2), ("w", 4, 2), ("f", 3), ("norm_pe",),
    ("w", 3, 3), ("qkv_pe",), ("w", 5, 1), ("w", 4, 3), ("norm_oe",), ("qkv_oe",),
    ("w", 6, 1), ("att0",), ("w", 5, 2), ("w", 7, 1), ("att1",), ("w", 6, 2),
    ("w", 8, 1), ("w", 5, 3), ("qkvf0",), ("w", 9, 1), ("w", 7, 2), ("w", 10, 1),
    ("w", 6, 3), ("qkvf1",), ("w", 8, 2), ("tkv_far",), ("att2",), ("w", 11, 1),
    ("w", 9, 2), ("w", 7, 3), ("att3",), ("w", 10, 2), ("w", 12, 1), ("w", 8, 3),
    ("w", 13, 1), ("w", 14, 1), ("w", 11, 2), ("proj_f",), ("w", 9, 3), ("w", 10, 3),
    ("w", 12, 2), ("norm2_f",), ("w", 15, 1), ("in_f_own0",), ("w", 13, 2), ("in_f_own1",),
    ("w", 14, 2), ("in_f_far0",), ("w", 16, 1), ("in_f_far1",), ("out_f", 0), ("out_f", 1),
    ("w", 15, 2), ("proj_n",), ("w", 13, 3), ("w", 14, 3), ("out_f", 4), ("w", 16, 2),
    ("norm2_n",), ("out_f", 2), ("out_f", 3), ("out_f", 5), ("in_n_own0",), ("in_n_own1",),
    ("in_n_far0",), ("in_n_far1",), ("out_n", 0), ("out_n", 1), ("out_n", 2), ("out_n", 3),
    ("out_n", 4), ("out_n", 5),
]


def normalised(values, scale_row, shift_row):
    center = jnp.mean(values, axis=-1, keepdims=True)
    moved = values - center
    spread = jnp.mean(moved * moved, axis=-1, keepdims=True)
    return moved * lax.rsqrt(spread + EPS_NORM) * (1.0 + scale_row) + shift_row


def gelu_tanh(v):
    return 0.5 * v * (1.0 + jnp.tanh(0.7978845608028654 * (v + 0.044715 * (v * v * v))))


def fused_kernel(
    unit_plan,
    image,
    text_hbm,
    mod_hbm,
    wa_hbm,
    wp_hbm,
    wi_hbm,
    wo_hbm,
    final_hbm,
    guidance_hbm,
    text_len_hbm,
    step_index_hbm,
    step_count_hbm,
    out_ref,
    text,
    mod,
    final_w,
    guidance,
    text_len,
    step_index,
    step_count,
    wa_own,
    wi_own,
    wo_own,
    wp,
    wa_far,
    wi_far,
    wo_far,
    hid,
    nrm,
    txt,
    txt_out,
    txt_in,
    q_s,
    k_s,
    v_s,
    kt_s,
    vt_s,
    att,
    hs,
    inner,
    rs,
    rr,
    mo,
    vel_own,
    vel_oth,
    pay_out,
    pay_in,
    sum_in,
    w_r,
    w_s,
    i_r,
    i_s,
    t_r,
    t_s,
    o_r,
    o_s,
    r_r,
    r_s,
    f_r,
    f_s,
    l_s,
):
    c = lax.axis_index("cfg")
    r = lax.axis_index("req")
    s = lax.axis_index("seq")
    half = s // 2
    is_mid = (s == 1) | (s == 2)
    om = 3 - s
    pe = half * 3
    oe = 3 - pe
    near_mid = 1 + half
    far_mid = 2 - half
    rows_local = image.shape[0]
    rows_all = hid.shape[0]
    near_rows = 2 * rows_local
    width = image.shape[1]
    piece = width // 8
    text_local = text.shape[0]
    text_all = txt.shape[0]

    rx = lax.rem(r + 2, 4)
    rc = r + 1 - 2 * lax.rem(r, 2)
    rcx = lax.rem(rc + 2, 4)
    cy = 1 - c
    dev_x = (c, rx, s)
    dev_y = (cy, r, s)
    dev_c = (c, rc, s)
    dev_om = (c, r, om)
    dev_pe = (c, r, pe)
    dev_oe = (c, r, oe)
    dev_near = (c, r, near_mid)
    dev_far = (c, r, far_mid)

    def rcopy(src, dst, ssem, rsem, dev):
        return pltpu.make_async_remote_copy(
            src_ref=src, dst_ref=dst, send_sem=ssem, recv_sem=rsem, device_id=dev, device_id_type=MESH_ID
        )

    def rows_of(first, count, align):
        return pl.ds(pl.multiple_of(first, align), count)

    own_rows = rows_of(s * rows_local, rows_local, 128)
    weights = {"a": (wa_hbm, wa_far), "i": (wi_hbm, wi_far), "o": (wo_hbm, wo_far)}
    units = len(unit_plan)

    def piece_rows(cc, rr_, first=0, count=None):
        start = (cc * 4 + rr_) * piece + first
        return rows_of(start, piece if count is None else count, 32)

    def wcopy(u, k, rows, dev, src=None):
        kind, col, ncol, _ = unit_plan[u]
        far = weights[kind][1]
        at = far.at[rows, pl.ds(col, ncol)]
        return rcopy(at if src is None else src, at, w_s.at[u, k], w_r.at[u, k], dev)

    hp = piece // 2

    def w_first(u, rows, line, core):
        for k, dev in line:
            wcopy(u, k, rows, dev).start()
        wcopy(u, core, rows, dev_c).start()

    def w_step(u, step):
        mode = unit_plan[u][3]
        mine = piece_rows(c, r)
        if step == 1:
            wcopy(u, 0, mine, dev_pe).wait_recv()
            if mode == "q":
                w_first(u, mine, ((1, dev_x), (2, dev_y)), 5)
            elif mode == "x":
                w_first(u, mine, ((1, dev_x),), 5)
                wcopy(u, 9, piece_rows(cy, r), dev_pe).wait_recv()
                w_first(u, piece_rows(cy, r), ((4, dev_x),), 7)
            else:
                w_first(u, mine, ((2, dev_y),), 5)
                wcopy(u, 9, piece_rows(c, rx), dev_pe).wait_recv()
                w_first(u, piece_rows(c, rx), ((3, dev_y),), 6)
        elif step == 2:
            if mode == "q":
                wcopy(u, 1, piece_rows(c, rx), dev_x).wait_recv()
                wcopy(u, 3, piece_rows(c, rx, 0, hp), dev_y).start()
                wcopy(u, 2, piece_rows(cy, r), dev_y).wait_recv()
                wcopy(u, 4, piece_rows(cy, r, hp, hp), dev_x).start()
                wcopy(u, 6, piece_rows(c, rx), dev_c).start()
                wcopy(u, 7, piece_rows(cy, r), dev_c).start()
            elif mode == "x":
                wcopy(u, 1, piece_rows(c, rx), dev_x).wait_recv()
                wcopy(u, 6, piece_rows(c, rx), dev_c).start()
                wcopy(u, 4, piece_rows(cy, rx), dev_x).wait_recv()
                wcopy(u, 8, piece_rows(cy, rx), dev_c).start()
            else:
                wcopy(u, 2, piece_rows(cy, r), dev_y).wait_recv()
                wcopy(u, 7, piece_rows(cy, r), dev_c).start()
                wcopy(u, 3, piece_rows(cy, rx), dev_y).wait_recv()
                wcopy(u, 8, piece_rows(cy, rx), dev_c).start()
        elif step == 3:
            if mode == "q":
                wcopy(u, 3, piece_rows(cy, rx, 0, hp), dev_y).wait_recv()
                wcopy(u, 4, piece_rows(cy, rx, hp, hp), dev_x).wait_recv()
                wcopy(u, 8, piece_rows(cy, rx), dev_c).start()
        elif step == 4:
            wcopy(u, 5, piece_rows(c, rc), dev_c).wait_recv()
            wcopy(u, 6, piece_rows(c, rcx), dev_c).wait_recv()
            wcopy(u, 7, piece_rows(cy, rc), dev_c).wait_recv()
            wcopy(u, 8, piece_rows(cy, rcx), dev_c).wait_recv()

    def w_sent(u):
        mode = unit_plan[u][3]
        mine = piece_rows(c, r)
        if mode != "y":
            wcopy(u, 1, mine, dev_x).wait_send()
        if mode != "x":
            wcopy(u, 2, mine, dev_y).wait_send()
        if mode == "q":
            wcopy(u, 3, piece_rows(c, rx, 0, hp), dev_y).wait_send()
            wcopy(u, 4, piece_rows(cy, r, hp, hp), dev_x).wait_send()
        elif mode == "x":
            wcopy(u, 4, piece_rows(cy, r), dev_x).wait_send()
        else:
            wcopy(u, 3, piece_rows(c, rx), dev_y).wait_send()
        wcopy(u, 5, mine, dev_c).wait_send()
        wcopy(u, 6, piece_rows(c, rx), dev_c).wait_send()
        wcopy(u, 7, piece_rows(cy, r), dev_c).wait_send()
        wcopy(u, 8, piece_rows(cy, rx), dev_c).wait_send()

    chunks = 4
    chunk = rows_local // chunks

    def end_image(k):
        src = image.at[pl.ds(k * chunk, chunk)]
        dst = hid.at[rows_of(s * rows_local + k * chunk, chunk, 32)]
        return rcopy(src, dst, i_s.at[k], i_r.at[k], dev_near)

    def pe_rows(k):
        return hid.at[rows_of(pe * rows_local + k * chunk, chunk, 32)]

    def oe_rows(k):
        return hid.at[rows_of(oe * rows_local + k * chunk, chunk, 32)]

    def forward_image(k):
        rcopy(pe_rows(k), pe_rows(k), i_s.at[k], i_r.at[k], dev_om).wait_recv()
        rcopy(pe_rows(k), pe_rows(k), i_s.at[chunks + k], i_r.at[chunks + k], dev_om).start()

    own_image = rcopy(image, hid.at[own_rows], i_s.at[2 * chunks], i_r.at[2 * chunks], dev_om)
    text_to_mid = rcopy(txt_out, txt_in, t_s.at[0], t_r.at[0], dev_near)

    def text_half(which):
        return txt.at[rows_of(which * 2 * text_local, 2 * text_local, 16)]

    def att_copy(j, pair):
        return rcopy(att.at[pair], att.at[pair], o_s.at[j], o_r.at[j], dev_om)

    out_units = [u for u in range(units) if unit_plan[u][0] == "o"]

    def r_copy(j):
        cols = pl.ds(unit_plan[out_units[j]][1], unit_plan[out_units[j]][2])
        return rcopy(rs.at[:, cols], rr.at[:, cols], r_s.at[j], r_r.at[j], dev_om)

    vel_copy = rcopy(vel_own, vel_oth, f_s.at[0], f_r.at[0], dev_y)
    pay_copy = rcopy(pay_out, pay_in, f_s.at[1], f_r.at[1], dev_pe)
    sums_at = pay_out.at[pl.ds(32, 8)]
    sum_copy_om = rcopy(sums_at, sum_in, f_s.at[2], f_r.at[2], dev_om)
    sum_copy_oe = rcopy(sums_at, sum_in, f_s.at[3], f_r.at[2], dev_oe)

    def load(i, src, dst):
        return pltpu.make_async_copy(src, dst, l_s.at[i])

    loads = [
        load(0, image, hid.at[own_rows]),
        load(1, wa_hbm, wa_own),
        load(2, wp_hbm, wp),
        load(3, wi_hbm, wi_own),
        load(4, wo_hbm, wo_own),
    ]
    early = [load(5, text_hbm, text), load(6, mod_hbm, mod)]
    late = [
        load(7, final_hbm, final_w),
        load(8, guidance_hbm, guidance),
        load(9, text_len_hbm, text_len),
        load(10, step_index_hbm, step_index),
        load(11, step_count_hbm, step_count),
    ]

    barrier = pltpu.get_barrier_semaphore()

    def greet(devs):
        for dev in devs:
            pl.semaphore_signal(barrier, inc=1, device_id=dev, device_id_type=MESH_ID)

    for item in early:
        item.start()

    @pl.when(is_mid)
    def _():
        for item in loads[:2]:
            item.start()
        greet((dev_pe, dev_om, dev_oe, dev_x, dev_y, dev_c))

    @pl.when(jnp.logical_not(is_mid))
    def _():
        greet((dev_near, dev_far))

    for item in late:
        item.start()
    for item in early:
        item.wait()

    text_norm = normalised(text[...].astype(F32), mod[4], mod[3])
    pad = txt_out.shape[0] - text_local
    txt_out[...] = jnp.concatenate([text_norm, jnp.zeros((pad, width), F32)], axis=0).astype(BF16)

    def finish(guided_half, sums):
        entries = 2.0 * guided_half.shape[0] * rows_all
        rms_cond = jnp.sqrt(sums[0:1, :] / entries + EPS_NORM)
        rms_guided = jnp.sqrt(sums[4:5, :] / entries + EPS_NORM)
        velocity = 0.7 * (guided_half * (rms_cond / rms_guided)) + 0.3 * guided_half
        now = step_index[...]
        after = jnp.minimum(now + step_count[...], STEPS)

        def sigma(i):
            remain = 1.0 - i.astype(F32) / STEPS
            return 3.0 * remain / (1.0 + 2.0 * remain)

        out_ref[0 : guided_half.shape[0], :] = velocity
        out_ref[guided_half.shape[0] :, :] = jnp.zeros(guided_half.shape, F32) + (sigma(after) - sigma(now))

    for item in late:
        item.wait()

    @pl.when(jnp.logical_not(is_mid))
    def _():
        pl.semaphore_wait(barrier, 2)

        def unit_send(u):
            kind, col, ncol, mode = unit_plan[u]
            sends = [(0, piece_rows(c, r))]
            if mode == "x":
                sends.append((9, piece_rows(cy, r)))
            elif mode == "y":
                sends.append((9, piece_rows(c, rx)))
            src = weights[kind][0]
            return [wcopy(u, k, rows, dev_near, src.at[rows, pl.ds(col, ncol)]) for k, rows in sends]

        order = []
        sent = set()
        for item in FIRST_SENDS:
            if item[0] == "w":
                order.append(unit_send(item[1])[item[2]])
                sent.add(item[1:])
            else:
                order.append(end_image(item[1]) if item[0] == "i" else text_to_mid)
        for u in range(units):
            order += [item for k, item in enumerate(unit_send(u)) if (u, k) not in sent]
        for at, item in enumerate(order):
            item.start()
            if at >= 1:
                order[at - 1].wait_send()
        order[-1].wait_send()
        pay_copy.wait_recv()
        sum_copy_oe.wait_recv()
        finish(pay_in[0:32, :], pay_in[32:40, :] + sum_in[...])

    @pl.when(is_mid)
    def _():
        pl.semaphore_wait(barrier, 6)
        own_image.start()
        for item in loads[2:]:
            item.start()

        def norm_rows(first, count, read, scale, shift):
            @pl.loop(0, count // 32)
            def _(b):
                at = first + b * 32
                out = normalised(read(at), mod[scale], mod[shift])
                nrm[rows_of(at, 32, 32), :] = out.astype(BF16)

        def read_hid(at):
            return hid[rows_of(at, 32, 32), :].astype(F32)

        def read_hs(at):
            return hs[rows_of(at, 32, 32), :]

        def qkv(rows, w, base):
            @pl.loop(0, 2)
            def _(p):
                cols = rows_of(p * 10 * HEAD, 10 * HEAD, 128)
                y = jnp.dot(nrm[rows, :], w[:, cols], preferred_element_type=F32)
                for j in range(2):
                    o = j * 5 * HEAD
                    head = base + 2 * p + j
                    q_s[head, rows, :] = y[:, o : o + HEAD].astype(BF16)
                    k_s[head, rows, :] = y[:, o + HEAD : o + 2 * HEAD].astype(BF16)
                    v_s[head, rows, :] = y[:, o + 2 * HEAD : o + 3 * HEAD].astype(BF16)

        def text_kv(w, base):
            @pl.loop(0, 2)
            def _(p):
                cols = rows_of(p * 10 * HEAD, 10 * HEAD, 128)
                y = jnp.dot(txt[...], w[:, cols], preferred_element_type=F32)
                for j in range(2):
                    o = j * 5 * HEAD + 3 * HEAD
                    head = base + 2 * p + j
                    kt_s[head] = y[:, o : o + HEAD].astype(BF16)
                    vt_s[head] = y[:, o + HEAD : o + 2 * HEAD].astype(BF16)

        slots = lax.broadcasted_iota(jnp.int32, (1, text_all), 1)
        valid = slots < text_len[...]
        nt = (((1,), (1,)), ((), ()))

        def attend(slot, pair):
            @pl.loop(0, rows_all // TILE)
            def _(b):
                rows = rows_of(b * TILE, TILE, TILE)
                parts = []
                for j in range(2):
                    head = slot + j
                    query = q_s[head, rows, :]
                    s_i = lax.dot_general(query, k_s[head], nt, preferred_element_type=F32)
                    s_t = lax.dot_general(query, kt_s[head], nt, preferred_element_type=F32)
                    s_t = jnp.where(valid, s_t, -1e30)
                    top = jnp.maximum(
                        jnp.max(s_i, axis=1, keepdims=True), jnp.max(s_t, axis=1, keepdims=True)
                    )
                    p_i = jnp.exp2((s_i - top) * EXP_SCALE)
                    p_t = jnp.exp2((s_t - top) * EXP_SCALE)
                    total = jnp.sum(p_i, axis=1, keepdims=True) + jnp.sum(p_t, axis=1, keepdims=True)
                    mixed = jnp.dot(p_i.astype(BF16), v_s[head], preferred_element_type=F32)
                    mixed += jnp.dot(p_t.astype(BF16), vt_s[head], preferred_element_type=F32)
                    parts.append(mixed / total)
                att[pair, rows, :] = jnp.concatenate(parts, axis=1).astype(BF16)

        def block(plane):
            return rows_of(plane * rows_local, rows_local, 128)

        def project(first):
            rows = rows_of(first, near_rows, TILE)
            @pl.loop(0, width // TILE)
            def _(t):
                cols = rows_of(t * TILE, TILE, TILE)
                lhs = jnp.concatenate([att[p, rows, :] for p in range(att.shape[0])], axis=1)
                y = jnp.dot(lhs, wp[:, cols], preferred_element_type=F32)
                hs[rows, cols] = hid[rows, cols].astype(F32) + mod[2, :, cols] * y

        def mlp_in(first, w, base, part):
            rows = rows_of(first, near_rows, TILE)
            tiles = width // TILE // 2
            @pl.loop(part * tiles, (part + 1) * tiles)
            def _(t):
                cols = rows_of(t * TILE, TILE, TILE)
                y = jnp.dot(nrm[rows, :], w[:, cols], preferred_element_type=F32)
                inner[rows, rows_of(base + t * TILE, TILE, TILE)] = gelu_tanh(y).astype(BF16)

        def mlp_out(first, col, ncol, far):
            rows = rows_of(first, near_rows, TILE)
            @pl.loop(0, ncol // TILE)
            def _(t):
                cols = rows_of(col + t * TILE, TILE, TILE)
                y = jnp.dot(inner[rows, 0:width], wo_own[:, cols], preferred_element_type=F32)
                y += jnp.dot(inner[rows, width : 2 * width], wo_far[:, cols], preferred_element_type=F32)
                if far:
                    rs[:, cols] = y.astype(BF16)
                else:
                    mo[:, cols] = y

        near_first = half * near_rows
        far_first = (1 - half) * near_rows

        text_send = rcopy(text_half(half), text_half(half), t_s.at[1], t_r.at[1], dev_om)
        held = set()

        def need_load(k):
            if ("load", k) not in held:
                held.add(("load", k))
                loads[k].wait()

        def need_units(kind, limit=None):
            for u in range(units):
                col, ncol = unit_plan[u][1:3]
                if unit_plan[u][0] == kind and ("w", u) not in held and (limit is None or limit(col, ncol)):
                    held.add(("w", u))
                    w_step(u, 4)

        def part_of(part):
            return lambda col, ncol: part == 1 or col < width // 2

        def stage(name, arg=None):
            if name == "f":
                forward_image(arg)
            elif name.startswith("norm_"):
                which = name[5:]
                if which == "own":
                    need_load(0)
                if which == "om":
                    own_image.wait_recv()
                if which == "oe":
                    for k in range(chunks):
                        rcopy(oe_rows(k), oe_rows(k), i_s.at[chunks + k], i_r.at[chunks + k], dev_om).wait_recv()
                plane = {"own": s, "om": om, "pe": pe, "oe": oe}[which]
                norm_rows(plane * rows_local, rows_local, read_hid, 1, 0)
            elif name.startswith("qkv_"):
                need_load(1)
                qkv(block({"own": s, "om": om, "pe": pe, "oe": oe}[name[4:]]), wa_own, 0)
            elif name == "tcomb":
                text_to_mid.wait_recv()
                theirs = txt_in[...].astype(F32)[0:text_local]
                mine = txt_out[...].astype(F32)[0:text_local]
                first = jnp.where(half == 0, theirs, mine)
                second = jnp.where(half == 0, mine, theirs)
                txt[rows_of(half * 2 * text_local, 2 * text_local, 16), :] = jnp.concatenate(
                    [first, second], axis=0
                ).astype(BF16)
                text_send.start()
            elif name == "tkv_own":
                need_load(1)
                rcopy(text_half(1 - half), text_half(1 - half), t_s.at[1], t_r.at[1], dev_om).wait_recv()
                text_kv(wa_own, 0)
            elif name == "tkv_far":
                need_units("a")
                text_kv(wa_far, 4)
            elif name.startswith("qkvf"):
                need_units("a")
                qkv(pl.ds(int(name[4]) * near_rows, near_rows), wa_far, 4)
            elif name.startswith("att"):
                k = int(name[3])
                pair = (2 * s, 2 * s + 1, 2 * pe, 2 * pe + 1)[k]
                attend(2 * k, pair)
                att_copy(k, pair).start()
            elif name == "proj_f":
                need_load(2)
                att_copy(0, 2 * om).wait_recv()
                att_copy(1, 2 * om + 1).wait_recv()
                att_copy(2, 2 * oe).wait_recv()
                att_copy(3, 2 * oe + 1).wait_recv()
                project(far_first)
            elif name == "proj_n":
                project(near_first)
            elif name.startswith("norm2_"):
                norm_rows(far_first if name[6] == "f" else near_first, near_rows, read_hs, 8, 7)
            elif name.startswith("in_"):
                first = far_first if name[3] == "f" else near_first
                part = int(name[-1])
                if "own" in name:
                    need_load(3)
                    mlp_in(first, wi_own, 0, part)
                else:
                    need_units("i", part_of(part))
                    mlp_in(first, wi_far, width, part)
            elif name.startswith("out_"):
                need_load(4)
                u = out_units[arg]
                need_units("o", lambda col, ncol: col == unit_plan[u][1])
                mlp_out(far_first if name[4] == "f" else near_first, unit_plan[u][1], unit_plan[u][2], name[4] == "f")
                if name[4] == "f":
                    r_copy(arg).start()

        for item in STREAM:
            if item[0] == "w":
                w_step(item[1], item[2])
            else:
                stage(*item)
        for j in range(len(out_units)):
            r_copy(j).wait_recv()

        @pl.loop(0, near_rows // 32)
        def _(b):
            at = near_first + b * 32
            here = rows_of(b * 32, 32, 32)
            rows = rows_of(at, 32, 32)
            value = hs[rows, :] + mod[9] * (mo[here, :] + rr[here, :].astype(F32))
            nrm[rows, :] = normalised(value, mod[6], mod[5]).astype(BF16)

        own_vel = lax.dot_general(
            final_w[...], nrm[rows_of(near_first, near_rows, TILE), :], nt, preferred_element_type=F32
        )
        vel_own[...] = own_vel
        vel_copy.start()
        vel_copy.wait_recv()
        oth_vel = vel_oth[...]
        cond = jnp.where(c == 0, own_vel, oth_vel)
        uncond = jnp.where(c == 0, oth_vel, own_vel)
        guided = uncond + guidance[0] * (cond - uncond)

        def total_of(v):
            return jnp.sum(jnp.sum(v * v, axis=1, keepdims=True), axis=0, keepdims=True)

        line = lax.broadcasted_iota(jnp.int32, (8, 128), 0)
        sums = jnp.where(line < 4, total_of(cond), total_of(guided))
        patch_half = pay_out.shape[0] - 8
        mine_half = jnp.where(c == 0, guided[0:patch_half, :], guided[patch_half:, :])
        low, high = mine_half[:, 0:rows_local], mine_half[:, rows_local:]
        pay_out[0:patch_half, :] = jnp.where(half == 0, low, high)
        pay_out[patch_half:, :] = sums
        sum_copy_om.start()
        sum_copy_oe.start()
        pay_copy.start()
        sum_copy_om.wait_recv()
        finish(jnp.where(half == 0, high, low), sums + sum_in[...])

        own_image.wait_send()
        for k in range(chunks):
            rcopy(pe_rows(k), pe_rows(k), i_s.at[chunks + k], i_r.at[chunks + k], dev_om).wait_send()
        text_send.wait_send()
        for j in range(4):
            att_copy(j, 2 * s).wait_send()
        for j in range(len(out_units)):
            r_copy(j).wait_send()
        for u in range(units):
            w_sent(u)
        vel_copy.wait_send()
        pay_copy.wait_send()
        sum_copy_om.wait_send()
        sum_copy_oe.wait_send()


def fused_local(
    image_hidden,
    text_hidden,
    modulation,
    attn_weight,
    proj_weight,
    mlp_in_weight,
    mlp_out_weight,
    final_weight,
    latents,
    guidance,
    text_lengths,
    step_index,
    step_count,
):
    rows, width = image_hidden.shape[2:]
    text_rows = text_hidden.shape[2]
    padded = -(-text_rows // 16) * 16
    cols_a = attn_weight.shape[1]
    units_here = mlp_in_weight.shape[1]
    plan = UNITS
    channels = latents.shape[1]
    heads = 2 * (HEADS // 4)
    near = 2 * rows
    count = len(plan)
    outs = sum(1 for item in plan if item[0] == "o")
    vmem = pl.BlockSpec(memory_space=pltpu.VMEM)
    anywhere = pl.BlockSpec(memory_space=pl.ANY)
    dma = pltpu.SemaphoreType.DMA
    result = pl.pallas_call(
        functools.partial(fused_kernel, plan),
        out_shape=jax.ShapeDtypeStruct((2 * channels, rows), F32),
        in_specs=[anywhere] * 12,
        out_specs=vmem,
        scratch_shapes=[
            pltpu.VMEM((text_rows, width), BF16),
            pltpu.VMEM((modulation.shape[2], 1, width), F32),
            pltpu.VMEM(final_weight.shape, BF16),
            pltpu.VMEM((1, 1), F32),
            pltpu.VMEM((1, 1), jnp.int32),
            pltpu.VMEM((1, 1), jnp.int32),
            pltpu.VMEM((1, 1), jnp.int32),
            pltpu.VMEM((width, cols_a), BF16),
            pltpu.VMEM((width, units_here), BF16),
            pltpu.VMEM((units_here, width), BF16),
            pltpu.VMEM(proj_weight.shape, BF16),
            pltpu.VMEM((width, cols_a), BF16),
            pltpu.VMEM((width, units_here), BF16),
            pltpu.VMEM((units_here, width), BF16),
            pltpu.VMEM((4 * rows, width), BF16),
            pltpu.VMEM((4 * rows, width), BF16),
            pltpu.VMEM((4 * text_rows, width), BF16),
            pltpu.VMEM((padded, width), BF16),
            pltpu.VMEM((padded, width), BF16),
            pltpu.VMEM((heads, 4 * rows, HEAD), BF16),
            pltpu.VMEM((heads, 4 * rows, HEAD), BF16),
            pltpu.VMEM((heads, 4 * rows, HEAD), BF16),
            pltpu.VMEM((heads, 4 * text_rows, HEAD), BF16),
            pltpu.VMEM((heads, 4 * text_rows, HEAD), BF16),
            pltpu.VMEM((HEADS // 2, 4 * rows, 2 * HEAD), BF16),
            pltpu.VMEM((4 * rows, width), F32),
            pltpu.VMEM((4 * rows, 2 * units_here), BF16),
            pltpu.VMEM((near, width), BF16),
            pltpu.VMEM((near, width), BF16),
            pltpu.VMEM((near, width), F32),
            pltpu.VMEM((2 * channels, near), F32),
            pltpu.VMEM((2 * channels, near), F32),
            pltpu.VMEM((channels + 8, rows), F32),
            pltpu.VMEM((channels + 8, rows), F32),
            pltpu.VMEM((8, 128), F32),
            dma((count, 10)),
            dma((count, 10)),
            dma((9,)),
            dma((9,)),
            dma((2,)),
            dma((2,)),
            dma((4,)),
            dma((4,)),
            dma((outs,)),
            dma((outs,)),
            dma((3,)),
            dma((4,)),
            dma((12,)),
        ],
        compiler_params=pltpu.CompilerParams(
            collective_id=0, has_side_effects=True, vmem_limit_bytes=60 * 2**20
        ),
        cost_estimate=pl.CostEstimate(flops=15 * 10**9, bytes_accessed=17 * 10**6, transcendentals=5 * 10**6),
    )(
        image_hidden[0, 0],
        text_hidden[0, 0],
        jnp.swapaxes(modulation[0], 0, 1),
        attn_weight,
        proj_weight,
        mlp_in_weight,
        mlp_out_weight,
        final_weight,
        guidance[None],
        text_lengths,
        step_index[None],
        step_count[None],
    )
    velocity, step_size = result[:channels], result[channels:]
    return velocity[None], latents + (step_size * velocity)[None]


def solution(mesh):
    in_specs = (
        P("cfg", "req", "seq", None),
        P("cfg", "req", "seq", None),
        P("cfg", "req", None, None),
        P(None, "seq"),
        P(),
        P(None, "seq"),
        P("seq", None),
        P(),
        P("req", "cfg", "seq"),
        P("req"),
        P("cfg", "req"),
        P("req"),
        P("req"),
    )
    out_specs = (P("req", "cfg", "seq"), P("req", "cfg", "seq"))
    shape = dict(mesh.shape)
    line = shape == {"cfg": 2, "req": 4, "seq": 4}
    body = fused_local if line else local
    return jax.shard_map(body, mesh=mesh, in_specs=in_specs, out_specs=out_specs, check_vma=False)
```

```python
import functools
import math

import jax
import jax.numpy as jnp
from jax import lax
from jax.experimental import pallas as pl
from jax.experimental.pallas import tpu as pltpu
from jax.sharding import PartitionSpec as P

HEADS = 16
HEAD = 64
STEPS = 28


EPS_NORM = 1e-06


def partner(value, axis, distance):
    mask = 2**distance
    pairs = [(source, source ^ mask) for source in range(lax.axis_size(axis))]
    return lax.ppermute(value, axis, pairs)


def shifted(value, axis, shift):
    size = lax.axis_size(axis)
    return lax.ppermute(value, axis, [(source, (source - shift) % size) for source in range(size)])


def modulate(rows_in, scale_row, shift_row):
    values = rows_in.astype(jnp.float32)
    center = jnp.mean(values, axis=-1, keepdims=True)
    spread = jnp.mean(jnp.square(values - center), axis=-1, keepdims=True)
    return (
        (values - center) * lax.rsqrt(spread + EPS_NORM) * (1.0 + scale_row) + shift_row
    ).astype(jnp.bfloat16)


def sigma_of(index):
    remain = 1.0 - index.astype(jnp.float32) / STEPS
    return 3.0 * remain / (1.0 + 2.0 * remain)


def split_columns(weight_piece):
    width_in = weight_piece.shape[0]
    head_count = weight_piece.shape[1] // (5 * HEAD)
    shaped = weight_piece.reshape(width_in, head_count, 5, HEAD)
    image_cols = shaped[:, :, 0:3, :].reshape(width_in, head_count * 3 * HEAD)
    text_cols = shaped[:, :, 3:5, :].reshape(width_in, head_count * 2 * HEAD)
    return (image_cols, text_cols)


def local(
    image_hidden,
    text_hidden,
    modulation,
    attn_weight,
    proj_weight,
    mlp_in_weight,
    mlp_out_weight,
    final_weight,
    latents,
    guidance,
    text_lengths,
    step_index,
    step_count,
):
    seq_size = lax.axis_size("seq")
    local_heads = HEADS // seq_size
    image_rows = image_hidden[0, 0]
    text_rows = text_hidden[0, 0]
    mod_rows = modulation[0, 0]
    local_rows = image_rows.shape[0]
    image_total = local_rows * seq_size
    text_total = text_rows.shape[0] * seq_size
    image_norm = modulate(image_rows, mod_rows[1], mod_rows[0])
    text_norm = modulate(text_rows, mod_rows[4], mod_rows[3])
    seq_index = lax.axis_index("seq")
    own_norm = jnp.concatenate([image_norm, text_norm], axis=0)
    gathered = jnp.stack([own_norm] + [shifted(own_norm, "seq", k) for k in range(1, seq_size)])
    image_all = gathered[:, :local_rows].reshape(image_total, -1)
    text_all = gathered[:, local_rows:].reshape(text_total, -1)
    image_cols, text_cols = split_columns(attn_weight)
    image_qkv = jnp.dot(image_all, image_cols, preferred_element_type=jnp.float32).astype(
        jnp.bfloat16
    )
    text_kv = jnp.dot(text_all, text_cols, preferred_element_type=jnp.float32).astype(
        jnp.bfloat16
    )
    image_qkv = image_qkv.reshape(image_total, local_heads, 3, HEAD)
    text_kv = text_kv.reshape(text_total, local_heads, 2, HEAD)
    keys_all = jnp.concatenate([image_qkv[:, :, 1], text_kv[:, :, 0]], axis=0)
    values_all = jnp.concatenate([image_qkv[:, :, 2], text_kv[:, :, 1]], axis=0)
    text_local = text_rows.shape[0]
    sources = (seq_index + jnp.arange(seq_size, dtype=jnp.int32)) % seq_size
    slots = (sources[:, None] * text_local + jnp.arange(text_local, dtype=jnp.int32)).reshape(-1)
    valid = jnp.concatenate([jnp.ones((image_total,), dtype=bool), slots < text_lengths[0, 0]])
    block_rows = local_rows
    while block_rows < 512 and image_total % (block_rows * 2) == 0:
        block_rows = block_rows * 2
    block_total = image_total // block_rows
    query_blocks = image_qkv[:, :, 0].reshape(block_total, block_rows, local_heads, HEAD)

    def attend(query_block):
        scores = jnp.einsum(
            "qhe,khe->hqk", query_block, keys_all, preferred_element_type=jnp.float32
        ) * HEAD ** (-0.5)
        scores = jnp.where(valid[None, None, :], scores, -1e30)
        row_max = jnp.max(scores, axis=2, keepdims=True)
        weights = jnp.exp(scores - row_max)
        total = jnp.sum(weights, axis=2, keepdims=True)
        probs = weights.astype(jnp.bfloat16)
        mixed = (
            jnp.einsum("hqk,khe->hqe", probs, values_all, preferred_element_type=jnp.float32)
            / total
        )
        return jnp.transpose(mixed.astype(jnp.bfloat16), (1, 0, 2))

    attended = lax.map(attend, query_blocks).reshape(image_total, local_heads * HEAD)
    attended = attended.reshape(seq_size, local_rows, local_heads * HEAD)
    head_width = local_heads * HEAD
    projected = jnp.zeros((local_rows, proj_weight.shape[1]), jnp.float32)
    for k in range(seq_size):
        piece = attended[k] if k == 0 else shifted(attended[k], "seq", -k)
        rows = lax.dynamic_slice_in_dim(
            proj_weight, ((seq_index - k) % seq_size) * head_width, head_width, 0
        )
        projected = projected + jnp.dot(piece, rows, preferred_element_type=jnp.float32)
    hidden = image_rows.astype(jnp.float32) + mod_rows[2] * projected
    mlp_norm = modulate(hidden, mod_rows[8], mod_rows[7])
    mlp_out = jnp.zeros((local_rows, mlp_out_weight.shape[1]), jnp.float32)
    for k in range(seq_size):
        piece = mlp_norm if k == 0 else shifted(mlp_norm, "seq", k)
        inner = jax.nn.gelu(
            jnp.dot(piece, mlp_in_weight, preferred_element_type=jnp.float32), approximate=True
        ).astype(jnp.bfloat16)
        part = jnp.dot(inner, mlp_out_weight, preferred_element_type=jnp.float32).astype(
            jnp.bfloat16
        )
        part = part if k == 0 else shifted(part, "seq", -k)
        mlp_out = mlp_out + part.astype(jnp.float32)
    block_out = hidden + mod_rows[9] * mlp_out
    final_norm = modulate(block_out, mod_rows[6], mod_rows[5])
    own_vel = lax.dot_general(
        final_weight, final_norm, (((1,), (1,)), ((), ())), preferred_element_type=jnp.float32
    )
    partner_vel = partner(own_vel.astype(jnp.bfloat16), "cfg", 0).astype(own_vel.dtype)
    leading = lax.axis_index("cfg") == 0
    cond_vel = jnp.where(leading, own_vel, partner_vel)
    uncond_vel = jnp.where(leading, partner_vel, own_vel)
    guided = uncond_vel + guidance[...] * (cond_vel - uncond_vel)
    squares = jnp.stack([jnp.sum(cond_vel * cond_vel), jnp.sum(guided * guided)])
    squares = sum(
        [squares] + [shifted(squares, "seq", k) for k in range(1, seq_size)], jnp.zeros(2)
    )
    cond_sq, guided_sq = squares[0], squares[1]
    entries = own_vel.shape[0] * image_total
    rms_cond = jnp.sqrt(cond_sq / entries + EPS_NORM)
    rms_guided = jnp.sqrt(guided_sq / entries + EPS_NORM)
    result_vel = 0.7 * (guided * (rms_cond / rms_guided)) + 0.3 * guided
    channel_half = latents.shape[1]
    channel_start = lax.axis_index("cfg") * channel_half
    own_channels = lax.dynamic_slice_in_dim(result_vel, channel_start, channel_half, 0)
    next_index = jnp.minimum(step_index[0] + step_count[0], STEPS)
    step_size = sigma_of(next_index) - sigma_of(step_index[0])
    moved = latents[0] + step_size * own_channels
    return (own_channels[None], moved[None])


BF16 = jnp.bfloat16
F32 = jnp.float32
MESH_ID = pl.DeviceIdType.MESH
EXP_SCALE = math.log2(math.e) * HEAD ** (-0.5)
TILE = 256
UNITS = [
    ("a", 0, 256, "q"), ("a", 256, 256, "q"), ("a", 512, 256, "q"), ("a", 768, 256, "q"),
    ("a", 1024, 256, "q"), ("i", 0, 256, "q"), ("i", 256, 256, "q"), ("i", 512, 256, "q"),
    ("i", 768, 256, "q"), ("i", 1024, 256, "q"), ("i", 1280, 256, "x"), ("o", 0, 256, "y"),
    ("o", 256, 256, "q"), ("o", 512, 256, "q"), ("o", 768, 256, "x"), ("o", 1024, 256, "y"),
    ("o", 1280, 256, "x"),
]
FIRST_SENDS = [
    ("w", 0, 0), ("w", 1, 0), ("w", 2, 0), ("i", 0), ("i", 1), ("w", 3, 0),
    ("t",), ("w", 4, 0), ("i", 2), ("i", 3),
]
STREAM = [
    ("norm_own",), ("w", 0, 1), ("qkv_own",), ("w", 1, 1), ("w", 0, 2), ("w", 2, 1),
    ("w", 1, 2), ("f", 0), ("norm_om",), ("w", 0, 3), ("qkv_om",), ("f", 1),
    ("w", 2, 2), ("w", 1, 3), ("w", 3, 1), ("w", 2, 3), ("tcomb",), ("w", 3, 2),
    ("w", 4, 1), ("w", 3, 3), ("f", 2), ("w", 4, 2), ("f", 3), ("norm_pe",),
    ("qkv_pe",), ("w", 4, 3), ("tkv_own",), ("w", 5, 1), ("tkv_far",), ("w", 6, 1),
    ("norm_oe",), ("qkv_oe",), ("w", 5, 2), ("w", 7, 1), ("att0",), ("w", 6, 2),
    ("att1",), ("w", 8, 1), ("w", 5, 3), ("qkvf0",), ("w", 9, 1), ("w", 7, 2),
    ("qkvf1",), ("w", 6, 3), ("att2",), ("att3",), ("w", 8, 2), ("w", 10, 1),
    ("w", 9, 2), ("w", 7, 3), ("w", 8, 3), ("w", 11, 1), ("w", 12, 1), ("proj_f",),
    ("w", 10, 2), ("norm2_f",), ("w", 13, 1), ("w", 9, 3), ("w", 11, 2), ("in_f_own0",),
    ("in_f_own1",), ("w", 12, 2), ("in_f_far0",), ("w", 14, 1), ("in_f_far1",), ("w", 13, 2),
    ("out_f", 0), ("w", 12, 3), ("proj_n",), ("out_f", 1), ("w", 15, 1), ("norm2_n",),
    ("w", 14, 2), ("in_n_own0",), ("w", 13, 3), ("in_n_own1",), ("out_f", 3), ("w", 16, 1),
    ("out_f", 2), ("in_n_far0",), ("w", 15, 2), ("in_n_far1",), ("out_n", 0), ("out_f", 4),
    ("out_n", 1), ("w", 16, 2), ("out_f", 5), ("out_n", 2),
]


def normalised(values, scale_row, shift_row):
    center = jnp.mean(values, axis=-1, keepdims=True)
    moved = values - center
    spread = jnp.mean(moved * moved, axis=-1, keepdims=True)
    return moved * lax.rsqrt(spread + EPS_NORM) * (1.0 + scale_row) + shift_row


def gelu_tanh(v):
    part = 0.5 * v
    return part + part * jnp.tanh(v * (0.7978845608028654 + 0.7978845608028654 * 0.044715 * (v * v)))


def fused_kernel(
    unit_plan,
    image,
    text_hbm,
    mod_hbm,
    wa_hbm,
    wp_hbm,
    wi_hbm,
    wo_hbm,
    final_hbm,
    guidance_hbm,
    text_len_hbm,
    step_index_hbm,
    step_count_hbm,
    out_ref,
    text,
    mod,
    final_w,
    guidance,
    text_len,
    step_index,
    step_count,
    wa_own,
    wi_own,
    wo_own,
    wp,
    wa_far,
    wi_far,
    wo_far,
    hid,
    nrm,
    txt,
    txt_out,
    txt_in,
    q_s,
    k_s,
    v_s,
    kt_s,
    vt_s,
    att,
    hs,
    inner,
    rs,
    rr,
    mo,
    vel_own,
    vel_oth,
    pay_out,
    pay_in,
    sum_in,
    sum_out,
    sum_near,
    w_r,
    w_s,
    i_r,
    i_s,
    t_r,
    t_s,
    o_r,
    o_s,
    r_r,
    r_s,
    f_r,
    f_s,
    l_s,
):
    c = lax.axis_index("cfg")
    r = lax.axis_index("req")
    s = lax.axis_index("seq")
    half = s // 2
    is_mid = (s == 1) | (s == 2)
    om = 3 - s
    pe = half * 3
    oe = 3 - pe
    near_mid = 1 + half
    far_mid = 2 - half
    rows_local = image.shape[0]
    rows_all = hid.shape[0]
    near_rows = 2 * rows_local
    width = image.shape[1]
    piece = width // 8
    text_local = text.shape[0]
    text_all = txt.shape[0]

    rx = lax.rem(r + 2, 4)
    rc = r + 1 - 2 * lax.rem(r, 2)
    rcx = lax.rem(rc + 2, 4)
    cy = 1 - c
    dev_x = (c, rx, s)
    dev_y = (cy, r, s)
    dev_c = (c, rc, s)
    dev_om = (c, r, om)
    dev_pe = (c, r, pe)
    dev_oe = (c, r, oe)
    dev_near = (c, r, near_mid)
    dev_far = (c, r, far_mid)

    def rcopy(src, dst, ssem, rsem, dev):
        return pltpu.make_async_remote_copy(
            src_ref=src, dst_ref=dst, send_sem=ssem, recv_sem=rsem, device_id=dev, device_id_type=MESH_ID
        )

    def rows_of(first, count, align):
        return pl.ds(pl.multiple_of(first, align), count)

    own_rows = rows_of(s * rows_local, rows_local, 128)
    weights = {"a": (wa_hbm, wa_far), "i": (wi_hbm, wi_far), "o": (wo_hbm, wo_far)}
    units = len(unit_plan)

    def piece_rows(cc, rr_, first=0, count=None):
        start = (cc * 4 + rr_) * piece + first
        return rows_of(start, piece if count is None else count, 32)

    def wcopy(u, k, rows, dev, src=None):
        kind, col, ncol, _ = unit_plan[u]
        far = weights[kind][1]
        at = far.at[rows, pl.ds(col, ncol)]
        return rcopy(at if src is None else src, at, w_s.at[u, k], w_r.at[u, k], dev)

    hp = piece // 2

    def w_first(u, rows, line, core):
        for k, dev in line:
            wcopy(u, k, rows, dev).start()
        wcopy(u, core, rows, dev_c).start()

    def w_step(u, step):
        mode = unit_plan[u][3]
        mine = piece_rows(c, r)
        if step == 1:
            wcopy(u, 0, mine, dev_pe).wait_recv()
            if mode == "q":
                w_first(u, mine, ((1, dev_x), (2, dev_y)), 5)
            elif mode == "x":
                w_first(u, mine, ((1, dev_x),), 5)
                wcopy(u, 9, piece_rows(cy, r), dev_pe).wait_recv()
                w_first(u, piece_rows(cy, r), ((4, dev_x),), 7)
            else:
                w_first(u, mine, ((2, dev_y),), 5)
                wcopy(u, 9, piece_rows(c, rx), dev_pe).wait_recv()
                w_first(u, piece_rows(c, rx), ((3, dev_y),), 6)
        elif step == 2:
            if mode == "q":
                wcopy(u, 1, piece_rows(c, rx), dev_x).wait_recv()
                wcopy(u, 3, piece_rows(c, rx, 0, hp), dev_y).start()
                wcopy(u, 2, piece_rows(cy, r), dev_y).wait_recv()
                wcopy(u, 4, piece_rows(cy, r, hp, hp), dev_x).start()
                wcopy(u, 6, piece_rows(c, rx), dev_c).start()
                wcopy(u, 7, piece_rows(cy, r), dev_c).start()
            elif mode == "x":
                wcopy(u, 1, piece_rows(c, rx), dev_x).wait_recv()
                wcopy(u, 6, piece_rows(c, rx), dev_c).start()
                wcopy(u, 4, piece_rows(cy, rx), dev_x).wait_recv()
                wcopy(u, 8, piece_rows(cy, rx), dev_c).start()
            else:
                wcopy(u, 2, piece_rows(cy, r), dev_y).wait_recv()
                wcopy(u, 7, piece_rows(cy, r), dev_c).start()
                wcopy(u, 3, piece_rows(cy, rx), dev_y).wait_recv()
                wcopy(u, 8, piece_rows(cy, rx), dev_c).start()
        elif step == 3:
            if mode == "q":
                wcopy(u, 3, piece_rows(cy, rx, 0, hp), dev_y).wait_recv()
                wcopy(u, 4, piece_rows(cy, rx, hp, hp), dev_x).wait_recv()
                wcopy(u, 8, piece_rows(cy, rx), dev_c).start()
        elif step == 4:
            wcopy(u, 5, piece_rows(c, rc), dev_c).wait_recv()
            wcopy(u, 6, piece_rows(c, rcx), dev_c).wait_recv()
            wcopy(u, 7, piece_rows(cy, rc), dev_c).wait_recv()
            wcopy(u, 8, piece_rows(cy, rcx), dev_c).wait_recv()

    def w_sent(u):
        mode = unit_plan[u][3]
        mine = piece_rows(c, r)
        if mode != "y":
            wcopy(u, 1, mine, dev_x).wait_send()
        if mode != "x":
            wcopy(u, 2, mine, dev_y).wait_send()
        if mode == "q":
            wcopy(u, 3, piece_rows(c, rx, 0, hp), dev_y).wait_send()
            wcopy(u, 4, piece_rows(cy, r, hp, hp), dev_x).wait_send()
        elif mode == "x":
            wcopy(u, 4, piece_rows(cy, r), dev_x).wait_send()
        else:
            wcopy(u, 3, piece_rows(c, rx), dev_y).wait_send()
        wcopy(u, 5, mine, dev_c).wait_send()
        wcopy(u, 6, piece_rows(c, rx), dev_c).wait_send()
        wcopy(u, 7, piece_rows(cy, r), dev_c).wait_send()
        wcopy(u, 8, piece_rows(cy, rx), dev_c).wait_send()

    chunks = 4
    chunk = rows_local // chunks

    def end_image(k):
        src = image.at[pl.ds(k * chunk, chunk)]
        dst = hid.at[rows_of(s * rows_local + k * chunk, chunk, 32)]
        return rcopy(src, dst, i_s.at[k], i_r.at[k], dev_near)

    def pe_rows(k):
        return hid.at[rows_of(pe * rows_local + k * chunk, chunk, 32)]

    def oe_rows(k):
        return hid.at[rows_of(oe * rows_local + k * chunk, chunk, 32)]

    def forward_image(k):
        rcopy(pe_rows(k), pe_rows(k), i_s.at[k], i_r.at[k], dev_om).wait_recv()
        rcopy(pe_rows(k), pe_rows(k), i_s.at[chunks + k], i_r.at[chunks + k], dev_om).start()

    own_image = rcopy(image, hid.at[own_rows], i_s.at[2 * chunks], i_r.at[2 * chunks], dev_om)
    text_to_mid = rcopy(txt_out, txt_in, t_s.at[0], t_r.at[0], dev_near)

    def text_half(which):
        return txt.at[rows_of(which * 2 * text_local, 2 * text_local, 16)]

    def att_copy(j, pair):
        return rcopy(att.at[pair], att.at[pair], o_s.at[j], o_r.at[j], dev_om)

    out_units = [u for u in range(units) if unit_plan[u][0] == "o"]

    def r_copy(j):
        cols = pl.ds(unit_plan[out_units[j]][1], unit_plan[out_units[j]][2])
        return rcopy(rs.at[:, cols], rr.at[:, cols], r_s.at[j], r_r.at[j], dev_om)

    vel_copy = rcopy(vel_own, vel_oth, f_s.at[0], f_r.at[0], dev_y)
    pay_copy = rcopy(pay_out, pay_in, f_s.at[1], f_r.at[1], dev_pe)
    sum_copy_om = rcopy(sum_out, sum_in, f_s.at[2], f_r.at[2], dev_om)
    sum_copy_oe = rcopy(sum_out, sum_in, f_s.at[3], f_r.at[2], dev_oe)
    sum_copy_pe = rcopy(sum_out, sum_near, f_s.at[4], f_r.at[3], dev_pe)

    def load(i, src, dst):
        return pltpu.make_async_copy(src, dst, l_s.at[i])

    loads = [
        load(0, image, hid.at[own_rows]),
        load(1, wa_hbm, wa_own),
        load(2, wp_hbm, wp),
        load(3, wi_hbm, wi_own),
        load(4, wo_hbm, wo_own),
    ]
    early = [load(5, text_hbm, text), load(6, mod_hbm, mod)]
    late = [
        load(7, final_hbm, final_w),
        load(8, guidance_hbm, guidance),
        load(9, text_len_hbm, text_len),
        load(10, step_index_hbm, step_index),
        load(11, step_count_hbm, step_count),
    ]

    barrier = pltpu.get_barrier_semaphore()

    def greet(devs):
        for dev in devs:
            pl.semaphore_signal(barrier, inc=1, device_id=dev, device_id_type=MESH_ID)

    for item in early:
        item.start()

    @pl.when(is_mid)
    def _():
        for item in loads[:2]:
            item.start()
        greet((dev_pe, dev_om, dev_oe, dev_x, dev_y, dev_c))

    @pl.when(jnp.logical_not(is_mid))
    def _():
        greet((dev_near, dev_far))

    for item in late:
        item.start()
    for item in early:
        item.wait()

    text_norm = normalised(text[...].astype(F32), mod[4], mod[3])
    pad = txt_out.shape[0] - text_local
    txt_out[...] = jnp.concatenate([text_norm, jnp.zeros((pad, width), F32)], axis=0).astype(BF16)

    def finish(guided_half, sums):
        entries = 2.0 * guided_half.shape[0] * rows_all
        rms_cond = jnp.sqrt(sums[0:1, :] / entries + EPS_NORM)
        rms_guided = jnp.sqrt(sums[4:5, :] / entries + EPS_NORM)
        rescaled = 0.7 * (guided_half * (rms_cond / rms_guided))
        now = step_index[...]
        after = jnp.minimum(now + step_count[...], STEPS)

        def sigma(i):
            remain = 1.0 - i.astype(F32) / STEPS
            return 3.0 * remain / (1.0 + 2.0 * remain)

        lines = guided_half.shape[0]
        out_ref[0:lines, :] = rescaled
        out_ref[lines : 2 * lines, :] = 0.3 * guided_half
        out_ref[2 * lines :, :] = jnp.zeros(guided_half.shape, F32) + (sigma(after) - sigma(now))

    for item in late:
        item.wait()

    @pl.when(jnp.logical_not(is_mid))
    def _():
        pl.semaphore_wait(barrier, 2)

        def unit_send(u):
            kind, col, ncol, mode = unit_plan[u]
            sends = [(0, piece_rows(c, r))]
            if mode == "x":
                sends.append((9, piece_rows(cy, r)))
            elif mode == "y":
                sends.append((9, piece_rows(c, rx)))
            src = weights[kind][0]
            return [wcopy(u, k, rows, dev_near, src.at[rows, pl.ds(col, ncol)]) for k, rows in sends]

        order = []
        sent = set()
        for item in FIRST_SENDS:
            if item[0] == "w":
                order.append(unit_send(item[1])[item[2]])
                sent.add(item[1:])
            else:
                order.append(end_image(item[1]) if item[0] == "i" else text_to_mid)
        for u in range(units):
            order += [item for k, item in enumerate(unit_send(u)) if (u, k) not in sent]
        for at, item in enumerate(order):
            item.start()
            if at >= 1:
                order[at - 1].wait_send()
        order[-1].wait_send()
        pay_copy.wait_recv()
        sum_copy_oe.wait_recv()
        sum_copy_pe.wait_recv()
        finish(pay_in[...], sum_near[...] + sum_in[...])

    @pl.when(is_mid)
    def _():
        pl.semaphore_wait(barrier, 6)
        own_image.start()
        for item in loads[2:]:
            item.start()

        def norm_rows(first, count, read, scale, shift):
            @pl.loop(0, count // 64)
            def _(b):
                at = first + b * 64
                out = normalised(read(at), mod[scale], mod[shift])
                nrm[rows_of(at, 64, 32), :] = out.astype(BF16)

        def read_hid(at):
            return hid[rows_of(at, 64, 32), :].astype(F32)

        def read_hs(at):
            return hs[rows_of(at, 64, 32), :]

        def qkv(rows, w, base):
            @pl.loop(0, 2)
            def _(p):
                cols = rows_of(p * 10 * HEAD, 8 * HEAD, 128)
                y = jnp.dot(nrm[rows, :], w[:, cols], preferred_element_type=F32).astype(BF16)
                for j in range(2):
                    o = j * 5 * HEAD
                    head = base + 2 * p + j
                    q_s[head, rows, :] = y[:, o : o + HEAD]
                    k_s[head, rows, :] = y[:, o + HEAD : o + 2 * HEAD]
                    v_s[head, rows, :] = y[:, o + 2 * HEAD : o + 3 * HEAD]

        def text_kv(w, base):
            @pl.loop(0, 2)
            def _(p):
                start = p * 10 * HEAD
                first = jnp.dot(txt[...], w[:, rows_of(start + 2 * HEAD, 4 * HEAD, 128)], preferred_element_type=F32)
                second = jnp.dot(txt[...], w[:, rows_of(start + 8 * HEAD, 2 * HEAD, 128)], preferred_element_type=F32)
                for j, y in enumerate((first[:, HEAD : 3 * HEAD], second)):
                    head = base + 2 * p + j
                    kt_s[head] = y[:, 0:HEAD].astype(BF16)
                    vt_s[head] = y[:, HEAD : 2 * HEAD].astype(BF16)

        slots = lax.broadcasted_iota(jnp.int32, (1, text_all), 1)
        valid = slots < text_len[...]
        nt = (((1,), (1,)), ((), ()))

        def attend(slot, pair):
            @pl.loop(0, rows_all // 512)
            def _(b):
                rows = rows_of(b * 512, 512, 128)
                parts = []
                for j in range(2):
                    head = slot + j
                    query = q_s[head, rows, :]
                    s_i = lax.dot_general(query, k_s[head], nt, preferred_element_type=F32)
                    s_t = lax.dot_general(query, kt_s[head], nt, preferred_element_type=F32)
                    s_t = jnp.where(valid, s_t, -1e30)
                    top = jnp.maximum(
                        jnp.max(s_i, axis=1, keepdims=True), jnp.max(s_t, axis=1, keepdims=True)
                    )
                    p_i = jnp.exp2((s_i - top) * EXP_SCALE)
                    p_t = jnp.exp2((s_t - top) * EXP_SCALE)
                    total = jnp.sum(p_i, axis=1, keepdims=True) + jnp.sum(p_t, axis=1, keepdims=True)
                    mixed = jnp.dot(p_i.astype(BF16), v_s[head], preferred_element_type=F32)
                    mixed += jnp.dot(p_t.astype(BF16), vt_s[head], preferred_element_type=F32)
                    parts.append(mixed / total)
                att[pair, rows, :] = jnp.concatenate(parts, axis=1).astype(BF16)

        def block(plane):
            return rows_of(plane * rows_local, rows_local, 128)

        def project(first):
            rows = rows_of(first, near_rows, TILE)
            @pl.loop(0, width // 512)
            def _(t):
                cols = rows_of(t * 512, 512, TILE)
                lhs = jnp.concatenate([att[p, rows, :] for p in range(att.shape[0])], axis=1)
                y = jnp.dot(lhs, wp[:, cols], preferred_element_type=F32)
                hs[rows, cols] = hid[rows, cols].astype(F32) + mod[2, :, cols] * y

        def mlp_in(first, w, base, part):
            rows = rows_of(first, near_rows, TILE)
            ncol = width // 2
            y = jnp.dot(nrm[rows, :], w[:, pl.ds(part * ncol, ncol)], preferred_element_type=F32)
            inner[rows, pl.ds(base + part * ncol, ncol)] = gelu_tanh(y).astype(BF16)

        def mlp_out(first, col, ncol, far):
            rows = rows_of(first, near_rows, TILE)
            cols = pl.ds(col, ncol)
            y = jnp.dot(inner[rows, 0:width], wo_own[:, cols], preferred_element_type=F32)
            y += jnp.dot(inner[rows, width : 2 * width], wo_far[:, cols], preferred_element_type=F32)
            if far:
                rs[:, cols] = y.astype(BF16)
            else:
                mo[:, cols] = y

        near_first = half * near_rows
        far_first = (1 - half) * near_rows

        text_send = rcopy(text_half(half), text_half(half), t_s.at[1], t_r.at[1], dev_om)
        held = set()

        def need_load(k):
            if ("load", k) not in held:
                held.add(("load", k))
                loads[k].wait()

        def need_units(kind, limit=None):
            for u in range(units):
                col, ncol = unit_plan[u][1:3]
                if unit_plan[u][0] == kind and ("w", u) not in held and (limit is None or limit(col, ncol)):
                    held.add(("w", u))
                    w_step(u, 4)

        def part_of(part):
            return lambda col, ncol: part == 1 or col < width // 2

        def stage(name, arg=None):
            if name == "f":
                forward_image(arg)
            elif name.startswith("norm_"):
                which = name[5:]
                if which == "own":
                    need_load(0)
                if which == "om":
                    own_image.wait_recv()
                if which == "oe":
                    for k in range(chunks):
                        rcopy(oe_rows(k), oe_rows(k), i_s.at[chunks + k], i_r.at[chunks + k], dev_om).wait_recv()
                plane = {"own": s, "om": om, "pe": pe, "oe": oe}[which]
                norm_rows(plane * rows_local, rows_local, read_hid, 1, 0)
            elif name.startswith("qkv_"):
                need_load(1)
                qkv(block({"own": s, "om": om, "pe": pe, "oe": oe}[name[4:]]), wa_own, 0)
            elif name == "tcomb":
                text_to_mid.wait_recv()
                theirs = txt_in[...].astype(F32)[0:text_local]
                mine = txt_out[...].astype(F32)[0:text_local]
                first = jnp.where(half == 0, theirs, mine)
                second = jnp.where(half == 0, mine, theirs)
                txt[rows_of(half * 2 * text_local, 2 * text_local, 16), :] = jnp.concatenate(
                    [first, second], axis=0
                ).astype(BF16)
                text_send.start()
            elif name == "tkv_own":
                need_load(1)
                rcopy(text_half(1 - half), text_half(1 - half), t_s.at[1], t_r.at[1], dev_om).wait_recv()
                text_kv(wa_own, 0)
            elif name == "tkv_far":
                need_units("a")
                text_kv(wa_far, 4)
            elif name.startswith("qkvf"):
                need_units("a")
                qkv(pl.ds(int(name[4]) * near_rows, near_rows), wa_far, 4)
            elif name.startswith("att"):
                k = int(name[3])
                pair = (2 * s, 2 * s + 1, 2 * pe, 2 * pe + 1)[k]
                attend(2 * k, pair)
                att_copy(k, pair).start()
            elif name == "proj_f":
                need_load(2)
                att_copy(0, 2 * om).wait_recv()
                att_copy(1, 2 * om + 1).wait_recv()
                att_copy(2, 2 * oe).wait_recv()
                att_copy(3, 2 * oe + 1).wait_recv()
                project(far_first)
            elif name == "proj_n":
                project(near_first)
            elif name.startswith("norm2_"):
                norm_rows(far_first if name[6] == "f" else near_first, near_rows, read_hs, 8, 7)
            elif name.startswith("in_"):
                first = far_first if name[3] == "f" else near_first
                part = int(name[-1])
                if "own" in name:
                    need_load(3)
                    mlp_in(first, wi_own, 0, part)
                else:
                    need_units("i", part_of(part))
                    mlp_in(first, wi_far, width, part)
            elif name == "out_f":
                need_load(4)
                u = out_units[arg]
                need_units("o", lambda col, ncol: col == unit_plan[u][1])
                mlp_out(far_first, unit_plan[u][1], unit_plan[u][2], True)
                r_copy(arg).start()
            elif name == "out_n":
                need_load(4)
                need_units("o", lambda col, ncol: col // 512 == arg)
                mlp_out(near_first, arg * 512, 512, False)

        for item in STREAM:
            if item[0] == "w":
                w_step(item[1], item[2])
            else:
                stage(*item)
        for j in range(len(out_units)):
            r_copy(j).wait_recv()

        @pl.loop(0, near_rows // 64)
        def _(b):
            here = rows_of(b * 64, 64, 64)
            rows = rows_of(near_first + b * 64, 64, 64)
            value = hs[rows, :] + mod[9] * (mo[here, :] + rr[here, :].astype(F32))
            nrm[rows, :] = normalised(value, mod[6], mod[5]).astype(BF16)

        own_vel = lax.dot_general(
            final_w[...], nrm[rows_of(near_first, near_rows, TILE), :], nt, preferred_element_type=F32
        )
        vel_own[...] = own_vel.astype(BF16)
        vel_copy.start()
        vel_copy.wait_recv()
        oth_vel = vel_oth[...].astype(F32)
        cond = jnp.where(c == 0, own_vel, oth_vel)
        uncond = jnp.where(c == 0, oth_vel, own_vel)
        guided = uncond + guidance[0] * (cond - uncond)

        def total_of(v):
            return jnp.sum(jnp.sum(v * v, axis=1, keepdims=True), axis=0, keepdims=True)

        patch_half = pay_out.shape[0]
        mine_half = jnp.where(c == 0, guided[0:patch_half, :], guided[patch_half:, :])
        low, high = mine_half[:, 0:rows_local], mine_half[:, rows_local:]
        pay_out[...] = jnp.where(half == 0, low, high)
        pay_copy.start()
        line = lax.broadcasted_iota(jnp.int32, (8, 128), 0)
        sums = jnp.where(line < 4, total_of(cond), total_of(guided))
        sum_out[...] = sums
        sum_copy_oe.start()
        sum_copy_om.start()
        sum_copy_pe.start()
        sum_copy_om.wait_recv()
        finish(jnp.where(half == 0, high, low), sums + sum_in[...])

        own_image.wait_send()
        for k in range(chunks):
            rcopy(pe_rows(k), pe_rows(k), i_s.at[chunks + k], i_r.at[chunks + k], dev_om).wait_send()
        text_send.wait_send()
        for j in range(4):
            att_copy(j, 2 * s).wait_send()
        for j in range(len(out_units)):
            r_copy(j).wait_send()
        for u in range(units):
            w_sent(u)
        vel_copy.wait_send()
        pay_copy.wait_send()
        sum_copy_om.wait_send()
        sum_copy_oe.wait_send()
        sum_copy_pe.wait_send()


def fused_local(
    image_hidden,
    text_hidden,
    modulation,
    attn_weight,
    proj_weight,
    mlp_in_weight,
    mlp_out_weight,
    final_weight,
    latents,
    guidance,
    text_lengths,
    step_index,
    step_count,
):
    rows, width = image_hidden.shape[2:]
    text_rows = text_hidden.shape[2]
    padded = -(-text_rows // 16) * 16
    cols_a = attn_weight.shape[1]
    units_here = mlp_in_weight.shape[1]
    plan = UNITS
    channels = latents.shape[1]
    heads = 2 * (HEADS // 4)
    near = 2 * rows
    count = len(plan)
    outs = sum(1 for item in plan if item[0] == "o")
    vmem = pl.BlockSpec(memory_space=pltpu.VMEM)
    anywhere = pl.BlockSpec(memory_space=pl.ANY)
    dma = pltpu.SemaphoreType.DMA
    result = pl.pallas_call(
        functools.partial(fused_kernel, plan),
        out_shape=jax.ShapeDtypeStruct((3 * channels, rows), F32),
        in_specs=[anywhere] * 12,
        out_specs=vmem,
        scratch_shapes=[
            pltpu.VMEM((text_rows, width), BF16),
            pltpu.VMEM((modulation.shape[2], 1, width), F32),
            pltpu.VMEM(final_weight.shape, BF16),
            pltpu.VMEM((1, 1), F32),
            pltpu.VMEM((1, 1), jnp.int32),
            pltpu.VMEM((1, 1), jnp.int32),
            pltpu.VMEM((1, 1), jnp.int32),
            pltpu.VMEM((width, cols_a), BF16),
            pltpu.VMEM((width, units_here), BF16),
            pltpu.VMEM((units_here, width), BF16),
            pltpu.VMEM(proj_weight.shape, BF16),
            pltpu.VMEM((width, cols_a), BF16),
            pltpu.VMEM((width, units_here), BF16),
            pltpu.VMEM((units_here, width), BF16),
            pltpu.VMEM((4 * rows, width), BF16),
            pltpu.VMEM((4 * rows, width), BF16),
            pltpu.VMEM((4 * text_rows, width), BF16),
            pltpu.VMEM((padded, width), BF16),
            pltpu.VMEM((padded, width), BF16),
            pltpu.VMEM((heads, 4 * rows, HEAD), BF16),
            pltpu.VMEM((heads, 4 * rows, HEAD), BF16),
            pltpu.VMEM((heads, 4 * rows, HEAD), BF16),
            pltpu.VMEM((heads, 4 * text_rows, HEAD), BF16),
            pltpu.VMEM((heads, 4 * text_rows, HEAD), BF16),
            pltpu.VMEM((HEADS // 2, 4 * rows, 2 * HEAD), BF16),
            pltpu.VMEM((4 * rows, width), F32),
            pltpu.VMEM((4 * rows, 2 * units_here), BF16),
            pltpu.VMEM((near, width), BF16),
            pltpu.VMEM((near, width), BF16),
            pltpu.VMEM((near, width), F32),
            pltpu.VMEM((2 * channels, near), BF16),
            pltpu.VMEM((2 * channels, near), BF16),
            pltpu.VMEM((channels, rows), F32),
            pltpu.VMEM((channels, rows), F32),
            pltpu.VMEM((8, 128), F32),
            pltpu.VMEM((8, 128), F32),
            pltpu.VMEM((8, 128), F32),
            dma((count, 10)),
            dma((count, 10)),
            dma((9,)),
            dma((9,)),
            dma((2,)),
            dma((2,)),
            dma((4,)),
            dma((4,)),
            dma((outs,)),
            dma((outs,)),
            dma((4,)),
            dma((5,)),
            dma((12,)),
        ],
        compiler_params=pltpu.CompilerParams(
            collective_id=0, has_side_effects=True, vmem_limit_bytes=60 * 2**20
        ),
        cost_estimate=pl.CostEstimate(flops=15 * 10**9, bytes_accessed=17 * 10**6, transcendentals=5 * 10**6),
    )(
        image_hidden[0, 0],
        text_hidden[0, 0],
        jnp.swapaxes(modulation[0], 0, 1),
        attn_weight,
        proj_weight,
        mlp_in_weight,
        mlp_out_weight,
        final_weight,
        guidance[None],
        text_lengths,
        step_index[None],
        step_count[None],
    )
    velocity = result[:channels] + result[channels : 2 * channels]
    return velocity[None], (latents[0] + result[2 * channels :] * velocity)[None]


def solution(mesh):
    in_specs = (
        P("cfg", "req", "seq", None),
        P("cfg", "req", "seq", None),
        P("cfg", "req", None, None),
        P(None, "seq"),
        P(),
        P(None, "seq"),
        P("seq", None),
        P(),
        P("req", "cfg", "seq"),
        P("req"),
        P("cfg", "req"),
        P("req"),
        P("req"),
    )
    out_specs = (P("req", "cfg", "seq"), P("req", "cfg", "seq"))
    shape = dict(mesh.shape)
    line = shape == {"cfg": 2, "req": 4, "seq": 4}
    body = fused_local if line else local
    return jax.shard_map(body, mesh=mesh, in_specs=in_specs, out_specs=out_specs, check_vma=False)
```

```python
import functools
import math

import jax
import jax.numpy as jnp
from jax import lax
from jax.experimental import pallas as pl
from jax.experimental.pallas import tpu as pltpu
from jax.sharding import PartitionSpec as P

HEADS = 16
HEAD = 64
STEPS = 28


EPS_NORM = 1e-06


def partner(value, axis, distance):
    mask = 2**distance
    pairs = [(source, source ^ mask) for source in range(lax.axis_size(axis))]
    return lax.ppermute(value, axis, pairs)


def shifted(value, axis, shift):
    size = lax.axis_size(axis)
    return lax.ppermute(value, axis, [(source, (source - shift) % size) for source in range(size)])


def modulate(rows_in, scale_row, shift_row):
    values = rows_in.astype(jnp.float32)
    center = jnp.mean(values, axis=-1, keepdims=True)
    spread = jnp.mean(jnp.square(values - center), axis=-1, keepdims=True)
    return (
        (values - center) * lax.rsqrt(spread + EPS_NORM) * (1.0 + scale_row) + shift_row
    ).astype(jnp.bfloat16)


def sigma_of(index):
    remain = 1.0 - index.astype(jnp.float32) / STEPS
    return 3.0 * remain / (1.0 + 2.0 * remain)


def split_columns(weight_piece):
    width_in = weight_piece.shape[0]
    head_count = weight_piece.shape[1] // (5 * HEAD)
    shaped = weight_piece.reshape(width_in, head_count, 5, HEAD)
    image_cols = shaped[:, :, 0:3, :].reshape(width_in, head_count * 3 * HEAD)
    text_cols = shaped[:, :, 3:5, :].reshape(width_in, head_count * 2 * HEAD)
    return (image_cols, text_cols)


def local(
    image_hidden,
    text_hidden,
    modulation,
    attn_weight,
    proj_weight,
    mlp_in_weight,
    mlp_out_weight,
    final_weight,
    latents,
    guidance,
    text_lengths,
    step_index,
    step_count,
):
    seq_size = lax.axis_size("seq")
    local_heads = HEADS // seq_size
    image_rows = image_hidden[0, 0]
    text_rows = text_hidden[0, 0]
    mod_rows = modulation[0, 0]
    local_rows = image_rows.shape[0]
    image_total = local_rows * seq_size
    text_total = text_rows.shape[0] * seq_size
    image_norm = modulate(image_rows, mod_rows[1], mod_rows[0])
    text_norm = modulate(text_rows, mod_rows[4], mod_rows[3])
    seq_index = lax.axis_index("seq")
    own_norm = jnp.concatenate([image_norm, text_norm], axis=0)
    gathered = jnp.stack([own_norm] + [shifted(own_norm, "seq", k) for k in range(1, seq_size)])
    image_all = gathered[:, :local_rows].reshape(image_total, -1)
    text_all = gathered[:, local_rows:].reshape(text_total, -1)
    image_cols, text_cols = split_columns(attn_weight)
    image_qkv = jnp.dot(image_all, image_cols, preferred_element_type=jnp.float32).astype(
        jnp.bfloat16
    )
    text_kv = jnp.dot(text_all, text_cols, preferred_element_type=jnp.float32).astype(
        jnp.bfloat16
    )
    image_qkv = image_qkv.reshape(image_total, local_heads, 3, HEAD)
    text_kv = text_kv.reshape(text_total, local_heads, 2, HEAD)
    keys_all = jnp.concatenate([image_qkv[:, :, 1], text_kv[:, :, 0]], axis=0)
    values_all = jnp.concatenate([image_qkv[:, :, 2], text_kv[:, :, 1]], axis=0)
    text_local = text_rows.shape[0]
    sources = (seq_index + jnp.arange(seq_size, dtype=jnp.int32)) % seq_size
    slots = (sources[:, None] * text_local + jnp.arange(text_local, dtype=jnp.int32)).reshape(-1)
    valid = jnp.concatenate([jnp.ones((image_total,), dtype=bool), slots < text_lengths[0, 0]])
    block_rows = local_rows
    while block_rows < 512 and image_total % (block_rows * 2) == 0:
        block_rows = block_rows * 2
    block_total = image_total // block_rows
    query_blocks = image_qkv[:, :, 0].reshape(block_total, block_rows, local_heads, HEAD)

    def attend(query_block):
        scores = jnp.einsum(
            "qhe,khe->hqk", query_block, keys_all, preferred_element_type=jnp.float32
        ) * HEAD ** (-0.5)
        scores = jnp.where(valid[None, None, :], scores, -1e30)
        row_max = jnp.max(scores, axis=2, keepdims=True)
        weights = jnp.exp(scores - row_max)
        total = jnp.sum(weights, axis=2, keepdims=True)
        probs = weights.astype(jnp.bfloat16)
        mixed = (
            jnp.einsum("hqk,khe->hqe", probs, values_all, preferred_element_type=jnp.float32)
            / total
        )
        return jnp.transpose(mixed.astype(jnp.bfloat16), (1, 0, 2))

    attended = lax.map(attend, query_blocks).reshape(image_total, local_heads * HEAD)
    attended = attended.reshape(seq_size, local_rows, local_heads * HEAD)
    head_width = local_heads * HEAD
    projected = jnp.zeros((local_rows, proj_weight.shape[1]), jnp.float32)
    for k in range(seq_size):
        piece = attended[k] if k == 0 else shifted(attended[k], "seq", -k)
        rows = lax.dynamic_slice_in_dim(
            proj_weight, ((seq_index - k) % seq_size) * head_width, head_width, 0
        )
        projected = projected + jnp.dot(piece, rows, preferred_element_type=jnp.float32)
    hidden = image_rows.astype(jnp.float32) + mod_rows[2] * projected
    mlp_norm = modulate(hidden, mod_rows[8], mod_rows[7])
    mlp_out = jnp.zeros((local_rows, mlp_out_weight.shape[1]), jnp.float32)
    for k in range(seq_size):
        piece = mlp_norm if k == 0 else shifted(mlp_norm, "seq", k)
        inner = jax.nn.gelu(
            jnp.dot(piece, mlp_in_weight, preferred_element_type=jnp.float32), approximate=True
        ).astype(jnp.bfloat16)
        part = jnp.dot(inner, mlp_out_weight, preferred_element_type=jnp.float32).astype(
            jnp.bfloat16
        )
        part = part if k == 0 else shifted(part, "seq", -k)
        mlp_out = mlp_out + part.astype(jnp.float32)
    block_out = hidden + mod_rows[9] * mlp_out
    final_norm = modulate(block_out, mod_rows[6], mod_rows[5])
    own_vel = lax.dot_general(
        final_weight, final_norm, (((1,), (1,)), ((), ())), preferred_element_type=jnp.float32
    )
    partner_vel = partner(own_vel.astype(jnp.bfloat16), "cfg", 0).astype(own_vel.dtype)
    leading = lax.axis_index("cfg") == 0
    cond_vel = jnp.where(leading, own_vel, partner_vel)
    uncond_vel = jnp.where(leading, partner_vel, own_vel)
    guided = uncond_vel + guidance[...] * (cond_vel - uncond_vel)
    squares = jnp.stack([jnp.sum(cond_vel * cond_vel), jnp.sum(guided * guided)])
    squares = sum(
        [squares] + [shifted(squares, "seq", k) for k in range(1, seq_size)], jnp.zeros(2)
    )
    cond_sq, guided_sq = squares[0], squares[1]
    entries = own_vel.shape[0] * image_total
    rms_cond = jnp.sqrt(cond_sq / entries + EPS_NORM)
    rms_guided = jnp.sqrt(guided_sq / entries + EPS_NORM)
    result_vel = 0.7 * (guided * (rms_cond / rms_guided)) + 0.3 * guided
    channel_half = latents.shape[1]
    channel_start = lax.axis_index("cfg") * channel_half
    own_channels = lax.dynamic_slice_in_dim(result_vel, channel_start, channel_half, 0)
    next_index = jnp.minimum(step_index[0] + step_count[0], STEPS)
    step_size = sigma_of(next_index) - sigma_of(step_index[0])
    moved = latents[0] + step_size * own_channels
    return (own_channels[None], moved[None])


BF16 = jnp.bfloat16
F32 = jnp.float32
MESH_ID = pl.DeviceIdType.MESH
EXP_SCALE = math.log2(math.e) * HEAD ** (-0.5)
TILE = 256
UNITS = [
    ("a", 0, 256, "q"), ("a", 256, 256, "q"), ("a", 512, 256, "q"), ("a", 768, 256, "q"),
    ("a", 1024, 256, "q"), ("i", 0, 256, "q"), ("i", 256, 256, "q"), ("i", 512, 256, "q"),
    ("i", 768, 256, "q"), ("i", 1024, 256, "q"), ("i", 1280, 256, "x"), ("o", 0, 256, "y"),
    ("o", 256, 256, "q"), ("o", 512, 256, "q"), ("o", 768, 256, "x"), ("o", 1024, 256, "y"),
    ("o", 1280, 256, "x"),
]
FIRST_SENDS = [
    ("w", 0, 0), ("w", 1, 0), ("w", 2, 0), ("i", 0), ("i", 1), ("w", 3, 0),
    ("t",), ("w", 4, 0), ("i", 2), ("i", 3),
]
STREAM = [
    ("norm_own",), ("qkv_own",), ("w", 0, 1), ("w", 1, 1), ("w", 2, 1), ("w", 0, 2),
    ("f", 0), ("w", 1, 2), ("norm_om",), ("qkv_om",), ("f", 1), ("w", 2, 2),
    ("w", 0, 3), ("w", 3, 1), ("w", 1, 3), ("w", 2, 3), ("tcomb",), ("w", 3, 2),
    ("w", 4, 1), ("w", 3, 3), ("f", 2), ("w", 4, 2), ("f", 3), ("norm_pe",),
    ("qkv_pe",), ("tkv_own",), ("w", 5, 1), ("w", 4, 3), ("w", 6, 1), ("tkv_far",),
    ("w", 7, 1), ("norm_oe",), ("w", 5, 2), ("qkv_oe",), ("att0",), ("w", 8, 1),
    ("w", 6, 2), ("att1",), ("w", 9, 1), ("w", 7, 2), ("w", 5, 3), ("qkvf0",),
    ("w", 8, 2), ("qkvf1",), ("w", 10, 1), ("w", 6, 3), ("att2",), ("w", 9, 2),
    ("att3",), ("w", 7, 3), ("w", 11, 1), ("w", 8, 3), ("w", 12, 1), ("w", 13, 1),
    ("w", 10, 2), ("w", 9, 3), ("proj_f",), ("w", 11, 2), ("norm2_f",), ("w", 14, 1),
    ("w", 12, 2), ("in_f_own0",), ("w", 13, 2), ("in_f_own1",), ("in_f_far0",), ("w", 15, 1),
    ("in_f_far1",), ("out_f", 0), ("w", 14, 2), ("proj_n",), ("w", 12, 3), ("w", 16, 1),
    ("w", 13, 3), ("out_f", 3), ("norm2_n",), ("w", 15, 2), ("out_f", 1), ("out_f", 2),
    ("in_n_own0",), ("out_f", 4), ("in_n_own1",), ("w", 16, 2), ("in_n_far0",), ("in_n_far1",),
    ("out_f", 5), ("out_n", 0), ("out_n", 1), ("out_n", 2),
]


def normalised(values, scale_row, shift_row):
    center = jnp.mean(values, axis=-1, keepdims=True)
    moved = values - center
    spread = jnp.mean(moved * moved, axis=-1, keepdims=True)
    return moved * lax.rsqrt(spread + EPS_NORM) * (1.0 + scale_row) + shift_row


def gelu_tanh(v):
    part = 0.5 * v
    return part + part * jnp.tanh(v * (0.7978845608028654 + 0.7978845608028654 * 0.044715 * (v * v)))


def fused_kernel(
    unit_plan,
    image,
    text_hbm,
    mod_hbm,
    wa_hbm,
    wp_hbm,
    wi_hbm,
    wo_hbm,
    final_hbm,
    guidance_hbm,
    text_len_hbm,
    step_index_hbm,
    step_count_hbm,
    out_ref,
    text,
    mod,
    final_w,
    guidance,
    text_len,
    step_index,
    step_count,
    wa_own,
    wi_own,
    wo_own,
    wp,
    wa_far,
    wi_far,
    wo_far,
    hid,
    nrm,
    txt,
    txt_out,
    txt_in,
    q_s,
    k_s,
    v_s,
    kt_s,
    vt_s,
    att,
    hs,
    inner,
    rs,
    rr,
    mo,
    vel_own,
    vel_oth,
    pay_out,
    pay_in,
    sum_in,
    sum_out,
    sum_near,
    w_r,
    w_s,
    i_r,
    i_s,
    t_r,
    t_s,
    o_r,
    o_s,
    r_r,
    r_s,
    f_r,
    f_s,
    l_s,
):
    c = lax.axis_index("cfg")
    r = lax.axis_index("req")
    s = lax.axis_index("seq")
    half = s // 2
    is_mid = (s == 1) | (s == 2)
    om = 3 - s
    pe = half * 3
    oe = 3 - pe
    near_mid = 1 + half
    far_mid = 2 - half
    rows_local = image.shape[0]
    rows_all = hid.shape[0]
    near_rows = 2 * rows_local
    width = image.shape[1]
    piece = width // 8
    text_local = text.shape[0]
    text_all = txt.shape[0]

    rx = lax.rem(r + 2, 4)
    rc = r + 1 - 2 * lax.rem(r, 2)
    rcx = lax.rem(rc + 2, 4)
    cy = 1 - c
    dev_x = (c, rx, s)
    dev_y = (cy, r, s)
    dev_c = (c, rc, s)
    dev_om = (c, r, om)
    dev_pe = (c, r, pe)
    dev_oe = (c, r, oe)
    dev_near = (c, r, near_mid)
    dev_far = (c, r, far_mid)

    def rcopy(src, dst, ssem, rsem, dev):
        return pltpu.make_async_remote_copy(
            src_ref=src, dst_ref=dst, send_sem=ssem, recv_sem=rsem, device_id=dev, device_id_type=MESH_ID
        )

    def rows_of(first, count, align):
        return pl.ds(pl.multiple_of(first, align), count)

    own_rows = rows_of(s * rows_local, rows_local, 128)
    weights = {"a": (wa_hbm, wa_far), "i": (wi_hbm, wi_far), "o": (wo_hbm, wo_far)}
    units = len(unit_plan)

    def piece_rows(cc, rr_, first=0, count=None):
        start = (cc * 4 + rr_) * piece + first
        return rows_of(start, piece if count is None else count, 32)

    def wcopy(u, k, rows, dev, src=None):
        kind, col, ncol, _ = unit_plan[u]
        far = weights[kind][1]
        at = far.at[rows, pl.ds(col, ncol)]
        return rcopy(at if src is None else src, at, w_s.at[u, k], w_r.at[u, k], dev)

    hp = piece // 2

    def w_first(u, rows, line, core):
        for k, dev in line:
            wcopy(u, k, rows, dev).start()
        wcopy(u, core, rows, dev_c).start()

    def w_step(u, step):
        mode = unit_plan[u][3]
        mine = piece_rows(c, r)
        if step == 1:
            wcopy(u, 0, mine, dev_pe).wait_recv()
            if mode == "q":
                w_first(u, mine, ((1, dev_x), (2, dev_y)), 5)
            elif mode == "x":
                w_first(u, mine, ((1, dev_x),), 5)
                wcopy(u, 9, piece_rows(cy, r), dev_pe).wait_recv()
                w_first(u, piece_rows(cy, r), ((4, dev_x),), 7)
            else:
                w_first(u, mine, ((2, dev_y),), 5)
                wcopy(u, 9, piece_rows(c, rx), dev_pe).wait_recv()
                w_first(u, piece_rows(c, rx), ((3, dev_y),), 6)
        elif step == 2:
            if mode == "q":
                wcopy(u, 1, piece_rows(c, rx), dev_x).wait_recv()
                wcopy(u, 3, piece_rows(c, rx, 0, hp), dev_y).start()
                wcopy(u, 2, piece_rows(cy, r), dev_y).wait_recv()
                wcopy(u, 4, piece_rows(cy, r, hp, hp), dev_x).start()
                wcopy(u, 6, piece_rows(c, rx), dev_c).start()
                wcopy(u, 7, piece_rows(cy, r), dev_c).start()
            elif mode == "x":
                wcopy(u, 1, piece_rows(c, rx), dev_x).wait_recv()
                wcopy(u, 6, piece_rows(c, rx), dev_c).start()
                wcopy(u, 4, piece_rows(cy, rx), dev_x).wait_recv()
                wcopy(u, 8, piece_rows(cy, rx), dev_c).start()
            else:
                wcopy(u, 2, piece_rows(cy, r), dev_y).wait_recv()
                wcopy(u, 7, piece_rows(cy, r), dev_c).start()
                wcopy(u, 3, piece_rows(cy, rx), dev_y).wait_recv()
                wcopy(u, 8, piece_rows(cy, rx), dev_c).start()
        elif step == 3:
            if mode == "q":
                wcopy(u, 3, piece_rows(cy, rx, 0, hp), dev_y).wait_recv()
                wcopy(u, 4, piece_rows(cy, rx, hp, hp), dev_x).wait_recv()
                wcopy(u, 8, piece_rows(cy, rx), dev_c).start()
        elif step == 4:
            wcopy(u, 5, piece_rows(c, rc), dev_c).wait_recv()
            wcopy(u, 6, piece_rows(c, rcx), dev_c).wait_recv()
            wcopy(u, 7, piece_rows(cy, rc), dev_c).wait_recv()
            wcopy(u, 8, piece_rows(cy, rcx), dev_c).wait_recv()

    def w_sent(u):
        mode = unit_plan[u][3]
        mine = piece_rows(c, r)
        if mode != "y":
            wcopy(u, 1, mine, dev_x).wait_send()
        if mode != "x":
            wcopy(u, 2, mine, dev_y).wait_send()
        if mode == "q":
            wcopy(u, 3, piece_rows(c, rx, 0, hp), dev_y).wait_send()
            wcopy(u, 4, piece_rows(cy, r, hp, hp), dev_x).wait_send()
        elif mode == "x":
            wcopy(u, 4, piece_rows(cy, r), dev_x).wait_send()
        else:
            wcopy(u, 3, piece_rows(c, rx), dev_y).wait_send()
        wcopy(u, 5, mine, dev_c).wait_send()
        wcopy(u, 6, piece_rows(c, rx), dev_c).wait_send()
        wcopy(u, 7, piece_rows(cy, r), dev_c).wait_send()
        wcopy(u, 8, piece_rows(cy, rx), dev_c).wait_send()

    chunks = 4
    chunk = rows_local // chunks

    def end_image(k):
        src = image.at[pl.ds(k * chunk, chunk)]
        dst = hid.at[rows_of(s * rows_local + k * chunk, chunk, 32)]
        return rcopy(src, dst, i_s.at[k], i_r.at[k], dev_near)

    def pe_rows(k):
        return hid.at[rows_of(pe * rows_local + k * chunk, chunk, 32)]

    def oe_rows(k):
        return hid.at[rows_of(oe * rows_local + k * chunk, chunk, 32)]

    def forward_image(k):
        rcopy(pe_rows(k), pe_rows(k), i_s.at[k], i_r.at[k], dev_om).wait_recv()
        rcopy(pe_rows(k), pe_rows(k), i_s.at[chunks + k], i_r.at[chunks + k], dev_om).start()

    own_image = rcopy(image, hid.at[own_rows], i_s.at[2 * chunks], i_r.at[2 * chunks], dev_om)
    text_to_mid = rcopy(txt_out, txt_in, t_s.at[0], t_r.at[0], dev_near)

    def text_half(which):
        return txt.at[rows_of(which * 2 * text_local, 2 * text_local, 16)]

    def att_copy(j, pair):
        return rcopy(att.at[pair], att.at[pair], o_s.at[j], o_r.at[j], dev_om)

    out_units = [u for u in range(units) if unit_plan[u][0] == "o"]

    def r_copy(j):
        cols = pl.ds(unit_plan[out_units[j]][1], unit_plan[out_units[j]][2])
        return rcopy(rs.at[:, cols], rr.at[:, cols], r_s.at[j], r_r.at[j], dev_om)

    vel_copy = rcopy(vel_own, vel_oth, f_s.at[0], f_r.at[0], dev_y)
    pay_copy = rcopy(pay_out, pay_in, f_s.at[1], f_r.at[1], dev_pe)
    sum_copy_om = rcopy(sum_out, sum_in, f_s.at[2], f_r.at[2], dev_om)
    sum_copy_oe = rcopy(sum_out, sum_in, f_s.at[3], f_r.at[2], dev_oe)
    sum_copy_pe = rcopy(sum_out, sum_near, f_s.at[4], f_r.at[3], dev_pe)

    def load(i, src, dst):
        return pltpu.make_async_copy(src, dst, l_s.at[i])

    loads = [
        load(0, image, hid.at[own_rows]),
        load(1, wa_hbm, wa_own),
        load(2, wp_hbm, wp),
        load(3, wi_hbm, wi_own),
        load(4, wo_hbm, wo_own),
    ]
    early = [load(5, text_hbm, text), load(6, mod_hbm, mod)]
    late = [
        load(7, final_hbm, final_w),
        load(8, guidance_hbm, guidance),
        load(9, text_len_hbm, text_len),
        load(10, step_index_hbm, step_index),
        load(11, step_count_hbm, step_count),
    ]

    barrier = pltpu.get_barrier_semaphore()

    def greet(devs):
        for dev in devs:
            pl.semaphore_signal(barrier, inc=1, device_id=dev, device_id_type=MESH_ID)

    for item in early:
        item.start()

    @pl.when(is_mid)
    def _():
        for item in loads[:2]:
            item.start()
        greet((dev_pe, dev_om, dev_oe, dev_x, dev_y, dev_c))

    @pl.when(jnp.logical_not(is_mid))
    def _():
        greet((dev_near, dev_far))

    for item in late:
        item.start()
    for item in early:
        item.wait()

    text_norm = normalised(text[...].astype(F32), mod[4], mod[3])
    pad = txt_out.shape[0] - text_local
    txt_out[...] = jnp.concatenate([text_norm, jnp.zeros((pad, width), F32)], axis=0).astype(BF16)

    def finish(guided_half, sums):
        entries = 2.0 * guided_half.shape[0] * rows_all
        rms_cond = jnp.sqrt(sums[0:1, :] / entries + EPS_NORM)
        rms_guided = jnp.sqrt(sums[4:5, :] / entries + EPS_NORM)
        rescaled = 0.7 * (guided_half * (rms_cond / rms_guided))
        now = step_index[...]
        after = jnp.minimum(now + step_count[...], STEPS)

        def sigma(i):
            remain = 1.0 - i.astype(F32) / STEPS
            return 3.0 * remain / (1.0 + 2.0 * remain)

        lines = guided_half.shape[0]
        out_ref[0:lines, :] = rescaled
        out_ref[lines : 2 * lines, :] = 0.3 * guided_half
        out_ref[2 * lines :, :] = jnp.zeros(guided_half.shape, F32) + (sigma(after) - sigma(now))

    for item in late:
        item.wait()

    @pl.when(jnp.logical_not(is_mid))
    def _():
        pl.semaphore_wait(barrier, 2)

        def unit_send(u):
            kind, col, ncol, mode = unit_plan[u]
            sends = [(0, piece_rows(c, r))]
            if mode == "x":
                sends.append((9, piece_rows(cy, r)))
            elif mode == "y":
                sends.append((9, piece_rows(c, rx)))
            src = weights[kind][0]
            return [wcopy(u, k, rows, dev_near, src.at[rows, pl.ds(col, ncol)]) for k, rows in sends]

        order = []
        sent = set()
        for item in FIRST_SENDS:
            if item[0] == "w":
                order.append(unit_send(item[1])[item[2]])
                sent.add(item[1:])
            else:
                order.append(end_image(item[1]) if item[0] == "i" else text_to_mid)
        for u in range(units):
            order += [item for k, item in enumerate(unit_send(u)) if (u, k) not in sent]
        for at, item in enumerate(order):
            item.start()
            if at >= 1:
                order[at - 1].wait_send()
        order[-1].wait_send()
        pay_copy.wait_recv()
        sum_copy_oe.wait_recv()
        sum_copy_pe.wait_recv()
        finish(pay_in[...], sum_near[...] + sum_in[...])

    @pl.when(is_mid)
    def _():
        pl.semaphore_wait(barrier, 6)
        own_image.start()
        for item in loads[2:]:
            item.start()

        def norm_rows(first, count, read, scale, shift):
            @pl.loop(0, count // 64)
            def _(b):
                at = first + b * 64
                out = normalised(read(at), mod[scale], mod[shift])
                nrm[rows_of(at, 64, 32), :] = out.astype(BF16)

        def read_hid(at):
            return hid[rows_of(at, 64, 32), :].astype(F32)

        def read_hs(at):
            return hs[rows_of(at, 64, 32), :]

        def qkv(rows, w, base):
            @pl.loop(0, 2)
            def _(p):
                cols = rows_of(p * 10 * HEAD, 8 * HEAD, 128)
                y = jnp.dot(nrm[rows, :], w[:, cols], preferred_element_type=F32).astype(BF16)
                for j in range(2):
                    o = j * 5 * HEAD
                    head = base + 2 * p + j
                    q_s[head, rows, :] = y[:, o : o + HEAD]
                    k_s[head, rows, :] = y[:, o + HEAD : o + 2 * HEAD]
                    v_s[head, rows, :] = y[:, o + 2 * HEAD : o + 3 * HEAD]

        def text_kv(w, base):
            @pl.loop(0, 2)
            def _(p):
                start = p * 10 * HEAD
                first = jnp.dot(txt[...], w[:, rows_of(start + 2 * HEAD, 4 * HEAD, 128)], preferred_element_type=F32)
                second = jnp.dot(txt[...], w[:, rows_of(start + 8 * HEAD, 2 * HEAD, 128)], preferred_element_type=F32)
                for j, y in enumerate((first[:, HEAD : 3 * HEAD], second)):
                    head = base + 2 * p + j
                    kt_s[head] = y[:, 0:HEAD].astype(BF16)
                    vt_s[head] = y[:, HEAD : 2 * HEAD].astype(BF16)

        slots = lax.broadcasted_iota(jnp.int32, (1, text_all), 1)
        valid = slots < text_len[...]
        nt = (((1,), (1,)), ((), ()))

        def attend(slot, pair):
            @pl.loop(0, rows_all // 512)
            def _(b):
                rows = rows_of(b * 512, 512, 128)
                parts = []
                for j in range(2):
                    head = slot + j
                    query = q_s[head, rows, :]
                    s_i = lax.dot_general(query, k_s[head], nt, preferred_element_type=F32)
                    s_t = lax.dot_general(query, kt_s[head], nt, preferred_element_type=F32)
                    s_t = jnp.where(valid, s_t, -1e30)
                    top = jnp.maximum(
                        jnp.max(s_i, axis=1, keepdims=True), jnp.max(s_t, axis=1, keepdims=True)
                    )
                    p_i = jnp.exp2((s_i - top) * EXP_SCALE)
                    p_t = jnp.exp2((s_t - top) * EXP_SCALE)
                    total = jnp.sum(p_i, axis=1, keepdims=True) + jnp.sum(p_t, axis=1, keepdims=True)
                    mixed = jnp.dot(p_i.astype(BF16), v_s[head], preferred_element_type=F32)
                    mixed += jnp.dot(p_t.astype(BF16), vt_s[head], preferred_element_type=F32)
                    parts.append(mixed / total)
                att[pair, rows, :] = jnp.concatenate(parts, axis=1).astype(BF16)

        def block(plane):
            return rows_of(plane * rows_local, rows_local, 128)

        def project(first):
            rows = rows_of(first, near_rows, TILE)
            @pl.loop(0, width // 512)
            def _(t):
                cols = rows_of(t * 512, 512, TILE)
                lhs = jnp.concatenate([att[p, rows, :] for p in range(att.shape[0])], axis=1)
                y = jnp.dot(lhs, wp[:, cols], preferred_element_type=F32)
                hs[rows, cols] = hid[rows, cols].astype(F32) + mod[2, :, cols] * y

        def mlp_in(first, w, base, part):
            rows = rows_of(first, near_rows, TILE)
            ncol = width // 2
            y = jnp.dot(nrm[rows, :], w[:, pl.ds(part * ncol, ncol)], preferred_element_type=F32)
            inner[rows, pl.ds(base + part * ncol, ncol)] = gelu_tanh(y).astype(BF16)

        def mlp_out(first, col, ncol, far):
            rows = rows_of(first, near_rows, TILE)
            cols = pl.ds(col, ncol)
            y = jnp.dot(inner[rows, 0:width], wo_own[:, cols], preferred_element_type=F32)
            y += jnp.dot(inner[rows, width : 2 * width], wo_far[:, cols], preferred_element_type=F32)
            if far:
                rs[:, cols] = y.astype(BF16)
            else:
                mo[:, cols] = y

        near_first = half * near_rows
        far_first = (1 - half) * near_rows

        text_send = rcopy(text_half(half), text_half(half), t_s.at[1], t_r.at[1], dev_om)
        held = set()

        def need_load(k):
            if ("load", k) not in held:
                held.add(("load", k))
                loads[k].wait()

        def need_units(kind, limit=None):
            for u in range(units):
                col, ncol = unit_plan[u][1:3]
                if unit_plan[u][0] == kind and ("w", u) not in held and (limit is None or limit(col, ncol)):
                    held.add(("w", u))
                    w_step(u, 4)

        def part_of(part):
            return lambda col, ncol: part == 1 or col < width // 2

        def stage(name, arg=None):
            if name == "f":
                forward_image(arg)
            elif name.startswith("norm_"):
                which = name[5:]
                if which == "own":
                    need_load(0)
                if which == "om":
                    own_image.wait_recv()
                if which == "oe":
                    for k in range(chunks):
                        rcopy(oe_rows(k), oe_rows(k), i_s.at[chunks + k], i_r.at[chunks + k], dev_om).wait_recv()
                plane = {"own": s, "om": om, "pe": pe, "oe": oe}[which]
                norm_rows(plane * rows_local, rows_local, read_hid, 1, 0)
            elif name.startswith("qkv_"):
                need_load(1)
                qkv(block({"own": s, "om": om, "pe": pe, "oe": oe}[name[4:]]), wa_own, 0)
            elif name == "tcomb":
                text_to_mid.wait_recv()
                theirs = txt_in[...].astype(F32)[0:text_local]
                mine = txt_out[...].astype(F32)[0:text_local]
                first = jnp.where(half == 0, theirs, mine)
                second = jnp.where(half == 0, mine, theirs)
                txt[rows_of(half * 2 * text_local, 2 * text_local, 16), :] = jnp.concatenate(
                    [first, second], axis=0
                ).astype(BF16)
                text_send.start()
            elif name == "tkv_own":
                need_load(1)
                rcopy(text_half(1 - half), text_half(1 - half), t_s.at[1], t_r.at[1], dev_om).wait_recv()
                text_kv(wa_own, 0)
            elif name == "tkv_far":
                need_units("a")
                text_kv(wa_far, 4)
            elif name.startswith("qkvf"):
                need_units("a")
                qkv(pl.ds(int(name[4]) * near_rows, near_rows), wa_far, 4)
            elif name.startswith("att"):
                k = int(name[3])
                pair = (2 * s, 2 * s + 1, 2 * pe, 2 * pe + 1)[k]
                attend(2 * k, pair)
                att_copy(k, pair).start()
            elif name == "proj_f":
                need_load(2)
                att_copy(0, 2 * om).wait_recv()
                att_copy(1, 2 * om + 1).wait_recv()
                att_copy(2, 2 * oe).wait_recv()
                att_copy(3, 2 * oe + 1).wait_recv()
                project(far_first)
            elif name == "proj_n":
                project(near_first)
            elif name.startswith("norm2_"):
                norm_rows(far_first if name[6] == "f" else near_first, near_rows, read_hs, 8, 7)
            elif name.startswith("in_"):
                first = far_first if name[3] == "f" else near_first
                part = int(name[-1])
                if "own" in name:
                    need_load(3)
                    mlp_in(first, wi_own, 0, part)
                else:
                    need_units("i", part_of(part))
                    mlp_in(first, wi_far, width, part)
            elif name == "out_f":
                need_load(4)
                u = out_units[arg]
                need_units("o", lambda col, ncol: col == unit_plan[u][1])
                mlp_out(far_first, unit_plan[u][1], unit_plan[u][2], True)
                r_copy(arg).start()
            elif name == "out_n":
                need_load(4)
                need_units("o", lambda col, ncol: col // 512 == arg)
                mlp_out(near_first, arg * 512, 512, False)

        for item in STREAM:
            if item[0] == "w":
                w_step(item[1], item[2])
            else:
                stage(*item)
        for j in range(len(out_units)):
            r_copy(j).wait_recv()

        @pl.loop(0, near_rows // 64)
        def _(b):
            here = rows_of(b * 64, 64, 64)
            rows = rows_of(near_first + b * 64, 64, 64)
            value = hs[rows, :] + mod[9] * (mo[here, :] + rr[here, :].astype(F32))
            nrm[rows, :] = normalised(value, mod[6], mod[5]).astype(BF16)

        own_vel = lax.dot_general(
            final_w[...], nrm[rows_of(near_first, near_rows, TILE), :], nt, preferred_element_type=F32
        )
        vel_own[...] = own_vel.astype(BF16)
        vel_copy.start()
        vel_copy.wait_recv()
        oth_vel = vel_oth[...].astype(F32)
        cond = jnp.where(c == 0, own_vel, oth_vel)
        uncond = jnp.where(c == 0, oth_vel, own_vel)
        guided = uncond + guidance[0] * (cond - uncond)

        def total_of(v):
            return jnp.sum(jnp.sum(v * v, axis=1, keepdims=True), axis=0, keepdims=True)

        patch_half = pay_out.shape[0]
        mine_half = jnp.where(c == 0, guided[0:patch_half, :], guided[patch_half:, :])
        low, high = mine_half[:, 0:rows_local], mine_half[:, rows_local:]
        pay_out[...] = jnp.where(half == 0, low, high)
        pay_copy.start()
        line = lax.broadcasted_iota(jnp.int32, (8, 128), 0)
        sums = jnp.where(line < 4, total_of(cond), total_of(guided))
        sum_out[...] = sums
        sum_copy_oe.start()
        sum_copy_om.start()
        sum_copy_pe.start()
        sum_copy_om.wait_recv()
        finish(jnp.where(half == 0, high, low), sums + sum_in[...])

        own_image.wait_send()
        for k in range(chunks):
            rcopy(pe_rows(k), pe_rows(k), i_s.at[chunks + k], i_r.at[chunks + k], dev_om).wait_send()
        text_send.wait_send()
        for j in range(4):
            att_copy(j, 2 * s).wait_send()
        for j in range(len(out_units)):
            r_copy(j).wait_send()
        for u in range(units):
            w_sent(u)
        vel_copy.wait_send()
        pay_copy.wait_send()
        sum_copy_om.wait_send()
        sum_copy_oe.wait_send()
        sum_copy_pe.wait_send()


def fused_local(
    image_hidden,
    text_hidden,
    modulation,
    attn_weight,
    proj_weight,
    mlp_in_weight,
    mlp_out_weight,
    final_weight,
    latents,
    guidance,
    text_lengths,
    step_index,
    step_count,
):
    rows, width = image_hidden.shape[2:]
    text_rows = text_hidden.shape[2]
    padded = -(-text_rows // 16) * 16
    cols_a = attn_weight.shape[1]
    units_here = mlp_in_weight.shape[1]
    plan = UNITS
    channels = latents.shape[1]
    heads = 2 * (HEADS // 4)
    near = 2 * rows
    count = len(plan)
    outs = sum(1 for item in plan if item[0] == "o")
    vmem = pl.BlockSpec(memory_space=pltpu.VMEM)
    anywhere = pl.BlockSpec(memory_space=pl.ANY)
    dma = pltpu.SemaphoreType.DMA
    result = pl.pallas_call(
        functools.partial(fused_kernel, plan),
        out_shape=jax.ShapeDtypeStruct((3 * channels, rows), F32),
        in_specs=[anywhere] * 12,
        out_specs=vmem,
        scratch_shapes=[
            pltpu.VMEM((text_rows, width), BF16),
            pltpu.VMEM((modulation.shape[2], 1, width), F32),
            pltpu.VMEM(final_weight.shape, BF16),
            pltpu.VMEM((1, 1), F32),
            pltpu.VMEM((1, 1), jnp.int32),
            pltpu.VMEM((1, 1), jnp.int32),
            pltpu.VMEM((1, 1), jnp.int32),
            pltpu.VMEM((width, cols_a), BF16),
            pltpu.VMEM((width, units_here), BF16),
            pltpu.VMEM((units_here, width), BF16),
            pltpu.VMEM(proj_weight.shape, BF16),
            pltpu.VMEM((width, cols_a), BF16),
            pltpu.VMEM((width, units_here), BF16),
            pltpu.VMEM((units_here, width), BF16),
            pltpu.VMEM((4 * rows, width), BF16),
            pltpu.VMEM((4 * rows, width), BF16),
            pltpu.VMEM((4 * text_rows, width), BF16),
            pltpu.VMEM((padded, width), BF16),
            pltpu.VMEM((padded, width), BF16),
            pltpu.VMEM((heads, 4 * rows, HEAD), BF16),
            pltpu.VMEM((heads, 4 * rows, HEAD), BF16),
            pltpu.VMEM((heads, 4 * rows, HEAD), BF16),
            pltpu.VMEM((heads, 4 * text_rows, HEAD), BF16),
            pltpu.VMEM((heads, 4 * text_rows, HEAD), BF16),
            pltpu.VMEM((HEADS // 2, 4 * rows, 2 * HEAD), BF16),
            pltpu.VMEM((4 * rows, width), F32),
            pltpu.VMEM((4 * rows, 2 * units_here), BF16),
            pltpu.VMEM((near, width), BF16),
            pltpu.VMEM((near, width), BF16),
            pltpu.VMEM((near, width), F32),
            pltpu.VMEM((2 * channels, near), BF16),
            pltpu.VMEM((2 * channels, near), BF16),
            pltpu.VMEM((channels, rows), F32),
            pltpu.VMEM((channels, rows), F32),
            pltpu.VMEM((8, 128), F32),
            pltpu.VMEM((8, 128), F32),
            pltpu.VMEM((8, 128), F32),
            dma((count, 10)),
            dma((count, 10)),
            dma((9,)),
            dma((9,)),
            dma((2,)),
            dma((2,)),
            dma((4,)),
            dma((4,)),
            dma((outs,)),
            dma((outs,)),
            dma((4,)),
            dma((5,)),
            dma((12,)),
        ],
        compiler_params=pltpu.CompilerParams(
            collective_id=0, has_side_effects=True, vmem_limit_bytes=60 * 2**20
        ),
        cost_estimate=pl.CostEstimate(flops=15 * 10**9, bytes_accessed=17 * 10**6, transcendentals=5 * 10**6),
    )(
        image_hidden[0, 0],
        text_hidden[0, 0],
        jnp.swapaxes(modulation[0], 0, 1),
        attn_weight,
        proj_weight,
        mlp_in_weight,
        mlp_out_weight,
        final_weight,
        guidance[None],
        text_lengths,
        step_index[None],
        step_count[None],
    )
    velocity = result[:channels] + result[channels : 2 * channels]
    return velocity[None], (latents[0] + result[2 * channels :] * velocity)[None]


def solution(mesh):
    in_specs = (
        P("cfg", "req", "seq", None),
        P("cfg", "req", "seq", None),
        P("cfg", "req", None, None),
        P(None, "seq"),
        P(),
        P(None, "seq"),
        P("seq", None),
        P(),
        P("req", "cfg", "seq"),
        P("req"),
        P("cfg", "req"),
        P("req"),
        P("req"),
    )
    out_specs = (P("req", "cfg", "seq"), P("req", "cfg", "seq"))
    shape = dict(mesh.shape)
    line = shape == {"cfg": 2, "req": 4, "seq": 4}
    body = fused_local if line else local
    return jax.shard_map(body, mesh=mesh, in_specs=in_specs, out_specs=out_specs, check_vma=False)
```

```python
import functools
import math

import jax
import jax.numpy as jnp
from jax import lax
from jax.experimental import pallas as pl
from jax.experimental.pallas import tpu as pltpu
from jax.sharding import PartitionSpec as P

HEADS = 16
HEAD = 64
STEPS = 28


EPS_NORM = 1e-06


def partner(value, axis, distance):
    mask = 2**distance
    pairs = [(source, source ^ mask) for source in range(lax.axis_size(axis))]
    return lax.ppermute(value, axis, pairs)


def shifted(value, axis, shift):
    size = lax.axis_size(axis)
    return lax.ppermute(value, axis, [(source, (source - shift) % size) for source in range(size)])


def modulate(rows_in, scale_row, shift_row):
    values = rows_in.astype(jnp.float32)
    center = jnp.mean(values, axis=-1, keepdims=True)
    spread = jnp.mean(jnp.square(values - center), axis=-1, keepdims=True)
    return (
        (values - center) * lax.rsqrt(spread + EPS_NORM) * (1.0 + scale_row) + shift_row
    ).astype(jnp.bfloat16)


def sigma_of(index):
    remain = 1.0 - index.astype(jnp.float32) / STEPS
    return 3.0 * remain / (1.0 + 2.0 * remain)


def split_columns(weight_piece):
    width_in = weight_piece.shape[0]
    head_count = weight_piece.shape[1] // (5 * HEAD)
    shaped = weight_piece.reshape(width_in, head_count, 5, HEAD)
    image_cols = shaped[:, :, 0:3, :].reshape(width_in, head_count * 3 * HEAD)
    text_cols = shaped[:, :, 3:5, :].reshape(width_in, head_count * 2 * HEAD)
    return (image_cols, text_cols)


def local(
    image_hidden,
    text_hidden,
    modulation,
    attn_weight,
    proj_weight,
    mlp_in_weight,
    mlp_out_weight,
    final_weight,
    latents,
    guidance,
    text_lengths,
    step_index,
    step_count,
):
    seq_size = lax.axis_size("seq")
    local_heads = HEADS // seq_size
    image_rows = image_hidden[0, 0]
    text_rows = text_hidden[0, 0]
    mod_rows = modulation[0, 0]
    local_rows = image_rows.shape[0]
    image_total = local_rows * seq_size
    text_total = text_rows.shape[0] * seq_size
    image_norm = modulate(image_rows, mod_rows[1], mod_rows[0])
    text_norm = modulate(text_rows, mod_rows[4], mod_rows[3])
    seq_index = lax.axis_index("seq")
    own_norm = jnp.concatenate([image_norm, text_norm], axis=0)
    gathered = jnp.stack([own_norm] + [shifted(own_norm, "seq", k) for k in range(1, seq_size)])
    image_all = gathered[:, :local_rows].reshape(image_total, -1)
    text_all = gathered[:, local_rows:].reshape(text_total, -1)
    image_cols, text_cols = split_columns(attn_weight)
    image_qkv = jnp.dot(image_all, image_cols, preferred_element_type=jnp.float32).astype(
        jnp.bfloat16
    )
    text_kv = jnp.dot(text_all, text_cols, preferred_element_type=jnp.float32).astype(
        jnp.bfloat16
    )
    image_qkv = image_qkv.reshape(image_total, local_heads, 3, HEAD)
    text_kv = text_kv.reshape(text_total, local_heads, 2, HEAD)
    keys_all = jnp.concatenate([image_qkv[:, :, 1], text_kv[:, :, 0]], axis=0)
    values_all = jnp.concatenate([image_qkv[:, :, 2], text_kv[:, :, 1]], axis=0)
    text_local = text_rows.shape[0]
    sources = (seq_index + jnp.arange(seq_size, dtype=jnp.int32)) % seq_size
    slots = (sources[:, None] * text_local + jnp.arange(text_local, dtype=jnp.int32)).reshape(-1)
    valid = jnp.concatenate([jnp.ones((image_total,), dtype=bool), slots < text_lengths[0, 0]])
    block_rows = local_rows
    while block_rows < 512 and image_total % (block_rows * 2) == 0:
        block_rows = block_rows * 2
    block_total = image_total // block_rows
    query_blocks = image_qkv[:, :, 0].reshape(block_total, block_rows, local_heads, HEAD)

    def attend(query_block):
        scores = jnp.einsum(
            "qhe,khe->hqk", query_block, keys_all, preferred_element_type=jnp.float32
        ) * HEAD ** (-0.5)
        scores = jnp.where(valid[None, None, :], scores, -1e30)
        row_max = jnp.max(scores, axis=2, keepdims=True)
        weights = jnp.exp(scores - row_max)
        total = jnp.sum(weights, axis=2, keepdims=True)
        probs = weights.astype(jnp.bfloat16)
        mixed = (
            jnp.einsum("hqk,khe->hqe", probs, values_all, preferred_element_type=jnp.float32)
            / total
        )
        return jnp.transpose(mixed.astype(jnp.bfloat16), (1, 0, 2))

    attended = lax.map(attend, query_blocks).reshape(image_total, local_heads * HEAD)
    attended = attended.reshape(seq_size, local_rows, local_heads * HEAD)
    head_width = local_heads * HEAD
    projected = jnp.zeros((local_rows, proj_weight.shape[1]), jnp.float32)
    for k in range(seq_size):
        piece = attended[k] if k == 0 else shifted(attended[k], "seq", -k)
        rows = lax.dynamic_slice_in_dim(
            proj_weight, ((seq_index - k) % seq_size) * head_width, head_width, 0
        )
        projected = projected + jnp.dot(piece, rows, preferred_element_type=jnp.float32)
    hidden = image_rows.astype(jnp.float32) + mod_rows[2] * projected
    mlp_norm = modulate(hidden, mod_rows[8], mod_rows[7])
    mlp_out = jnp.zeros((local_rows, mlp_out_weight.shape[1]), jnp.float32)
    for k in range(seq_size):
        piece = mlp_norm if k == 0 else shifted(mlp_norm, "seq", k)
        inner = jax.nn.gelu(
            jnp.dot(piece, mlp_in_weight, preferred_element_type=jnp.float32), approximate=True
        ).astype(jnp.bfloat16)
        part = jnp.dot(inner, mlp_out_weight, preferred_element_type=jnp.float32).astype(
            jnp.bfloat16
        )
        part = part if k == 0 else shifted(part, "seq", -k)
        mlp_out = mlp_out + part.astype(jnp.float32)
    block_out = hidden + mod_rows[9] * mlp_out
    final_norm = modulate(block_out, mod_rows[6], mod_rows[5])
    own_vel = lax.dot_general(
        final_weight, final_norm, (((1,), (1,)), ((), ())), preferred_element_type=jnp.float32
    )
    partner_vel = partner(own_vel.astype(jnp.bfloat16), "cfg", 0).astype(own_vel.dtype)
    leading = lax.axis_index("cfg") == 0
    cond_vel = jnp.where(leading, own_vel, partner_vel)
    uncond_vel = jnp.where(leading, partner_vel, own_vel)
    guided = uncond_vel + guidance[...] * (cond_vel - uncond_vel)
    squares = jnp.stack([jnp.sum(cond_vel * cond_vel), jnp.sum(guided * guided)])
    squares = sum(
        [squares] + [shifted(squares, "seq", k) for k in range(1, seq_size)], jnp.zeros(2)
    )
    cond_sq, guided_sq = squares[0], squares[1]
    entries = own_vel.shape[0] * image_total
    rms_cond = jnp.sqrt(cond_sq / entries + EPS_NORM)
    rms_guided = jnp.sqrt(guided_sq / entries + EPS_NORM)
    result_vel = 0.7 * (guided * (rms_cond / rms_guided)) + 0.3 * guided
    channel_half = latents.shape[1]
    channel_start = lax.axis_index("cfg") * channel_half
    own_channels = lax.dynamic_slice_in_dim(result_vel, channel_start, channel_half, 0)
    next_index = jnp.minimum(step_index[0] + step_count[0], STEPS)
    step_size = sigma_of(next_index) - sigma_of(step_index[0])
    moved = latents[0] + step_size * own_channels
    return (own_channels[None], moved[None])


BF16 = jnp.bfloat16
F32 = jnp.float32
MESH_ID = pl.DeviceIdType.MESH
EXP_SCALE = math.log2(math.e) * HEAD ** (-0.5)
TILE = 256
UNITS = [
    ("a", 0, 256, "q"), ("a", 256, 256, "q"), ("a", 512, 256, "q"), ("a", 768, 256, "q"),
    ("a", 1024, 256, "q"), ("i", 0, 256, "q"), ("i", 256, 256, "q"), ("i", 512, 256, "q"),
    ("i", 768, 256, "q"), ("i", 1024, 256, "q"), ("i", 1280, 256, "x"), ("o", 0, 256, "y"),
    ("o", 256, 256, "q"), ("o", 512, 256, "q"), ("o", 768, 256, "x"), ("o", 1024, 256, "y"),
    ("o", 1280, 256, "x"),
]
FIRST_SENDS = [
    ("w", 0, 0), ("w", 1, 0), ("w", 2, 0), ("i", 0), ("i", 1), ("w", 3, 0),
    ("t",), ("w", 4, 0), ("i", 2), ("i", 3),
]
STREAM = [
    ("norm_own",), ("qkv_own",), ("w", 0, 1), ("w", 1, 1), ("w", 0, 2), ("w", 2, 1),
    ("w", 1, 2), ("f", 0), ("norm_om",), ("qkv_om",), ("w", 0, 3), ("f", 1),
    ("w", 2, 2), ("w", 1, 3), ("w", 3, 1), ("w", 2, 3), ("tcomb",), ("w", 3, 2),
    ("w", 4, 1), ("f", 2), ("w", 3, 3), ("f", 3), ("w", 4, 2), ("norm_pe",),
    ("qkv_pe",), ("tkv_own",), ("w", 5, 1), ("w", 4, 3), ("w", 6, 1), ("tkv_far",),
    ("w", 7, 1), ("norm_oe",), ("w", 5, 2), ("qkv_oe",), ("w", 8, 1), ("att0",),
    ("w", 6, 2), ("w", 9, 1), ("att1",), ("w", 7, 2), ("w", 5, 3), ("qkvf0",),
    ("qkvf1",), ("w", 8, 2), ("w", 10, 1), ("w", 6, 3), ("att2",), ("w", 9, 2),
    ("att3",), ("w", 7, 3), ("w", 11, 1), ("w", 8, 3), ("w", 12, 1), ("w", 13, 1),
    ("w", 10, 2), ("w", 9, 3), ("proj_f",), ("w", 11, 2), ("w", 14, 1), ("norm2_f",),
    ("w", 12, 2), ("in_f_own0",), ("w", 13, 2), ("in_f_own1",), ("w", 15, 1), ("in_f_far0",),
    ("in_f_far1",), ("w", 14, 2), ("out_f", 0), ("w", 12, 3), ("proj_n",), ("w", 16, 1),
    ("w", 13, 3), ("out_f", 3), ("out_f", 1), ("w", 15, 2), ("norm2_n",), ("out_f", 2),
    ("in_n_own0",), ("out_f", 4), ("in_n_own1",), ("w", 16, 2), ("in_n_far0",), ("in_n_far1",),
    ("out_n", 0), ("out_f", 5), ("out_n", 1), ("out_n", 2),
]


def normalised(values, scale_row, shift_row):
    center = jnp.mean(values, axis=-1, keepdims=True)
    moved = values - center
    spread = jnp.mean(moved * moved, axis=-1, keepdims=True)
    return moved * lax.rsqrt(spread + EPS_NORM) * (1.0 + scale_row) + shift_row


def gelu_tanh(v):
    part = 0.5 * v
    return part + part * jnp.tanh(v * (0.7978845608028654 + 0.7978845608028654 * 0.044715 * (v * v)))


def fused_kernel(
    unit_plan,
    image,
    text_hbm,
    mod_hbm,
    wa_hbm,
    wp_hbm,
    wi_hbm,
    wo_hbm,
    final_hbm,
    guidance_hbm,
    text_len_hbm,
    step_index_hbm,
    step_count_hbm,
    out_ref,
    text,
    mod,
    final_w,
    guidance,
    text_len,
    step_index,
    step_count,
    wa_own,
    wi_own,
    wo_own,
    wp,
    wa_far,
    wi_far,
    wo_far,
    hid,
    nrm,
    txt,
    txt_out,
    txt_in,
    q_s,
    k_s,
    v_s,
    kt_s,
    vt_s,
    att,
    hs,
    inner,
    rs,
    rr,
    mo,
    vel_own,
    vel_oth,
    pay_out,
    pay_in,
    sum_in,
    sum_out,
    sum_near,
    w_r,
    w_s,
    i_r,
    i_s,
    t_r,
    t_s,
    o_r,
    o_s,
    r_r,
    r_s,
    f_r,
    f_s,
    l_s,
):
    c = lax.axis_index("cfg")
    r = lax.axis_index("req")
    s = lax.axis_index("seq")
    half = s // 2
    is_mid = (s == 1) | (s == 2)
    om = 3 - s
    pe = half * 3
    oe = 3 - pe
    near_mid = 1 + half
    far_mid = 2 - half
    rows_local = image.shape[0]
    rows_all = hid.shape[0]
    near_rows = 2 * rows_local
    width = image.shape[1]
    piece = width // 8
    text_local = text.shape[0]
    text_all = txt.shape[0]

    rx = lax.rem(r + 2, 4)
    rc = r + 1 - 2 * lax.rem(r, 2)
    rcx = lax.rem(rc + 2, 4)
    cy = 1 - c
    dev_x = (c, rx, s)
    dev_y = (cy, r, s)
    dev_c = (c, rc, s)
    dev_om = (c, r, om)
    dev_pe = (c, r, pe)
    dev_oe = (c, r, oe)
    dev_near = (c, r, near_mid)
    dev_far = (c, r, far_mid)

    def rcopy(src, dst, ssem, rsem, dev):
        return pltpu.make_async_remote_copy(
            src_ref=src, dst_ref=dst, send_sem=ssem, recv_sem=rsem, device_id=dev, device_id_type=MESH_ID
        )

    def rows_of(first, count, align):
        return pl.ds(pl.multiple_of(first, align), count)

    own_rows = rows_of(s * rows_local, rows_local, 128)
    weights = {"a": (wa_hbm, wa_far), "i": (wi_hbm, wi_far), "o": (wo_hbm, wo_far)}
    units = len(unit_plan)

    def piece_rows(cc, rr_, first=0, count=None):
        start = (cc * 4 + rr_) * piece + first
        return rows_of(start, piece if count is None else count, 32)

    def wcopy(u, k, rows, dev, src=None):
        kind, col, ncol, _ = unit_plan[u]
        far = weights[kind][1]
        at = far.at[rows, pl.ds(col, ncol)]
        return rcopy(at if src is None else src, at, w_s.at[u, k], w_r.at[u, k], dev)

    hp = piece // 2

    def w_first(u, rows, line, core):
        for k, dev in line:
            wcopy(u, k, rows, dev).start()
        wcopy(u, core, rows, dev_c).start()

    def w_step(u, step):
        mode = unit_plan[u][3]
        mine = piece_rows(c, r)
        if step == 1:
            wcopy(u, 0, mine, dev_pe).wait_recv()
            if mode == "q":
                w_first(u, mine, ((1, dev_x), (2, dev_y)), 5)
            elif mode == "x":
                w_first(u, mine, ((1, dev_x),), 5)
                wcopy(u, 9, piece_rows(cy, r), dev_pe).wait_recv()
                w_first(u, piece_rows(cy, r), ((4, dev_x),), 7)
            else:
                w_first(u, mine, ((2, dev_y),), 5)
                wcopy(u, 9, piece_rows(c, rx), dev_pe).wait_recv()
                w_first(u, piece_rows(c, rx), ((3, dev_y),), 6)
        elif step == 2:
            if mode == "q":
                wcopy(u, 1, piece_rows(c, rx), dev_x).wait_recv()
                wcopy(u, 3, piece_rows(c, rx, 0, hp), dev_y).start()
                wcopy(u, 2, piece_rows(cy, r), dev_y).wait_recv()
                wcopy(u, 4, piece_rows(cy, r, hp, hp), dev_x).start()
                wcopy(u, 6, piece_rows(c, rx), dev_c).start()
                wcopy(u, 7, piece_rows(cy, r), dev_c).start()
            elif mode == "x":
                wcopy(u, 1, piece_rows(c, rx), dev_x).wait_recv()
                wcopy(u, 6, piece_rows(c, rx), dev_c).start()
                wcopy(u, 4, piece_rows(cy, rx), dev_x).wait_recv()
                wcopy(u, 8, piece_rows(cy, rx), dev_c).start()
            else:
                wcopy(u, 2, piece_rows(cy, r), dev_y).wait_recv()
                wcopy(u, 7, piece_rows(cy, r), dev_c).start()
                wcopy(u, 3, piece_rows(cy, rx), dev_y).wait_recv()
                wcopy(u, 8, piece_rows(cy, rx), dev_c).start()
        elif step == 3:
            if mode == "q":
                wcopy(u, 3, piece_rows(cy, rx, 0, hp), dev_y).wait_recv()
                wcopy(u, 4, piece_rows(cy, rx, hp, hp), dev_x).wait_recv()
                wcopy(u, 8, piece_rows(cy, rx), dev_c).start()
        elif step == 4:
            wcopy(u, 5, piece_rows(c, rc), dev_c).wait_recv()
            wcopy(u, 6, piece_rows(c, rcx), dev_c).wait_recv()
            wcopy(u, 7, piece_rows(cy, rc), dev_c).wait_recv()
            wcopy(u, 8, piece_rows(cy, rcx), dev_c).wait_recv()

    def w_sent(u):
        mode = unit_plan[u][3]
        mine = piece_rows(c, r)
        if mode != "y":
            wcopy(u, 1, mine, dev_x).wait_send()
        if mode != "x":
            wcopy(u, 2, mine, dev_y).wait_send()
        if mode == "q":
            wcopy(u, 3, piece_rows(c, rx, 0, hp), dev_y).wait_send()
            wcopy(u, 4, piece_rows(cy, r, hp, hp), dev_x).wait_send()
        elif mode == "x":
            wcopy(u, 4, piece_rows(cy, r), dev_x).wait_send()
        else:
            wcopy(u, 3, piece_rows(c, rx), dev_y).wait_send()
        wcopy(u, 5, mine, dev_c).wait_send()
        wcopy(u, 6, piece_rows(c, rx), dev_c).wait_send()
        wcopy(u, 7, piece_rows(cy, r), dev_c).wait_send()
        wcopy(u, 8, piece_rows(cy, rx), dev_c).wait_send()

    chunks = 4
    chunk = rows_local // chunks

    def end_image(k):
        src = image.at[pl.ds(k * chunk, chunk)]
        dst = hid.at[rows_of(s * rows_local + k * chunk, chunk, 32)]
        return rcopy(src, dst, i_s.at[k], i_r.at[k], dev_near)

    def pe_rows(k):
        return hid.at[rows_of(pe * rows_local + k * chunk, chunk, 32)]

    def oe_rows(k):
        return hid.at[rows_of(oe * rows_local + k * chunk, chunk, 32)]

    def forward_image(k):
        rcopy(pe_rows(k), pe_rows(k), i_s.at[k], i_r.at[k], dev_om).wait_recv()
        rcopy(pe_rows(k), pe_rows(k), i_s.at[chunks + k], i_r.at[chunks + k], dev_om).start()

    own_image = rcopy(image, hid.at[own_rows], i_s.at[2 * chunks], i_r.at[2 * chunks], dev_om)
    text_to_mid = rcopy(txt_out, txt_in, t_s.at[0], t_r.at[0], dev_near)

    def text_half(which):
        return txt.at[rows_of(which * 2 * text_local, 2 * text_local, 16)]

    def att_copy(j, pair):
        return rcopy(att.at[pair], att.at[pair], o_s.at[j], o_r.at[j], dev_om)

    out_units = [u for u in range(units) if unit_plan[u][0] == "o"]

    def r_copy(j):
        cols = pl.ds(unit_plan[out_units[j]][1], unit_plan[out_units[j]][2])
        return rcopy(rs.at[:, cols], rr.at[:, cols], r_s.at[j], r_r.at[j], dev_om)

    vel_copy = rcopy(vel_own, vel_oth, f_s.at[0], f_r.at[0], dev_y)
    pay_copy = rcopy(pay_out, pay_in, f_s.at[1], f_r.at[1], dev_pe)
    sum_copy_om = rcopy(sum_out, sum_in, f_s.at[2], f_r.at[2], dev_om)
    sum_copy_oe = rcopy(sum_out, sum_in, f_s.at[3], f_r.at[2], dev_oe)
    sum_copy_pe = rcopy(sum_out, sum_near, f_s.at[4], f_r.at[3], dev_pe)

    def load(i, src, dst):
        return pltpu.make_async_copy(src, dst, l_s.at[i])

    loads = [
        load(0, image, hid.at[own_rows]),
        load(1, wa_hbm, wa_own),
        load(2, wp_hbm, wp),
        load(3, wi_hbm, wi_own),
        load(4, wo_hbm, wo_own),
    ]
    early = [load(5, text_hbm, text), load(6, mod_hbm, mod)]
    late = [
        load(7, final_hbm, final_w),
        load(8, guidance_hbm, guidance),
        load(9, text_len_hbm, text_len),
        load(10, step_index_hbm, step_index),
        load(11, step_count_hbm, step_count),
    ]

    barrier = pltpu.get_barrier_semaphore()

    def greet(devs):
        for dev in devs:
            pl.semaphore_signal(barrier, inc=1, device_id=dev, device_id_type=MESH_ID)

    for item in early:
        item.start()

    @pl.when(is_mid)
    def _():
        for item in loads[:2]:
            item.start()
        greet((dev_pe, dev_om, dev_oe, dev_x, dev_y, dev_c))

    @pl.when(jnp.logical_not(is_mid))
    def _():
        greet((dev_near, dev_far))

    for item in late:
        item.start()
    for item in early:
        item.wait()

    text_norm = normalised(text[...].astype(F32), mod[4], mod[3])
    pad = txt_out.shape[0] - text_local
    txt_out[...] = jnp.concatenate([text_norm, jnp.zeros((pad, width), F32)], axis=0).astype(BF16)

    def finish(guided_half, sums):
        entries = 2.0 * guided_half.shape[0] * rows_all
        rms_cond = jnp.sqrt(sums[0:1, :] / entries + EPS_NORM)
        rms_guided = jnp.sqrt(sums[4:5, :] / entries + EPS_NORM)
        rescaled = 0.7 * (guided_half * (rms_cond / rms_guided))
        now = step_index[...]
        after = jnp.minimum(now + step_count[...], STEPS)

        def sigma(i):
            remain = 1.0 - i.astype(F32) / STEPS
            return 3.0 * remain / (1.0 + 2.0 * remain)

        lines = guided_half.shape[0]
        out_ref[0:lines, :] = rescaled
        out_ref[lines : 2 * lines, :] = 0.3 * guided_half
        out_ref[2 * lines :, :] = jnp.zeros(guided_half.shape, F32) + (sigma(after) - sigma(now))

    for item in late:
        item.wait()

    @pl.when(jnp.logical_not(is_mid))
    def _():
        pl.semaphore_wait(barrier, 2)

        def unit_send(u):
            kind, col, ncol, mode = unit_plan[u]
            sends = [(0, piece_rows(c, r))]
            if mode == "x":
                sends.append((9, piece_rows(cy, r)))
            elif mode == "y":
                sends.append((9, piece_rows(c, rx)))
            src = weights[kind][0]
            return [wcopy(u, k, rows, dev_near, src.at[rows, pl.ds(col, ncol)]) for k, rows in sends]

        order = []
        sent = set()
        for item in FIRST_SENDS:
            if item[0] == "w":
                order.append(unit_send(item[1])[item[2]])
                sent.add(item[1:])
            else:
                order.append(end_image(item[1]) if item[0] == "i" else text_to_mid)
        for u in range(units):
            order += [item for k, item in enumerate(unit_send(u)) if (u, k) not in sent]
        for at, item in enumerate(order):
            item.start()
            if at >= 1:
                order[at - 1].wait_send()
        order[-1].wait_send()
        pay_copy.wait_recv()
        sum_copy_oe.wait_recv()
        sum_copy_pe.wait_recv()
        finish(pay_in[...], sum_near[...] + sum_in[...])

    @pl.when(is_mid)
    def _():
        pl.semaphore_wait(barrier, 6)
        own_image.start()
        for item in loads[2:]:
            item.start()

        def norm_rows(first, count, read, scale, shift):
            @pl.loop(0, count // 64)
            def _(b):
                at = first + b * 64
                out = normalised(read(at), mod[scale], mod[shift])
                nrm[rows_of(at, 64, 32), :] = out.astype(BF16)

        def read_hid(at):
            return hid[rows_of(at, 64, 32), :].astype(F32)

        def read_hs(at):
            return hs[rows_of(at, 64, 32), :]

        def qkv(rows, w, base):
            @pl.loop(0, 2)
            def _(p):
                cols = rows_of(p * 10 * HEAD, 8 * HEAD, 128)
                y = jnp.dot(nrm[rows, :], w[:, cols], preferred_element_type=F32).astype(BF16)
                for j in range(2):
                    o = j * 5 * HEAD
                    head = base + 2 * p + j
                    q_s[head, rows, :] = y[:, o : o + HEAD]
                    k_s[head, rows, :] = y[:, o + HEAD : o + 2 * HEAD]
                    v_s[head, rows, :] = y[:, o + 2 * HEAD : o + 3 * HEAD]

        def text_kv(w, base):
            @pl.loop(0, 2)
            def _(p):
                start = p * 10 * HEAD
                first = jnp.dot(txt[...], w[:, rows_of(start + 2 * HEAD, 4 * HEAD, 128)], preferred_element_type=F32)
                second = jnp.dot(txt[...], w[:, rows_of(start + 8 * HEAD, 2 * HEAD, 128)], preferred_element_type=F32)
                for j, y in enumerate((first[:, HEAD : 3 * HEAD], second)):
                    head = base + 2 * p + j
                    kt_s[head] = y[:, 0:HEAD].astype(BF16)
                    vt_s[head] = y[:, HEAD : 2 * HEAD].astype(BF16)

        slots = lax.broadcasted_iota(jnp.int32, (1, text_all), 1)
        valid = slots < text_len[...]
        nt = (((1,), (1,)), ((), ()))

        def attend(slot, pair):
            @pl.loop(0, rows_all // 512)
            def _(b):
                rows = rows_of(b * 512, 512, 128)
                parts = []
                for j in range(2):
                    head = slot + j
                    query = q_s[head, rows, :]
                    s_i = lax.dot_general(query, k_s[head], nt, preferred_element_type=F32)
                    s_t = lax.dot_general(query, kt_s[head], nt, preferred_element_type=F32)
                    s_t = jnp.where(valid, s_t, -1e30)
                    top = jnp.maximum(
                        jnp.max(s_i, axis=1, keepdims=True), jnp.max(s_t, axis=1, keepdims=True)
                    )
                    p_i = jnp.exp2((s_i - top) * EXP_SCALE)
                    p_t = jnp.exp2((s_t - top) * EXP_SCALE)
                    total = jnp.sum(p_i, axis=1, keepdims=True) + jnp.sum(p_t, axis=1, keepdims=True)
                    mixed = jnp.dot(p_i.astype(BF16), v_s[head], preferred_element_type=F32)
                    mixed += jnp.dot(p_t.astype(BF16), vt_s[head], preferred_element_type=F32)
                    parts.append(mixed / total)
                att[pair, rows, :] = jnp.concatenate(parts, axis=1).astype(BF16)

        def block(plane):
            return rows_of(plane * rows_local, rows_local, 128)

        def project(first):
            rows = rows_of(first, near_rows, TILE)
            @pl.loop(0, width // 512)
            def _(t):
                cols = rows_of(t * 512, 512, TILE)
                lhs = jnp.concatenate([att[p, rows, :] for p in range(att.shape[0])], axis=1)
                y = jnp.dot(lhs, wp[:, cols], preferred_element_type=F32)
                hs[rows, cols] = hid[rows, cols].astype(F32) + mod[2, :, cols] * y

        def mlp_in(first, w, base, part):
            rows = rows_of(first, near_rows, TILE)
            ncol = width // 2
            y = jnp.dot(nrm[rows, :], w[:, pl.ds(part * ncol, ncol)], preferred_element_type=F32)
            inner[rows, pl.ds(base + part * ncol, ncol)] = gelu_tanh(y).astype(BF16)

        def mlp_out(first, col, ncol, far):
            rows = rows_of(first, near_rows, TILE)
            cols = pl.ds(col, ncol)
            y = jnp.dot(inner[rows, 0:width], wo_own[:, cols], preferred_element_type=F32)
            y += jnp.dot(inner[rows, width : 2 * width], wo_far[:, cols], preferred_element_type=F32)
            if far:
                rs[:, cols] = y.astype(BF16)
            else:
                mo[:, cols] = y

        near_first = half * near_rows
        far_first = (1 - half) * near_rows

        text_send = rcopy(text_half(half), text_half(half), t_s.at[1], t_r.at[1], dev_om)
        held = set()

        def need_load(k):
            if ("load", k) not in held:
                held.add(("load", k))
                loads[k].wait()

        def need_units(kind, limit=None):
            for u in range(units):
                col, ncol = unit_plan[u][1:3]
                if unit_plan[u][0] == kind and ("w", u) not in held and (limit is None or limit(col, ncol)):
                    held.add(("w", u))
                    w_step(u, 4)

        def part_of(part):
            return lambda col, ncol: part == 1 or col < width // 2

        def stage(name, arg=None):
            if name == "f":
                forward_image(arg)
            elif name.startswith("norm_"):
                which = name[5:]
                if which == "own":
                    need_load(0)
                if which == "om":
                    own_image.wait_recv()
                if which == "oe":
                    for k in range(chunks):
                        rcopy(oe_rows(k), oe_rows(k), i_s.at[chunks + k], i_r.at[chunks + k], dev_om).wait_recv()
                plane = {"own": s, "om": om, "pe": pe, "oe": oe}[which]
                norm_rows(plane * rows_local, rows_local, read_hid, 1, 0)
            elif name.startswith("qkv_"):
                need_load(1)
                qkv(block({"own": s, "om": om, "pe": pe, "oe": oe}[name[4:]]), wa_own, 0)
            elif name == "tcomb":
                text_to_mid.wait_recv()
                theirs = txt_in[...].astype(F32)[0:text_local]
                mine = txt_out[...].astype(F32)[0:text_local]
                first = jnp.where(half == 0, theirs, mine)
                second = jnp.where(half == 0, mine, theirs)
                txt[rows_of(half * 2 * text_local, 2 * text_local, 16), :] = jnp.concatenate(
                    [first, second], axis=0
                ).astype(BF16)
                text_send.start()
            elif name == "tkv_own":
                need_load(1)
                rcopy(text_half(1 - half), text_half(1 - half), t_s.at[1], t_r.at[1], dev_om).wait_recv()
                text_kv(wa_own, 0)
            elif name == "tkv_far":
                need_units("a")
                text_kv(wa_far, 4)
            elif name.startswith("qkvf"):
                need_units("a")
                qkv(pl.ds(int(name[4]) * near_rows, near_rows), wa_far, 4)
            elif name.startswith("att"):
                k = int(name[3])
                pair = (2 * s, 2 * s + 1, 2 * pe, 2 * pe + 1)[k]
                attend(2 * k, pair)
                att_copy(k, pair).start()
            elif name == "proj_f":
                need_load(2)
                att_copy(0, 2 * om).wait_recv()
                att_copy(1, 2 * om + 1).wait_recv()
                att_copy(2, 2 * oe).wait_recv()
                att_copy(3, 2 * oe + 1).wait_recv()
                project(far_first)
            elif name == "proj_n":
                project(near_first)
            elif name.startswith("norm2_"):
                norm_rows(far_first if name[6] == "f" else near_first, near_rows, read_hs, 8, 7)
            elif name.startswith("in_"):
                first = far_first if name[3] == "f" else near_first
                part = int(name[-1])
                if "own" in name:
                    need_load(3)
                    mlp_in(first, wi_own, 0, part)
                else:
                    need_units("i", part_of(part))
                    mlp_in(first, wi_far, width, part)
            elif name == "out_f":
                need_load(4)
                u = out_units[arg]
                need_units("o", lambda col, ncol: col == unit_plan[u][1])
                mlp_out(far_first, unit_plan[u][1], unit_plan[u][2], True)
                r_copy(arg).start()
            elif name == "out_n":
                need_load(4)
                need_units("o", lambda col, ncol: col // 512 == arg)
                mlp_out(near_first, arg * 512, 512, False)

        for item in STREAM:
            if item[0] == "w":
                w_step(item[1], item[2])
            else:
                stage(*item)
        for j in range(len(out_units)):
            r_copy(j).wait_recv()

        @pl.loop(0, near_rows // 64)
        def _(b):
            here = rows_of(b * 64, 64, 64)
            rows = rows_of(near_first + b * 64, 64, 64)
            value = hs[rows, :] + mod[9] * (mo[here, :] + rr[here, :].astype(F32))
            nrm[rows, :] = normalised(value, mod[6], mod[5]).astype(BF16)

        own_vel = lax.dot_general(
            final_w[...], nrm[rows_of(near_first, near_rows, TILE), :], nt, preferred_element_type=F32
        )
        vel_own[...] = own_vel.astype(BF16)
        vel_copy.start()
        vel_copy.wait_recv()
        oth_vel = vel_oth[...].astype(F32)
        cond = jnp.where(c == 0, own_vel, oth_vel)
        uncond = jnp.where(c == 0, oth_vel, own_vel)
        guided = uncond + guidance[0] * (cond - uncond)

        def total_of(v):
            return jnp.sum(jnp.sum(v * v, axis=1, keepdims=True), axis=0, keepdims=True)

        patch_half = pay_out.shape[0]
        mine_half = jnp.where(c == 0, guided[0:patch_half, :], guided[patch_half:, :])
        low, high = mine_half[:, 0:rows_local], mine_half[:, rows_local:]
        pay_out[...] = jnp.where(half == 0, low, high)
        pay_copy.start()
        line = lax.broadcasted_iota(jnp.int32, (8, 128), 0)
        sums = jnp.where(line < 4, total_of(cond), total_of(guided))
        sum_out[...] = sums
        sum_copy_oe.start()
        sum_copy_om.start()
        sum_copy_pe.start()
        sum_copy_om.wait_recv()
        finish(jnp.where(half == 0, high, low), sums + sum_in[...])

        own_image.wait_send()
        for k in range(chunks):
            rcopy(pe_rows(k), pe_rows(k), i_s.at[chunks + k], i_r.at[chunks + k], dev_om).wait_send()
        text_send.wait_send()
        for j in range(4):
            att_copy(j, 2 * s).wait_send()
        for j in range(len(out_units)):
            r_copy(j).wait_send()
        for u in range(units):
            w_sent(u)
        vel_copy.wait_send()
        pay_copy.wait_send()
        sum_copy_om.wait_send()
        sum_copy_oe.wait_send()
        sum_copy_pe.wait_send()


def fused_local(
    image_hidden,
    text_hidden,
    modulation,
    attn_weight,
    proj_weight,
    mlp_in_weight,
    mlp_out_weight,
    final_weight,
    latents,
    guidance,
    text_lengths,
    step_index,
    step_count,
):
    rows, width = image_hidden.shape[2:]
    text_rows = text_hidden.shape[2]
    padded = -(-text_rows // 16) * 16
    cols_a = attn_weight.shape[1]
    units_here = mlp_in_weight.shape[1]
    plan = UNITS
    channels = latents.shape[1]
    heads = 2 * (HEADS // 4)
    near = 2 * rows
    count = len(plan)
    outs = sum(1 for item in plan if item[0] == "o")
    vmem = pl.BlockSpec(memory_space=pltpu.VMEM)
    anywhere = pl.BlockSpec(memory_space=pl.ANY)
    dma = pltpu.SemaphoreType.DMA
    result = pl.pallas_call(
        functools.partial(fused_kernel, plan),
        out_shape=jax.ShapeDtypeStruct((3 * channels, rows), F32),
        in_specs=[anywhere] * 12,
        out_specs=vmem,
        scratch_shapes=[
            pltpu.VMEM((text_rows, width), BF16),
            pltpu.VMEM((modulation.shape[2], 1, width), F32),
            pltpu.VMEM(final_weight.shape, BF16),
            pltpu.VMEM((1, 1), F32),
            pltpu.VMEM((1, 1), jnp.int32),
            pltpu.VMEM((1, 1), jnp.int32),
            pltpu.VMEM((1, 1), jnp.int32),
            pltpu.VMEM((width, cols_a), BF16),
            pltpu.VMEM((width, units_here), BF16),
            pltpu.VMEM((units_here, width), BF16),
            pltpu.VMEM(proj_weight.shape, BF16),
            pltpu.VMEM((width, cols_a), BF16),
            pltpu.VMEM((width, units_here), BF16),
            pltpu.VMEM((units_here, width), BF16),
            pltpu.VMEM((4 * rows, width), BF16),
            pltpu.VMEM((4 * rows, width), BF16),
            pltpu.VMEM((4 * text_rows, width), BF16),
            pltpu.VMEM((padded, width), BF16),
            pltpu.VMEM((padded, width), BF16),
            pltpu.VMEM((heads, 4 * rows, HEAD), BF16),
            pltpu.VMEM((heads, 4 * rows, HEAD), BF16),
            pltpu.VMEM((heads, 4 * rows, HEAD), BF16),
            pltpu.VMEM((heads, 4 * text_rows, HEAD), BF16),
            pltpu.VMEM((heads, 4 * text_rows, HEAD), BF16),
            pltpu.VMEM((HEADS // 2, 4 * rows, 2 * HEAD), BF16),
            pltpu.VMEM((4 * rows, width), F32),
            pltpu.VMEM((4 * rows, 2 * units_here), BF16),
            pltpu.VMEM((near, width), BF16),
            pltpu.VMEM((near, width), BF16),
            pltpu.VMEM((near, width), F32),
            pltpu.VMEM((2 * channels, near), BF16),
            pltpu.VMEM((2 * channels, near), BF16),
            pltpu.VMEM((channels, rows), F32),
            pltpu.VMEM((channels, rows), F32),
            pltpu.VMEM((8, 128), F32),
            pltpu.VMEM((8, 128), F32),
            pltpu.VMEM((8, 128), F32),
            dma((count, 10)),
            dma((count, 10)),
            dma((9,)),
            dma((9,)),
            dma((2,)),
            dma((2,)),
            dma((4,)),
            dma((4,)),
            dma((outs,)),
            dma((outs,)),
            dma((4,)),
            dma((5,)),
            dma((12,)),
        ],
        compiler_params=pltpu.CompilerParams(
            collective_id=0, has_side_effects=True, vmem_limit_bytes=60 * 2**20
        ),
        cost_estimate=pl.CostEstimate(flops=15 * 10**9, bytes_accessed=17 * 10**6, transcendentals=5 * 10**6),
    )(
        image_hidden[0, 0],
        text_hidden[0, 0],
        jnp.swapaxes(modulation[0], 0, 1),
        attn_weight,
        proj_weight,
        mlp_in_weight,
        mlp_out_weight,
        final_weight,
        guidance[None],
        text_lengths,
        step_index[None],
        step_count[None],
    )
    velocity = result[:channels] + result[channels : 2 * channels]
    return velocity[None], (latents[0] + result[2 * channels :] * velocity)[None]


def solution(mesh):
    in_specs = (
        P("cfg", "req", "seq", None),
        P("cfg", "req", "seq", None),
        P("cfg", "req", None, None),
        P(None, "seq"),
        P(),
        P(None, "seq"),
        P("seq", None),
        P(),
        P("req", "cfg", "seq"),
        P("req"),
        P("cfg", "req"),
        P("req"),
        P("req"),
    )
    out_specs = (P("req", "cfg", "seq"), P("req", "cfg", "seq"))
    shape = dict(mesh.shape)
    line = shape == {"cfg": 2, "req": 4, "seq": 4}
    body = fused_local if line else local
    return jax.shard_map(body, mesh=mesh, in_specs=in_specs, out_specs=out_specs, check_vma=False)
```
